32 devices in a mesh: tab: 8 (over z, x), blk: 4 (over y, core).
Axes of the slice: x: 2, y: 2, z: 4, core: 2. Of those that a mesh axis runs over, the one named last changes fastest.
Arguments:
- tables: bfloat16 [64, 512, 768], P('tab', 'blk'), may hold values from -6 to 6
- lengths: int32 [64], P('tab'), may hold values from 60 to 512, as said below
- cotangent: bfloat16 [64, 512, 768], P('tab', 'blk'), may hold values from -6 to 6
- step_count: int32 [1], replicated, may hold values from 2 to 20
- w_qkv: float32 [768, 2304], P('tab'), may hold values from -0.21875 to 0.21875
- w_out: float32 [768, 768], P('tab'), may hold values from -3.5 to 3.5
- w_up: float32 [768, 3072], P('tab'), may hold values from -0.21875 to 0.21875
- w_down: float32 [3072, 768], P('tab'), may hold values from -0.109375 to 0.109375
- vectors: float32 [768, 12], P('tab')
- first_qkv: float32 [768, 2304], P('tab'), may hold values from -128 to 128
- first_out: float32 [768, 768], P('tab'), may hold values from -12 to 12
- first_up: float32 [768, 3072], P('tab'), may hold values from -80 to 80
- first_down: float32 [3072, 768], P('tab'), may hold values from -64 to 64
- first_vec: float32 [768, 12], P('tab'), may hold values from -128 to 128
- second_qkv: float32 [768, 2304], P('tab'), may hold values from 16.384 to 262.144
- second_out: float32 [768, 768], P('tab'), may hold values from 0.16384 to 2.62144
- second_up: float32 [768, 3072], P('tab'), may hold values from 8.192 to 131.072
- second_down: float32 [3072, 768], P('tab'), may hold values from 5.89824 to 95.0272
- second_vec: float32 [768, 12], P('tab'), may hold values from 16.384 to 262.144
Outputs:
- output: bfloat16 [64, 512, 768], P('tab', 'blk')
- grad_input: float32 [64, 512, 768], P('tab', 'blk')
- moment_qkv: float32 [768, 2304], P('tab')
- square_qkv: float32 [768, 2304], P('tab')
- master_qkv: float32 [768, 2304], P('tab')
- copy_qkv: bfloat16 [768, 2304], P('tab')
- moment_out: float32 [768, 768], P('tab')
- square_out: float32 [768, 768], P('tab')
- master_out: float32 [768, 768], P('tab')
- copy_out: bfloat16 [768, 768], P('tab')
- moment_up: float32 [768, 3072], P('tab')
- square_up: float32 [768, 3072], P('tab')
- master_up: float32 [768, 3072], P('tab')
- copy_up: bfloat16 [768, 3072], P('tab')
- moment_down: float32 [3072, 768], P('tab')
- square_down: float32 [3072, 768], P('tab')
- master_down: float32 [3072, 768], P('tab')
- copy_down: bfloat16 [3072, 768], P('tab')
- moment_vec: float32 [768, 12], P('tab')
- square_vec: float32 [768, 12], P('tab')
- master_vec: float32 [768, 12], P('tab')
- copy_vec: bfloat16 [768, 12], P('tab')
The draws below stay inside these ranges and needn't reach their ends.
Inputs may be any that keep to these rules, and one draw needn't show every extreme that they name: `lengths`: positions from a table's length on are padding; some table has exactly 512 live tokens.
All inputs are finite; a program needn't handle non-finite values.
Results may differ from the reference program's by a relative error of at most 0.018.
Values may be sent and summed in bfloat16 or wider, within the bound.
A program may use at most 256 MiB of HBM per device.

```python
import math
import jax
import jax.numpy as jnp
from jax import lax

D = 768
H = 12
HD = 64
FF = 3072
LEN = 512
TABLES = 64


def draw_lengths(key, part):
    key_one, key_two, key_three = jax.random.split(key, 3)
    shortest = LEN * 15 // 128
    drawn_len = jax.random.randint(key_one, (TABLES,), shortest, LEN + 1)
    longest_at = jax.random.randint(key_two, (), 0, TABLES)
    shortest_at = (longest_at + jax.random.randint(key_three, (), 1, TABLES)) % TABLES
    drawn_len = drawn_len.at[longest_at].set(LEN)
    drawn_len = drawn_len.at[shortest_at].set(shortest)
    return drawn_len.astype(jnp.int32)


def draw_vectors(key, part):
    noise_v = jax.random.normal(key, (D, 12), jnp.float32)
    column = jnp.arange(12)[None, :]
    is_gain = (column == 4) | (column == 6)
    return jnp.where(is_gain, 1.0 + 0.1 * noise_v, 0.2 * noise_v).astype(jnp.float32)


def block_scale(rng, extent, shards, least, top_value):
    factor_of = 1.0
    for dim, blocks in shards:
        draws = jax.random.uniform(jax.random.fold_in(jax.random.fold_in(rng, 6), dim), (blocks,), jnp.float32, least / len(shards), top_value / len(shards))
        factor_of = factor_of * jnp.repeat(jnp.exp(draws), extent[dim] // blocks).reshape((-1,) + (1,) * (len(extent) - 1 - dim))
    return factor_of


def gaussian(stream_key, extent, scale, bound, cuts=(), kind=jnp.bfloat16):
    level = block_scale(stream_key, extent, cuts, -0.22, 0.18) if cuts else 1.0
    values = jax.random.normal(stream_key, extent, jnp.float32) * scale * level
    return jnp.minimum(jnp.maximum(values, -bound), bound).astype(kind)


def setup_inputs(seed: int = 0) -> dict:
    streams_of = jax.random.split(jax.random.key(seed), 20)
    tables = gaussian(streams_of[0], (TABLES, LEN, D), 1.0, 6.0, ((0, 8), (1, 4)))
    lengths = draw_lengths(jax.random.fold_in(streams_of[19], 71), 0)
    cotangent = gaussian(streams_of[2], (TABLES, LEN, D), 1.0, 6.0, ((0, 8), (1, 4)))
    step_count = jax.random.randint(streams_of[3], (1,), 2, 21).astype(jnp.int32)
    w_qkv = gaussian(streams_of[4], (D, 3 * D), D ** -0.5, 0.21875, ((0, 8),), jnp.float32)
    w_out = gaussian(streams_of[5], (D, D), (max(1, 2 * D // LEN)) ** -0.5, 3.5, ((0, 8),), jnp.float32)
    w_up = gaussian(streams_of[6], (D, FF), D ** -0.5, 0.21875, ((0, 8),), jnp.float32)
    w_down = gaussian(streams_of[7], (FF, D), FF ** -0.5, 0.109375, ((0, 8),), jnp.float32)
    vectors = draw_vectors(jax.random.fold_in(streams_of[19], 71), 0)
    first_qkv = gaussian(streams_of[9], (D, 3 * D), (0.11 * (TABLES * LEN) ** 0.5), 128.0, ((0, 8),), jnp.float32)
    first_out = gaussian(streams_of[10], (D, D), (0.011 * (TABLES * LEN) ** 0.5), 12.0, ((0, 8),), jnp.float32)
    first_up = gaussian(streams_of[11], (D, FF), (0.077 * (TABLES * LEN) ** 0.5), 80.0, ((0, 8),), jnp.float32)
    first_down = gaussian(streams_of[12], (FF, D), (0.066 * (TABLES * LEN) ** 0.5), 64.0, ((0, 8),), jnp.float32)
    first_vec = gaussian(streams_of[13], (D, 12), (0.11 * (TABLES * LEN) ** 0.5), 128.0, ((0, 8),), jnp.float32)
    second_qkv = jnp.clip(jnp.exp(math.log(262.144) - 2.7725887 * jax.random.uniform(streams_of[14], (D, 3 * D), jnp.float32) ** block_scale(streams_of[14], (D, 3 * D), ((0, 8),), -0.2, 0.2)), 16.384, 262.144)
    second_out = jnp.clip(jnp.exp(math.log(2.62144) - 2.7725887 * jax.random.uniform(streams_of[15], (D, D), jnp.float32) ** block_scale(streams_of[15], (D, D), ((0, 8),), -0.2, 0.2)), 0.16384, 2.62144)
    second_up = jnp.clip(jnp.exp(math.log(131.072) - 2.7725887 * jax.random.uniform(streams_of[16], (D, FF), jnp.float32) ** block_scale(streams_of[16], (D, FF), ((0, 8),), -0.2, 0.2)), 8.192, 131.072)
    second_down = jnp.clip(jnp.exp(math.log(95.0272) - 2.779509 * jax.random.uniform(streams_of[17], (FF, D), jnp.float32) ** block_scale(streams_of[17], (FF, D), ((0, 8),), -0.2, 0.2)), 5.89824, 95.0272)
    second_vec = jnp.clip(jnp.exp(math.log(262.144) - 2.7725887 * jax.random.uniform(streams_of[18], (D, 12), jnp.float32) ** block_scale(streams_of[18], (D, 12), ((0, 8),), -0.2, 0.2)), 16.384, 262.144)
    return dict(tables=tables, lengths=lengths, cotangent=cotangent, step_count=step_count, w_qkv=w_qkv, w_out=w_out, w_up=w_up, w_down=w_down, vectors=vectors, first_qkv=first_qkv, first_out=first_out, first_up=first_up, first_down=first_down, first_vec=first_vec, second_qkv=second_qkv, second_out=second_out, second_up=second_up, second_down=second_down, second_vec=second_vec)


EPS = 1e-06
NEGATIVE = -1e+30
BETA_ONE = 0.9
BETA_TWO = 0.999
ADAM_EPS = 1e-08
DECAY = 0.01
RATES = (1.0, 15.0, 1.0, 0.5, 5.0)

@jax.custom_vjp
def low(v):
    return lax.optimization_barrier(v.astype(jnp.bfloat16)).astype(jnp.float32)

@jax.custom_vjp
def low_back(v):
    return v

def low_keep(v):
    return (low(v), None)

def low_pass(kept, grad):
    return (grad,)

def back_keep(v):
    return (v, None)

def back_low(kept, grad):
    return (low(grad),)
low.defvjp(low_keep, low_pass)
low_back.defvjp(back_keep, back_low)

def matmul(left, right):
    return jnp.dot(left, right, precision=lax.Precision.HIGHEST, preferred_element_type=jnp.float32)

def layer_norm(hidden, gain_vec, shift_vec):
    row_mean = lax.optimization_barrier(jnp.mean(hidden, axis=-1, keepdims=True))
    centred = hidden - row_mean
    variance = lax.optimization_barrier(jnp.mean(centred * centred, axis=-1, keepdims=True))
    return centred * lax.rsqrt(variance + EPS) * gain_vec + shift_vec

def forward(weights, group_x, group_len):
    w_qkv, w_out, w_up, w_down, vectors = weights
    table_count = group_x.shape[0]
    tok_rows = group_x.reshape(-1, D)
    bias_up = vectors[:, 8:12].T.reshape(FF)
    proj_qkv = low_back(matmul(tok_rows, w_qkv))
    query_h = low(proj_qkv[:, :D] + vectors[:, 0]).reshape(table_count, LEN, H, HD)
    key_all = low(proj_qkv[:, D:2 * D]).reshape(table_count, LEN, H, HD)
    value_all = low(proj_qkv[:, 2 * D:] + vectors[:, 1]).reshape(table_count, LEN, H, HD)
    raw_scores = jnp.einsum('gqhd,gkhd->ghqk', query_h, key_all, precision=lax.Precision.HIGHEST) * HD ** (-0.5)
    scores = low_back(raw_scores)
    valid_keys = lax.broadcasted_iota(jnp.int32, (table_count, 1, 1, LEN), 3) < group_len.astype(jnp.int32)[:, None, None, None]
    scores = jnp.where(valid_keys, scores, NEGATIVE)
    attn_probs = low(jax.nn.softmax(scores, axis=-1))
    mixed_heads = jnp.einsum('ghqk,gkhd->gqhd', attn_probs, value_all, precision=lax.Precision.HIGHEST).reshape(-1, D)
    mixed_heads = low(low_back(mixed_heads))
    attn_out = low_back(matmul(mixed_heads, w_out)) + vectors[:, 2]
    normed_one = layer_norm(tok_rows + attn_out, vectors[:, 4], vectors[:, 5])
    hidden = low_back(matmul(low(normed_one), w_up)) + bias_up
    active = low(jax.nn.gelu(hidden, approximate=False))
    branch = low_back(matmul(active, w_down)) + vectors[:, 3]
    result = layer_norm(normed_one + branch, vectors[:, 6], vectors[:, 7])
    return result.reshape(table_count, LEN, D)

def adam(master, gradient, first_moment, second_moment, rate_now, step_float):
    moment_new = BETA_ONE * first_moment + (1.0 - BETA_ONE) * gradient
    square_new = BETA_TWO * second_moment + (1.0 - BETA_TWO) * gradient * gradient
    fix_one = 1.0 - jnp.power(BETA_ONE, step_float)
    fix_two = 1.0 - jnp.power(BETA_TWO, step_float)
    update = moment_new / fix_one / (jnp.sqrt(square_new / fix_two) + ADAM_EPS)
    master_new = master - rate_now * (update + DECAY * master)
    return (moment_new, square_new, master_new, master_new.astype(jnp.bfloat16))

def reference(tables, lengths, cotangent, step_count, w_qkv, w_out, w_up, w_down, vectors, first_qkv, first_out, first_up, first_down, first_vec, second_qkv, second_out, second_up, second_down, second_vec):
    masters = (w_qkv, w_out, w_up, w_down, vectors)
    firsts = (first_qkv, first_out, first_up, first_down, first_vec)
    seconds = (second_qkv, second_out, second_up, second_down, second_vec)
    params = tuple((member.astype(jnp.bfloat16).astype(jnp.float32) for member in masters))
    group_size = math.gcd(TABLES, 8)
    group_count = TABLES // group_size
    inputs = (tables.astype(jnp.float32).reshape(group_count, group_size, LEN, D), lengths.astype(jnp.int32).reshape(group_count, group_size), cotangent.astype(jnp.float32).reshape(group_count, group_size, LEN, D))

    def advance(totals, member):
        group_x, group_len, group_cot = member
        result, pull_back = jax.vjp(lambda weights, values: forward(weights, values, group_len), params, group_x)
        gradients, grad_x = pull_back(group_cot)
        totals = jax.tree.map(jnp.add, totals, gradients)
        return (totals, (result.astype(jnp.bfloat16), grad_x))
    zero_init = tuple((jnp.zeros_like(member) for member in params))
    gradients, (outputs, grad_in) = lax.scan(advance, zero_init, inputs)
    step_float = step_count[0].astype(jnp.float32)
    results = [outputs.reshape(TABLES, LEN, D), grad_in.reshape(TABLES, LEN, D)]
    for position in range(5):
        results.extend(adam(masters[position], gradients[position], firsts[position], seconds[position], RATES[position], step_float))
    return tuple(results)
```

```python
from functools import partial

import jax
import jax.numpy as jnp
from jax import lax
from jax.experimental import pallas as pl
from jax.experimental.pallas import tpu as pltpu
from jax.sharding import PartitionSpec as P

D = 768
H = 12
HD = 64
LEN = 512
FF = 3072
PAIR = 2 * HD

EPS = 1e-06
NEGATIVE = -1e30
BETA_ONE = 0.9
BETA_TWO = 0.999
ADAM_EPS = 1e-08
DECAY = 0.01
RATES = (1.0, 15.0, 1.0, 0.5, 5.0)

F32 = jnp.float32
BF16 = jnp.bfloat16
MESH_ID = pl.DeviceIdType.MESH
VMEM_ALL = 64 * 1000 * 1024


def layer_norm(hidden, gain_vec, shift_vec):
    row_mean = jnp.mean(hidden, axis=-1, keepdims=True)
    centred = hidden - row_mean
    variance = jnp.mean(centred * centred, axis=-1, keepdims=True)
    return centred * lax.rsqrt(variance + EPS) * gain_vec + shift_vec


def inner(left, right):
    return lax.dot_general(left, right, (((0,), (0,)), ((), ())), preferred_element_type=F32)


def back_mul(left, right):
    return lax.dot_general(left, right, (((1,), (1,)), ((), ())), preferred_element_type=F32)


def adam(master, gradient, first_moment, second_moment, rate_now, step_float):
    moment_new = BETA_ONE * first_moment + (1.0 - BETA_ONE) * gradient
    square_new = BETA_TWO * second_moment + (1.0 - BETA_TWO) * gradient * gradient
    fix_one = 1.0 - jnp.power(BETA_ONE, step_float)
    fix_two = 1.0 - jnp.power(BETA_TWO, step_float)
    update = moment_new / fix_one / (jnp.sqrt(square_new / fix_two) + ADAM_EPS)
    master_new = master - rate_now * (update + DECAY * master)
    return (moment_new, square_new, master_new, master_new.astype(BF16))


def head_masks(dtype):
    lane = lax.broadcasted_iota(jnp.int32, (1, PAIR), 1)
    return [(lane < HD).astype(dtype), (lane >= HD).astype(dtype)]


def attn_fwd_kernel(len_ref, q_ref, k_ref, v_ref, o_ref, l_ref):
    live = len_ref[pl.program_id(0)]
    masks = head_masks(BF16)
    keys = k_ref[...]
    values = v_ref[...]
    rows = 256
    key_at = lax.broadcasted_iota(jnp.int32, (1, LEN), 1)
    bias = jnp.where(key_at < live, 0.0, NEGATIVE)
    lane = lax.broadcasted_iota(jnp.int32, (1, PAIR), 1)
    for start in range(0, LEN, rows):
        query = q_ref[pl.ds(start, rows), :] * jnp.asarray(HD ** (-0.5), BF16)
        mixed, logs = [], []
        for head in range(2):
            scores = back_mul(query * masks[head], keys) + bias
            top = jnp.max(scores, axis=-1, keepdims=True)
            raised = jnp.exp(scores - top)
            total = jnp.sum(raised, axis=-1, keepdims=True)
            probs = (raised * (1.0 / total)).astype(BF16)
            mixed.append(jnp.dot(probs, values, preferred_element_type=F32))
            logs.append(top + jnp.log(total))
        o_ref[pl.ds(start, rows), :] = jnp.where(lane < HD, mixed[0], mixed[1]).astype(BF16)
        both = jnp.where(lane < HD, logs[0], logs[1])
        flat = both.T
        l_ref[0, 0, 0:1, pl.ds(start, rows)] = flat[0:1, :]
        l_ref[0, 0, 1:2, pl.ds(start, rows)] = flat[HD : HD + 1, :]


def attention_forward(lengths, qkv, tables):
    pairs = H // 2
    spec = lambda part: pl.BlockSpec((LEN, PAIR), lambda t, h, n: (t, part * pairs + h))
    return pl.pallas_call(
        attn_fwd_kernel,
        grid_spec=pltpu.PrefetchScalarGridSpec(
            num_scalar_prefetch=1,
            grid=(tables, pairs),
            in_specs=[spec(0), spec(1), spec(2)],
            out_specs=[
                pl.BlockSpec((LEN, PAIR), lambda t, h, n: (t, h)),
                pl.BlockSpec((1, 1, 8, LEN), lambda t, h, n: (t, h, 0, 0)),
            ],
        ),
        out_shape=[
            jax.ShapeDtypeStruct((tables * LEN, D), BF16),
            jax.ShapeDtypeStruct((tables, pairs, 8, LEN), F32),
        ],
        name="attn_fwd",
    )(lengths, qkv, qkv, qkv)


def attn_bwd_kernel(len_ref, q_ref, k_ref, v_ref, o_ref, l_ref, do_ref, d_ref, sums_ref):
    live = len_ref[pl.program_id(0)]
    masks = head_masks(BF16)
    keys = k_ref[...]
    values = v_ref[...]
    query = q_ref[...] * jnp.asarray(HD ** (-0.5), BF16)
    grad_out = do_ref[...]
    dots = (grad_out.astype(F32) * o_ref[...].astype(F32)).T
    rows = 256
    q_masked = [query * m for m in masks]
    g_masked = [grad_out * m for m in masks]
    deltas = [jnp.sum(dots[h * HD : (h + 1) * HD, :], axis=0, keepdims=True) for h in range(2)]
    logs = [l_ref[0, 0, h : h + 1, :] for h in range(2)]
    grad_q = jnp.zeros((LEN, PAIR), F32)
    sum_v = jnp.zeros((1, PAIR), F32)
    for start in range(0, LEN, rows):
        part_k = keys[start : start + rows, :]
        part_v = values[start : start + rows, :]
        key_at = start + lax.broadcasted_iota(jnp.int32, (rows, 1), 0)
        bias = jnp.where(key_at < live, 0.0, NEGATIVE)
        grad_k = jnp.zeros((rows, PAIR), F32)
        grad_v = jnp.zeros((rows, PAIR), F32)
        for head in range(2):
            scores = back_mul(part_k, q_masked[head])
            probs = jnp.exp(scores + bias - logs[head])
            grad_probs = back_mul(part_v, g_masked[head])
            grad_s = (probs * (grad_probs - deltas[head])).astype(BF16)
            grad_v += jnp.dot(probs.astype(BF16), g_masked[head], preferred_element_type=F32)
            grad_k += jnp.dot(grad_s, q_masked[head], preferred_element_type=F32)
            grad_q += inner(grad_s, part_k * masks[head])
        d_ref[1, pl.ds(start, rows), :] = grad_k.astype(BF16)
        d_ref[2, pl.ds(start, rows), :] = grad_v.astype(BF16)
        sum_v += jnp.sum(grad_v, axis=0, keepdims=True)
    grad_q = grad_q * HD ** (-0.5)
    d_ref[0, :, :] = grad_q.astype(BF16)
    sums_ref[0, 0, 0:1, :] = jnp.sum(grad_q, axis=0, keepdims=True)
    sums_ref[0, 0, 1:2, :] = sum_v


def attention_backward(lengths, qkv, mixed, logs, grad_mixed, tables):
    pairs = H // 2
    spec = lambda part: pl.BlockSpec((LEN, PAIR), lambda t, h, n: (t, part * pairs + h))
    block = pl.BlockSpec((LEN, PAIR), lambda t, h, n: (t, h))
    return pl.pallas_call(
        attn_bwd_kernel,
        grid_spec=pltpu.PrefetchScalarGridSpec(
            num_scalar_prefetch=1,
            grid=(tables, pairs),
            in_specs=[
                spec(0),
                spec(1),
                spec(2),
                block,
                pl.BlockSpec((1, 1, 8, LEN), lambda t, h, n: (t, h, 0, 0)),
                block,
            ],
            out_specs=[
                pl.BlockSpec((3, LEN, PAIR), lambda t, h, n: (0, t, h)),
                pl.BlockSpec((1, 1, 8, PAIR), lambda t, h, n: (t, h, 0, 0)),
            ],
        ),
        out_shape=[
            jax.ShapeDtypeStruct((3, tables * LEN, D), BF16),
            jax.ShapeDtypeStruct((tables, pairs, 8, PAIR), F32),
        ],
        name="attn_bwd",
    )(lengths, qkv, qkv, qkv, mixed, logs, grad_mixed)


def place():
    tab, blk = lax.axis_index("tab"), lax.axis_index("blk")
    return tab // 2, tab % 2, blk // 2, blk % 2


class Wires:
    def __init__(self, send, recv):
        self.send, self.recv, self.count, self.sent = send, recv, 0, []

    def copy(self, src, dst, to):
        index, self.count = self.count, self.count + 1
        z, x, y, c = to
        made = pltpu.make_async_remote_copy(
            src_ref=src,
            dst_ref=dst,
            send_sem=self.send.at[index],
            recv_sem=self.recv.at[index],
            device_id=(z * 2 + x, y * 2 + c),
            device_id_type=MESH_ID,
        )
        made.start()
        self.sent.append(made)
        return made

    def finish(self):
        for made in self.sent:
            made.wait_send()


def greet(peers):
    barrier = pltpu.get_barrier_semaphore()
    for z, x, y, c in peers:
        pl.semaphore_signal(
            barrier, inc=1, device_id=(z * 2 + x, y * 2 + c), device_id_type=MESH_ID
        )
    pl.semaphore_wait(barrier, len(peers))


def all_peers():
    z, x, y, c = place()
    z_peers = [((z + j) % 4, x, y, c) for j in range(1, 4)]
    rest = [(z, 1 - x, y, c), (z, x, 1 - y, c), (z, x, y, 1 - c), (z, x, 1 - y, 1 - c)]
    return z_peers + rest


def by_columns(width):
    return lambda ref, t, part: ref.at[t, :, pl.ds(pl.multiple_of(part * width, 128), width)]


def by_rows(height):
    return lambda ref, t, part: ref.at[t, pl.ds(pl.multiple_of(part * height, 16), height), :]


PIECES = (
    (by_columns(FF // 4), True),
    (by_rows(FF // 32), True),
    (by_columns(3 * D // 2), False),
    (by_columns(D // 2), False),
)
N_WIRES = 160


def gather_kernel(
    x_in, cot_in, up_in, down_in, qkv_in, out_in, vec_in,
    x_out, cot_out, up_out, down_out, qkv_out, out_out, vec_out,
    send, recv, own,
):
    z, x, y, c = place()
    tab, blk = z * 2 + x, y * 2 + c
    greet(all_peers())
    wires = Wires(send, recv)
    shards = (up_in, down_in, qkv_in, out_in)
    wholes = (up_out, down_out, qkv_out, out_out)
    share, span = x_in.shape[0] // 4, x_in.shape[1]
    mine = pl.ds(blk * share, share)
    kept = [
        pltpu.make_async_copy(x_in.at[mine], x_out.at[:, pl.ds(blk * span, span), :], own.at[0]),
        pltpu.make_async_copy(cot_in.at[mine], cot_out.at[:, pl.ds(blk * span, span), :], own.at[1]),
        pltpu.make_async_copy(vec_in.at[0], vec_out.at[tab], own.at[2]),
    ]
    for at in range(4):
        kept.append(pltpu.make_async_copy(shards[at].at[0], wholes[at].at[tab], own.at[3 + at]))
    for made in kept:
        made.start()

    def trade(src, dst):
        made = []
        for other in ((z, x, 1 - y, c), (z, x, 1 - y, 1 - c), (z, x, y, 1 - c)):
            their = other[2] * 2 + other[3]
            made.append(
                wires.copy(
                    src.at[pl.ds(their * share, share)],
                    dst.at[:, pl.ds(blk * span, span), :],
                    other,
                )
            )
        return made

    waits = trade(x_in, x_out)
    along_z = []
    for at in range(4):
        piece, split = PIECES[at]
        part = blk if split else c
        along_z.append(
            [
                wires.copy(
                    piece(shards[at], 0, part),
                    piece(wholes[at], tab, part),
                    ((z + j) % 4, x, y, c),
                )
                for j in range(1, 4)
            ]
        )
    vec_z = [
        wires.copy(vec_in.at[0], vec_out.at[tab], ((z + j) % 4, x, y, c)) for j in range(1, 4)
    ]
    for at in range(4):
        piece, split = PIECES[at]
        whole = wholes[at]
        part = blk if split else c
        along_x, along_y = [], []

        def onward(t, local_part, kind):
            src = piece(whole, t, local_part)
            if kind == "y":
                along_y.append((t, wires.copy(src, src, (z, x, 1 - y, c))))
            else:
                waits.append(wires.copy(src, src, (z, x, y, 1 - c)))

        src = piece(shards[at], 0, part)
        along_x.append(wires.copy(src, piece(whole, tab, part), (z, 1 - x, y, c)))
        for j in range(1, 4):
            t = (z + 4 - j) % 4 * 2 + x
            along_z[at][j - 1].wait_recv()
            src = piece(whole, t, part)
            along_x.append(wires.copy(src, src, (z, 1 - x, y, c)))
            if split:
                onward(t, part, "y")
            onward(t, part, "c")
        for j in range(4):
            t = (z + 4 - j) % 4 * 2 + 1 - x
            along_x[j].wait_recv()
            if split:
                onward(t, part, "y")
            onward(t, part, "c")
        for t, made in along_y:
            made.wait_recv()
            onward(t, (1 - y) * 2 + c, "c")
    src = vec_in.at[0]
    vec_x = [wires.copy(src, vec_out.at[tab], (z, 1 - x, y, c))]
    for j in range(1, 4):
        t = (z + 4 - j) % 4 * 2 + x
        vec_z[j - 1].wait_recv()
        vec_x.append(wires.copy(vec_out.at[t], vec_out.at[t], (z, 1 - x, y, c)))
    waits += trade(cot_in, cot_out)
    for made in waits + vec_x:
        made.wait_recv()
    wires.finish()
    for made in kept:
        made.wait()


def gather_all(tables, cotangent, up, down, qkv, out, vec):
    share, span = tables.shape[0] // 4, tables.shape[1] * 4
    vmem = pl.BlockSpec(memory_space=pltpu.VMEM)
    hbm = pl.BlockSpec(memory_space=pl.ANY)
    shape = lambda a: jax.ShapeDtypeStruct((8,) + a.shape[1:], BF16)
    return pl.pallas_call(
        gather_kernel,
        in_specs=[vmem] * 7,
        out_specs=[hbm] * 7,
        out_shape=[
            jax.ShapeDtypeStruct((share, span, D), BF16),
            jax.ShapeDtypeStruct((share, span, D), BF16),
            shape(up), shape(down), shape(qkv), shape(out), shape(vec),
        ],
        scratch_shapes=[
            pltpu.SemaphoreType.DMA((N_WIRES,)),
            pltpu.SemaphoreType.DMA((N_WIRES,)),
            pltpu.SemaphoreType.DMA((7,)),
        ],
        compiler_params=pltpu.CompilerParams(
            collective_id=0, has_side_effects=True, vmem_limit_bytes=VMEM_ALL
        ),
        name="gather_all",
    )(tables, cotangent, up, down, qkv, out, vec)


class Plan:
    def __init__(self, send, recv):
        self.send, self.recv, self.makers = send, recv, []

    def add(self, maker):
        self.makers.append(maker)
        return len(self.makers) - 1

    def build(self, index):
        src, dst, (z, x, y, c) = self.makers[index]()
        return pltpu.make_async_remote_copy(
            src_ref=src,
            dst_ref=dst,
            send_sem=self.send.at[index],
            recv_sem=self.recv.at[index],
            device_id=(z * 2 + x, y * 2 + c),
            device_id_type=MESH_ID,
        )

    def start(self, index):
        self.build(index).start()

    def arrived(self, index):
        self.build(index).wait_recv()

    def finish(self):
        for index in range(len(self.makers)):
            self.build(index).wait_send()


class Slab:
    def __init__(self, rows, cols, split, axis, first=0, dtype=BF16):
        self.rows, self.cols, self.split, self.axis = rows, cols, split, axis
        self.first, self.dtype = first, dtype
        self.tile = 128 if axis == 1 else (16 if dtype == BF16 else 8)

    def cut(self, index):
        if self.axis == 1:
            return pl.ds(0, self.rows), pl.ds(
                pl.multiple_of(index * self.cols, self.tile), self.cols
            )
        start = pl.multiple_of(self.first + index * self.rows, self.tile)
        return pl.ds(start, self.rows), pl.ds(0, self.cols)

    def scratch(self):
        ways = 2 if self.split else 1
        vmem = lambda *lead: pltpu.VMEM(lead + (self.rows, self.cols), self.dtype)
        late = vmem(4, 2) if self.split else vmem(1, 1)
        return [vmem(ways, 4, 2), vmem(ways, 4, 2), late, vmem(4), vmem(3), vmem()]

    def copies(self):
        return (2 if self.split else 1) + 1 + 1 + 3 + 3


class Reduction:
    def __init__(self, slab, source, target, scratch, plan, own, own_at):
        self.slab, self.source, self.target, self.plan = slab, source, target, plan
        self.held, self.from_c, self.from_y, self.from_x, self.from_z, self.done = scratch
        self.own, self.own_at = own, own_at
        z, x, y, c = place()
        self.at = z, x, y, c
        self.slot = y if slab.split else 0
        side = (z, x, y, 1 - c)
        over = (z, x, 1 - y, c)

        def index_of(half, core):
            return half * 2 + core if slab.split else core

        def cut_all(ref, index):
            rows, cols = slab.cut(index)
            return ref.at[:, :, rows, cols]

        def cut_out(index):
            rows, cols = slab.cut(index)
            return target.at[rows, cols]

        ways = 2 if slab.split else 1
        self.loads = [
            lambda half=half: pltpu.make_async_copy(
                cut_all(source, index_of(half, c)), self.held.at[half], own.at[own_at + half]
            )
            for half in range(ways)
        ]
        self.to_core = [
            plan.add(
                lambda half=half: (
                    cut_all(source, index_of(half, 1 - c)), self.from_c.at[half], side,
                )
            )
            for half in range(ways)
        ]
        if slab.split:
            self.to_y = plan.add(lambda: (self.held.at[1 - y], self.from_y, over))
        else:
            self.to_y = plan.add(lambda: (self.done, self.from_y.at[0, 0], over))
        self.to_x = plan.add(
            lambda: (self.held.at[self.slot, :, 1 - x], self.from_x, (z, 1 - x, y, c))
        )
        self.to_z = [
            plan.add(
                lambda j=j: (
                    self.held.at[self.slot, (z + j) % 4, x],
                    self.from_z.at[j - 1],
                    ((z + j) % 4, x, y, c),
                )
            )
            for j in range(1, 4)
        ]
        mine = lambda: cut_out(index_of(y, c))
        self.store = lambda: pltpu.make_async_copy(self.done, mine(), own.at[own_at + 2])
        self.share_core = plan.add(lambda: (self.done, mine(), side))
        if slab.split:
            theirs = lambda: cut_out(index_of(1 - y, c))
            self.share_y = plan.add(lambda: (self.done, mine(), over))
            self.share_far = plan.add(lambda: (theirs(), theirs(), side))

    def begin(self):
        for load in self.loads:
            load().start()
        for index in self.to_core:
            self.plan.start(index)

    def summed(self, total, *others):
        value = total[...].astype(F32)
        for other in others:
            value = value + other[...].astype(F32)
        total[...] = value.astype(self.slab.dtype)

    def after_core(self):
        for half, load in enumerate(self.loads):
            load().wait()
            self.plan.arrived(self.to_core[half])

        def step(t, carry):
            for half in range(len(self.loads)):
                self.summed(self.held.at[half, t // 2, t % 2], self.from_c.at[half, t // 2, t % 2])
            return carry

        lax.fori_loop(0, 8, step, 0)
        self.plan.start(self.to_y if self.slab.split else self.to_x)

    def after_y(self):
        if not self.slab.split:
            return
        self.plan.arrived(self.to_y)

        def step(t, carry):
            self.summed(self.held.at[self.slot, t // 2, t % 2], self.from_y.at[t // 2, t % 2])
            return carry

        lax.fori_loop(0, 8, step, 0)
        self.plan.start(self.to_x)

    def after_x(self):
        z, x, y, c = self.at
        self.plan.arrived(self.to_x)

        def step(t, carry):
            self.summed(self.held.at[self.slot, t, x], self.from_x.at[t])
            return carry

        lax.fori_loop(0, 4, step, 0)
        for index in self.to_z:
            self.plan.start(index)

    def after_z(self):
        z, x, y, c = self.at
        for index in self.to_z:
            self.plan.arrived(index)
        value = self.held[self.slot, z, x].astype(F32)
        for j in range(3):
            value = value + self.from_z[j].astype(F32)
        self.done[...] = value.astype(self.slab.dtype)
        if self.slab.split:
            self.plan.start(self.share_y)
            self.plan.start(self.share_core)
            self.store().start()
        else:
            self.plan.start(self.to_y)

    def after_final(self):
        if self.slab.split:
            self.plan.arrived(self.share_y)
            self.plan.start(self.share_far)
        else:
            self.plan.arrived(self.to_y)
            self.plan.build(self.to_y).wait_send()
            self.summed(self.done, self.from_y.at[0, 0])
            self.plan.start(self.share_core)
            self.store().start()

    def end(self):
        self.plan.arrived(self.share_core)
        if self.slab.split:
            self.plan.arrived(self.share_far)
        self.store().wait()

    def finish_sends(self):
        done_early = () if self.slab.split else (self.to_y,)
        sends = self.to_core + [self.to_y, self.to_x] + self.to_z + [self.share_core]
        if self.slab.split:
            sends += [self.share_y, self.share_far]
        for index in sends:
            if index not in done_early:
                self.plan.build(index).wait_send()


STAGES = ("begin", "after_core", "after_y", "after_x", "after_z", "after_final", "end")

SLABS = (
    (0, Slab(96, FF // 4, True, 1)),
    (1, Slab(32, D, True, 0)),
    (1, Slab(128, D, False, 0, first=128)),
    (2, Slab(96, 3 * D // 2, False, 1)),
    (3, Slab(96, D // 2, False, 1)),
    (4, Slab(8, 128, False, 0, dtype=F32)),
)


def reduce_kernel(*refs):
    (gin_in, y_in), sources = refs[:2], refs[2:7]
    (gin_out, y_out), targets = refs[7:9], refs[9:14]
    scratch, (send, recv, own) = refs[14:-3], refs[-3:]
    z, x, y, c = place()
    blk = y * 2 + c
    greet(all_peers())
    plan = Plan(send, recv)
    share, span = gin_out.shape[0] // 4, gin_out.shape[1]
    kept, traded = [], []
    works = []
    for at, (number, slab) in enumerate(SLABS):
        part = scratch[6 * at : 6 * at + 6]
        works.append(
            Reduction(slab, sources[number], targets[number], part, plan, own, 2 + 3 * at)
        )
    for at, (src, dst) in enumerate(((gin_in, gin_out), (y_in, y_out))):
        mine = dst.at[pl.ds(blk * share, share)]
        kept.append(
            pltpu.make_async_copy(src.at[:, pl.ds(blk * span, span), :], mine, own.at[at])
        )
        kept[-1].start()
        for other in ((z, x, 1 - y, c), (z, x, 1 - y, 1 - c), (z, x, y, 1 - c)):
            their = other[2] * 2 + other[3]
            maker = lambda src=src, mine=mine, their=their, other=other: (
                src.at[:, pl.ds(their * span, span), :], mine, other,
            )
            traded.append(plan.add(maker))
    for stage in STAGES:
        for work in works:
            getattr(work, stage)()
        if stage == "after_y":
            for index in traded:
                plan.start(index)
    for index in traded:
        plan.arrived(index)
    for work in works:
        work.finish_sends()
    for index in traded:
        plan.build(index).wait_send()
    for made in kept:
        made.wait()


def reduce_all(grad_in, result, up, down, qkv, out, vec):
    share, length = grad_in.shape[:2]
    vmem = pl.BlockSpec(memory_space=pltpu.VMEM)
    hbm = pl.BlockSpec(memory_space=pl.ANY)
    shape = lambda a: jax.ShapeDtypeStruct(a.shape[2:], a.dtype)
    back = jax.ShapeDtypeStruct((share * 4, length // 4, D), BF16)
    grads = (up, down, qkv, out, vec)
    scratch = [s for _, slab in SLABS for s in slab.scratch()]
    wires = 6 + sum(slab.copies() for _, slab in SLABS)
    return pl.pallas_call(
        reduce_kernel,
        in_specs=[vmem] * 2 + [hbm] * 5,
        out_specs=[hbm] * 7,
        out_shape=[back, back] + [shape(a) for a in grads],
        scratch_shapes=scratch
        + [
            pltpu.SemaphoreType.DMA((wires,)),
            pltpu.SemaphoreType.DMA((wires,)),
            pltpu.SemaphoreType.DMA((2 + 3 * len(SLABS),)),
        ],
        compiler_params=pltpu.CompilerParams(
            collective_id=1, has_side_effects=True, vmem_limit_bytes=VMEM_ALL
        ),
        name="reduce_all",
    )(grad_in, result, *grads)


def local(*args):
    tables, lengths, cotangent, step_count = args[:4]
    masters, firsts, seconds = args[4:9], args[9:14], args[14:19]
    w_qkv, w_out, w_up, w_down, vectors = masters
    blocks = lax.axis_size("blk")
    shards = lax.axis_size("tab")
    table_count, local_len = tables.shape[:2]
    share = table_count // blocks
    tuned = shards == 8 and blocks == 4
    vec_pad = jnp.pad(vectors.astype(BF16).T, ((0, 4), (0, 128 - vectors.shape[0])))
    narrow = [w.astype(BF16) for w in (w_up, w_down, w_qkv, w_out)]
    if tuned:
        mine, cot, *wholes = gather_all(
            tables, cotangent, *[w[None] for w in narrow], vec_pad[None]
        )
    else:
        spread = partial(lax.all_to_all, axis_name="blk", split_axis=0, concat_axis=1, tiled=True)
        mine, cot = spread(tables), spread(cotangent)
        wholes = [lax.all_gather(w, "tab", axis=0) for w in narrow + [vec_pad]]
    full_up, full_down, full_qkv, full_out = [
        w.reshape(-1, w.shape[-1]) for w in wholes[:4]
    ]
    vec_f = wholes[4][:, :12, : vectors.shape[0]].transpose(1, 0, 2).reshape(12, D).astype(F32)
    my_lengths = lax.dynamic_slice(lengths, (lax.axis_index("blk") * share,), (share,))
    bias_up = vec_f[8:12].reshape(-1)
    bias_qkv = jnp.concatenate([vec_f[0], jnp.zeros((D,), F32), vec_f[1]])

    rows = mine.reshape(-1, D)
    qkv = (jnp.dot(rows, full_qkv, preferred_element_type=F32) + bias_qkv).astype(BF16)
    mixed, logs = attention_forward(my_lengths, qkv, share)
    attn_out = jnp.dot(mixed, full_out, preferred_element_type=F32) + vec_f[2]
    normed_one, norm_one_back = jax.vjp(
        layer_norm, rows.astype(F32) + attn_out, vec_f[4], vec_f[5]
    )
    normed_b = normed_one.astype(BF16)
    hidden = jnp.dot(normed_b, full_up, preferred_element_type=F32) + bias_up
    active, gelu_back = jax.vjp(partial(jax.nn.gelu, approximate=False), hidden)
    active_b = active.astype(BF16)
    branch = jnp.dot(active_b, full_down, preferred_element_type=F32) + vec_f[3]
    result, norm_two_back = jax.vjp(layer_norm, normed_one + branch, vec_f[6], vec_f[7])
    result = result.astype(BF16).reshape(mine.shape)
    grad_two, grad_g2, grad_c2 = norm_two_back(cot.reshape(-1, D).astype(F32))
    grad_b2 = jnp.sum(grad_two, axis=0)
    branch_b = grad_two.astype(BF16)
    gw_down = inner(active_b, branch_b).astype(BF16)
    grad_hidden = gelu_back(back_mul(branch_b, full_down))[0]
    grad_b1 = jnp.sum(grad_hidden, axis=0)
    hidden_b = grad_hidden.astype(BF16)
    gw_up = inner(normed_b, hidden_b).astype(BF16)
    grad_one, grad_g1, grad_c1 = norm_one_back(grad_two + back_mul(hidden_b, full_up))
    grad_bo = jnp.sum(grad_one, axis=0)
    attn_b = grad_one.astype(BF16)
    gw_out = inner(mixed, attn_b).astype(BF16)
    grad_mixed = back_mul(attn_b, full_out).astype(BF16)
    grad_three, sums = attention_backward(my_lengths, qkv, mixed, logs, grad_mixed, share)
    sums = jnp.sum(sums[:, :, :2], axis=0)
    grad_bq, grad_bv = sums[:, 0].reshape(-1), sums[:, 1].reshape(-1)
    grad_qkv = jnp.concatenate([grad_three[i] for i in range(3)], axis=1)
    gw_qkv = inner(rows, grad_qkv).astype(BF16)
    grad_in = grad_one + back_mul(grad_qkv, full_qkv)
    grad_in = grad_in.astype(BF16).reshape(mine.shape)
    gw_vec = jnp.concatenate(
        [
            jnp.stack([grad_bq, grad_bv, grad_bo, grad_b2, grad_g1, grad_c1, grad_g2, grad_c2]),
            grad_b1.reshape(4, D),
        ]
    )
    owned = vectors.shape[0]
    if tuned:
        pads = ((0, 0), (0, 0), (0, 2), (0, 128 - owned))
        wide_vec = jnp.pad(gw_vec.reshape(2, 6, shards, owned).transpose(2, 0, 1, 3), pads)
        by_owner = lambda g: g.reshape(4, 2, -1, g.shape[-1])
        grad_input, output, *sums = reduce_all(
            grad_in, result, by_owner(gw_up), by_owner(gw_down), by_owner(gw_qkv),
            by_owner(gw_out), wide_vec.reshape(4, 2, 16, 128),
        )
        sum_vec = sums[4].reshape(2, 8, 128)[:, :6, :owned].reshape(12, owned).T
        shares = [s.astype(F32) for s in (sums[2], sums[3], sums[0], sums[1], sum_vec)]
    else:
        back = partial(lax.all_to_all, axis_name="blk", split_axis=1, concat_axis=0, tiled=True)
        grad_input, output = back(grad_in), back(result)

        def collect(grad):
            part = lax.psum_scatter(
                grad.reshape(shards, -1, grad.shape[-1]), "tab", scatter_dimension=0
            )
            return lax.psum(part.astype(BF16), "blk").astype(F32)

        shares = [collect(g) for g in (gw_qkv, gw_out, gw_up, gw_down)]
        shares.append(collect(gw_vec.T.astype(BF16)))
    grad_input = grad_input.astype(F32)
    step_float = step_count[0].astype(F32)
    results = [output, grad_input]
    for at in range(5):
        results.extend(
            adam(masters[at], shares[at], firsts[at], seconds[at], RATES[at], step_float)
        )
    return tuple(results)


def solution(mesh):
    tokens, flat, rows = P("tab", "blk", None), P("tab"), P("tab", None)
    return jax.shard_map(
        local,
        mesh=mesh,
        in_specs=(tokens, flat, tokens, P()) + (rows,) * 15,
        out_specs=(tokens, tokens) + (rows,) * 20,
        check_vma=False,
    )
```

```python
import math
from functools import partial

import jax
import jax.numpy as jnp
from jax import lax
from jax.experimental import pallas as pl
from jax.experimental.pallas import tpu as pltpu
from jax.sharding import PartitionSpec as P

D = 768
H = 12
HD = 64
LEN = 512
FF = 3072
PAIR = 2 * HD

EPS = 1e-06
NEGATIVE = -1e30
BETA_ONE = 0.9
BETA_TWO = 0.999
ADAM_EPS = 1e-08
DECAY = 0.01
RATES = (1.0, 15.0, 1.0, 0.5, 5.0)

F32 = jnp.float32
BF16 = jnp.bfloat16
MESH_ID = pl.DeviceIdType.MESH
VMEM_ALL = 64 * 1000 * 1024


def layer_norm(hidden, gain_vec, shift_vec):
    row_mean = jnp.mean(hidden, axis=-1, keepdims=True)
    centred = hidden - row_mean
    variance = jnp.mean(centred * centred, axis=-1, keepdims=True)
    return centred * lax.rsqrt(variance + EPS) * gain_vec + shift_vec


def inner(left, right):
    return lax.dot_general(left, right, (((0,), (0,)), ((), ())), preferred_element_type=F32)


def back_mul(left, right):
    return lax.dot_general(left, right, (((1,), (1,)), ((), ())), preferred_element_type=F32)


def adam(master, gradient, first_moment, second_moment, rate_now, step_float):
    moment_new = BETA_ONE * first_moment + (1.0 - BETA_ONE) * gradient
    square_new = BETA_TWO * second_moment + (1.0 - BETA_TWO) * gradient * gradient
    fix_one = 1.0 - jnp.power(BETA_ONE, step_float)
    fix_two = 1.0 - jnp.power(BETA_TWO, step_float)
    update = moment_new / fix_one / (jnp.sqrt(square_new / fix_two) + ADAM_EPS)
    master_new = master - rate_now * (update + DECAY * master)
    return (moment_new, square_new, master_new, master_new.astype(BF16))


def head_masks(dtype):
    lane = lax.broadcasted_iota(jnp.int32, (1, PAIR), 1)
    return [(lane < HD).astype(dtype), (lane >= HD).astype(dtype)]


def attn_fwd_kernel(len_ref, q_ref, k_ref, v_ref, o_ref, l_ref):
    live = len_ref[pl.program_id(0)]
    masks = head_masks(BF16)
    keys = k_ref[...]
    values = v_ref[...]
    rows = 256
    key_at = lax.broadcasted_iota(jnp.int32, (1, LEN), 1)
    bias = jnp.where(key_at < live, 0.0, NEGATIVE)
    lane = lax.broadcasted_iota(jnp.int32, (1, PAIR), 1)
    for start in range(0, LEN, rows):
        query = q_ref[pl.ds(start, rows), :] * jnp.asarray(HD ** (-0.5), BF16)
        mixed, logs = [], []
        for head in range(2):
            scores = back_mul(query * masks[head], keys) + bias
            top = jnp.max(scores, axis=-1, keepdims=True)
            raised = jnp.exp(scores - top)
            total = jnp.sum(raised, axis=-1, keepdims=True)
            probs = (raised * (1.0 / total)).astype(BF16)
            mixed.append(jnp.dot(probs, values, preferred_element_type=F32))
            logs.append(top + jnp.log(total))
        o_ref[pl.ds(start, rows), :] = jnp.where(lane < HD, mixed[0], mixed[1]).astype(BF16)
        both = jnp.where(lane < HD, logs[0], logs[1])
        flat = both.T
        l_ref[0, 0, 0:1, pl.ds(start, rows)] = flat[0:1, :]
        l_ref[0, 0, 1:2, pl.ds(start, rows)] = flat[HD : HD + 1, :]


def attention_forward(lengths, qkv, tables):
    pairs = H // 2
    spec = lambda part: pl.BlockSpec((LEN, PAIR), lambda t, h, n: (t, part * pairs + h))
    return pl.pallas_call(
        attn_fwd_kernel,
        grid_spec=pltpu.PrefetchScalarGridSpec(
            num_scalar_prefetch=1,
            grid=(tables, pairs),
            in_specs=[spec(0), spec(1), spec(2)],
            out_specs=[
                pl.BlockSpec((LEN, PAIR), lambda t, h, n: (t, h)),
                pl.BlockSpec((1, 1, 8, LEN), lambda t, h, n: (t, h, 0, 0)),
            ],
        ),
        out_shape=[
            jax.ShapeDtypeStruct((tables * LEN, D), BF16),
            jax.ShapeDtypeStruct((tables, pairs, 8, LEN), F32),
        ],
        name="attn_fwd",
    )(lengths, qkv, qkv, qkv)


def attn_bwd_kernel(len_ref, q_ref, k_ref, v_ref, o_ref, l_ref, do_ref, d_ref, sums_ref):
    live = len_ref[pl.program_id(0)]
    masks = head_masks(BF16)
    keys = k_ref[...]
    values = v_ref[...]
    query = q_ref[...] * jnp.asarray(HD ** (-0.5), BF16)
    grad_out = do_ref[...]
    dots = (grad_out.astype(F32) * o_ref[...].astype(F32)).T
    rows = 256
    q_masked = [query * m for m in masks]
    g_masked = [grad_out * m for m in masks]
    deltas = [jnp.sum(dots[h * HD : (h + 1) * HD, :], axis=0, keepdims=True) for h in range(2)]
    logs = [l_ref[0, 0, h : h + 1, :] for h in range(2)]
    grad_q = jnp.zeros((LEN, PAIR), F32)
    sum_v = jnp.zeros((1, PAIR), F32)
    for start in range(0, LEN, rows):
        part_k = keys[start : start + rows, :]
        part_v = values[start : start + rows, :]
        key_at = start + lax.broadcasted_iota(jnp.int32, (rows, 1), 0)
        bias = jnp.where(key_at < live, 0.0, NEGATIVE)
        grad_k = jnp.zeros((rows, PAIR), F32)
        grad_v = jnp.zeros((rows, PAIR), F32)
        for head in range(2):
            scores = back_mul(part_k, q_masked[head])
            probs = jnp.exp(scores + bias - logs[head])
            grad_probs = back_mul(part_v, g_masked[head])
            grad_s = (probs * (grad_probs - deltas[head])).astype(BF16)
            grad_v += jnp.dot(probs.astype(BF16), g_masked[head], preferred_element_type=F32)
            grad_k += jnp.dot(grad_s, q_masked[head], preferred_element_type=F32)
            grad_q += inner(grad_s, part_k * masks[head])
        d_ref[1, pl.ds(start, rows), :] = grad_k.astype(BF16)
        d_ref[2, pl.ds(start, rows), :] = grad_v.astype(BF16)
        sum_v += jnp.sum(grad_v, axis=0, keepdims=True)
    grad_q = grad_q * HD ** (-0.5)
    d_ref[0, :, :] = grad_q.astype(BF16)
    sums_ref[0, 0, 0:1, :] = jnp.sum(grad_q, axis=0, keepdims=True)
    sums_ref[0, 0, 1:2, :] = sum_v


def attention_backward(lengths, qkv, mixed, logs, grad_mixed, tables):
    pairs = H // 2
    spec = lambda part: pl.BlockSpec((LEN, PAIR), lambda t, h, n: (t, part * pairs + h))
    block = pl.BlockSpec((LEN, PAIR), lambda t, h, n: (t, h))
    return pl.pallas_call(
        attn_bwd_kernel,
        grid_spec=pltpu.PrefetchScalarGridSpec(
            num_scalar_prefetch=1,
            grid=(tables, pairs),
            in_specs=[
                spec(0),
                spec(1),
                spec(2),
                block,
                pl.BlockSpec((1, 1, 8, LEN), lambda t, h, n: (t, h, 0, 0)),
                block,
            ],
            out_specs=[
                pl.BlockSpec((3, LEN, PAIR), lambda t, h, n: (0, t, h)),
                pl.BlockSpec((1, 1, 8, PAIR), lambda t, h, n: (t, h, 0, 0)),
            ],
        ),
        out_shape=[
            jax.ShapeDtypeStruct((3, tables * LEN, D), BF16),
            jax.ShapeDtypeStruct((tables, pairs, 8, PAIR), F32),
        ],
        name="attn_bwd",
    )(lengths, qkv, qkv, qkv, mixed, logs, grad_mixed)


def place():
    tab, blk = lax.axis_index("tab"), lax.axis_index("blk")
    return tab // 2, tab % 2, blk // 2, blk % 2


class Wires:
    def __init__(self, send, recv):
        self.send, self.recv, self.count, self.sent = send, recv, 0, []

    def copy(self, src, dst, to):
        index, self.count = self.count, self.count + 1
        z, x, y, c = to
        made = pltpu.make_async_remote_copy(
            src_ref=src,
            dst_ref=dst,
            send_sem=self.send.at[index],
            recv_sem=self.recv.at[index],
            device_id=(z * 2 + x, y * 2 + c),
            device_id_type=MESH_ID,
        )
        made.start()
        self.sent.append(made)
        return made

    def finish(self):
        for made in self.sent:
            made.wait_send()


def greet(peers):
    barrier = pltpu.get_barrier_semaphore()
    for z, x, y, c in peers:
        pl.semaphore_signal(
            barrier, inc=1, device_id=(z * 2 + x, y * 2 + c), device_id_type=MESH_ID
        )
    pl.semaphore_wait(barrier, len(peers))


def all_peers():
    z, x, y, c = place()
    z_peers = [((z + j) % 4, x, y, c) for j in range(1, 4)]
    rest = [(z, 1 - x, y, c), (z, x, 1 - y, c), (z, x, y, 1 - c), (z, x, 1 - y, 1 - c)]
    return z_peers + rest


def by_columns(width):
    return lambda ref, t, part: ref.at[t, :, pl.ds(pl.multiple_of(part * width, 128), width)]


def by_rows(height):
    return lambda ref, t, part: ref.at[t, pl.ds(pl.multiple_of(part * height, 16), height), :]


PIECES = (
    (by_columns(FF // 4), True),
    (by_rows(FF // 32), True),
    (by_columns(3 * D // 2), False),
    (by_columns(D // 2), False),
)
N_WIRES = 160


def gather_kernel(
    x_in, cot_in, up_in, down_in, qkv_in, out_in, vec_in,
    x_out, cot_out, up_out, down_out, qkv_out, out_out, vec_out,
    send, recv, own,
):
    z, x, y, c = place()
    tab, blk = z * 2 + x, y * 2 + c
    greet(all_peers())
    wires = Wires(send, recv)
    shards = (up_in, down_in, qkv_in, out_in)
    wholes = (up_out, down_out, qkv_out, out_out)
    share, span = x_in.shape[0] // 4, x_in.shape[1]
    mine = pl.ds(blk * share, share)
    kept = [
        pltpu.make_async_copy(x_in.at[mine], x_out.at[:, pl.ds(blk * span, span), :], own.at[0]),
        pltpu.make_async_copy(cot_in.at[mine], cot_out.at[:, pl.ds(blk * span, span), :], own.at[1]),
        pltpu.make_async_copy(vec_in.at[0], vec_out.at[tab], own.at[2]),
    ]
    for at in range(4):
        kept.append(pltpu.make_async_copy(shards[at].at[0], wholes[at].at[tab], own.at[3 + at]))
    for made in kept:
        made.start()

    def trade(src, dst):
        made = []
        for other in ((z, x, 1 - y, c), (z, x, 1 - y, 1 - c), (z, x, y, 1 - c)):
            their = other[2] * 2 + other[3]
            made.append(
                wires.copy(
                    src.at[pl.ds(their * share, share)],
                    dst.at[:, pl.ds(blk * span, span), :],
                    other,
                )
            )
        return made

    waits = trade(x_in, x_out)
    along_z = []
    for at in range(4):
        piece, split = PIECES[at]
        part = blk if split else c
        along_z.append(
            [
                wires.copy(
                    piece(shards[at], 0, part),
                    piece(wholes[at], tab, part),
                    ((z + j) % 4, x, y, c),
                )
                for j in range(1, 4)
            ]
        )
    vec_z = [
        wires.copy(vec_in.at[0], vec_out.at[tab], ((z + j) % 4, x, y, c)) for j in range(1, 4)
    ]
    for at in range(4):
        piece, split = PIECES[at]
        whole = wholes[at]
        part = blk if split else c
        along_x, along_y = [], []

        def onward(t, local_part, kind):
            src = piece(whole, t, local_part)
            if kind == "y":
                along_y.append((t, wires.copy(src, src, (z, x, 1 - y, c))))
            else:
                waits.append(wires.copy(src, src, (z, x, y, 1 - c)))

        src = piece(shards[at], 0, part)
        along_x.append(wires.copy(src, piece(whole, tab, part), (z, 1 - x, y, c)))
        for j in range(1, 4):
            t = (z + 4 - j) % 4 * 2 + x
            along_z[at][j - 1].wait_recv()
            src = piece(whole, t, part)
            along_x.append(wires.copy(src, src, (z, 1 - x, y, c)))
            if split:
                onward(t, part, "y")
            onward(t, part, "c")
        for j in range(4):
            t = (z + 4 - j) % 4 * 2 + 1 - x
            along_x[j].wait_recv()
            if split:
                onward(t, part, "y")
            onward(t, part, "c")
        for t, made in along_y:
            made.wait_recv()
            onward(t, (1 - y) * 2 + c, "c")
    src = vec_in.at[0]
    vec_x = [wires.copy(src, vec_out.at[tab], (z, 1 - x, y, c))]
    for j in range(1, 4):
        t = (z + 4 - j) % 4 * 2 + x
        vec_z[j - 1].wait_recv()
        vec_x.append(wires.copy(vec_out.at[t], vec_out.at[t], (z, 1 - x, y, c)))
    waits += trade(cot_in, cot_out)
    for made in waits + vec_x:
        made.wait_recv()
    wires.finish()
    for made in kept:
        made.wait()


def gather_all(tables, cotangent, up, down, qkv, out, vec):
    share, span = tables.shape[0] // 4, tables.shape[1] * 4
    vmem = pl.BlockSpec(memory_space=pltpu.VMEM)
    hbm = pl.BlockSpec(memory_space=pl.ANY)
    shape = lambda a: jax.ShapeDtypeStruct((8,) + a.shape[1:], BF16)
    return pl.pallas_call(
        gather_kernel,
        in_specs=[vmem] * 7,
        out_specs=[hbm] * 7,
        out_shape=[
            jax.ShapeDtypeStruct((share, span, D), BF16),
            jax.ShapeDtypeStruct((share, span, D), BF16),
            shape(up), shape(down), shape(qkv), shape(out), shape(vec),
        ],
        scratch_shapes=[
            pltpu.SemaphoreType.DMA((N_WIRES,)),
            pltpu.SemaphoreType.DMA((N_WIRES,)),
            pltpu.SemaphoreType.DMA((7,)),
        ],
        compiler_params=pltpu.CompilerParams(
            collective_id=0, has_side_effects=True, vmem_limit_bytes=VMEM_ALL
        ),
        name="gather_all",
    )(tables, cotangent, up, down, qkv, out, vec)


class Plan:
    def __init__(self, send, recv):
        self.send, self.recv, self.makers = send, recv, []

    def add(self, maker):
        self.makers.append(maker)
        return len(self.makers) - 1

    def build(self, index):
        src, dst, (z, x, y, c) = self.makers[index]()
        return pltpu.make_async_remote_copy(
            src_ref=src,
            dst_ref=dst,
            send_sem=self.send.at[index],
            recv_sem=self.recv.at[index],
            device_id=(z * 2 + x, y * 2 + c),
            device_id_type=MESH_ID,
        )

    def start(self, index):
        self.build(index).start()

    def arrived(self, index):
        self.build(index).wait_recv()

    def finish(self):
        for index in range(len(self.makers)):
            self.build(index).wait_send()


class Slab:
    def __init__(self, rows, cols, split, axis, first=0, dtype=BF16):
        self.rows, self.cols, self.split, self.axis = rows, cols, split, axis
        self.first, self.dtype = first, dtype
        self.tile = 128 if axis == 1 else (16 if dtype == BF16 else 8)

    def cut(self, index):
        if self.axis == 1:
            return pl.ds(0, self.rows), pl.ds(
                pl.multiple_of(index * self.cols, self.tile), self.cols
            )
        start = pl.multiple_of(self.first + index * self.rows, self.tile)
        return pl.ds(start, self.rows), pl.ds(0, self.cols)

    def scratch(self):
        ways = 2 if self.split else 1
        vmem = lambda *lead: pltpu.VMEM(lead + (self.rows, self.cols), self.dtype)
        late = vmem(4, 2) if self.split else vmem(1, 1)
        return [vmem(ways, 4, 2), vmem(ways, 4, 2), late, vmem(4), vmem(3), vmem()]

    def copies(self):
        return (2 if self.split else 1) + 1 + 1 + 3 + 3


class Reduction:
    def __init__(self, slab, source, target, scratch, plan, own, own_at):
        self.slab, self.source, self.target, self.plan = slab, source, target, plan
        self.held, self.from_c, self.from_y, self.from_x, self.from_z, self.done = scratch
        self.own, self.own_at = own, own_at
        z, x, y, c = place()
        self.at = z, x, y, c
        self.slot = y if slab.split else 0
        side = (z, x, y, 1 - c)
        over = (z, x, 1 - y, c)

        def index_of(half, core):
            return half * 2 + core if slab.split else core

        def cut_all(ref, index):
            rows, cols = slab.cut(index)
            return ref.at[:, :, rows, cols]

        def cut_out(index):
            rows, cols = slab.cut(index)
            return target.at[rows, cols]

        ways = 2 if slab.split else 1
        self.loads = [
            lambda half=half: pltpu.make_async_copy(
                cut_all(source, index_of(half, c)), self.held.at[half], own.at[own_at + half]
            )
            for half in range(ways)
        ]
        self.to_core = [
            plan.add(
                lambda half=half: (
                    cut_all(source, index_of(half, 1 - c)), self.from_c.at[half], side,
                )
            )
            for half in range(ways)
        ]
        if slab.split:
            self.to_y = plan.add(lambda: (self.held.at[1 - y], self.from_y, over))
        else:
            self.to_y = plan.add(lambda: (self.done, self.from_y.at[0, 0], over))
        self.to_x = plan.add(
            lambda: (self.held.at[self.slot, :, 1 - x], self.from_x, (z, 1 - x, y, c))
        )
        self.to_z = [
            plan.add(
                lambda j=j: (
                    self.held.at[self.slot, (z + j) % 4, x],
                    self.from_z.at[j - 1],
                    ((z + j) % 4, x, y, c),
                )
            )
            for j in range(1, 4)
        ]
        mine = lambda: cut_out(index_of(y, c))
        self.store = lambda: pltpu.make_async_copy(self.done, mine(), own.at[own_at + 2])
        self.share_core = plan.add(lambda: (self.done, mine(), side))
        if slab.split:
            theirs = lambda: cut_out(index_of(1 - y, c))
            self.share_y = plan.add(lambda: (self.done, mine(), over))
            self.share_far = plan.add(lambda: (theirs(), theirs(), side))

    def begin(self):
        for load in self.loads:
            load().start()
        for index in self.to_core:
            self.plan.start(index)

    def summed(self, total, *others):
        value = total[...].astype(F32)
        for other in others:
            value = value + other[...].astype(F32)
        total[...] = value.astype(self.slab.dtype)

    def after_core(self):
        for half, load in enumerate(self.loads):
            load().wait()
            self.plan.arrived(self.to_core[half])

        def step(t, carry):
            for half in range(len(self.loads)):
                self.summed(self.held.at[half, t // 2, t % 2], self.from_c.at[half, t // 2, t % 2])
            return carry

        lax.fori_loop(0, 8, step, 0)
        self.plan.start(self.to_y if self.slab.split else self.to_x)

    def after_y(self):
        if not self.slab.split:
            return
        self.plan.arrived(self.to_y)

        def step(t, carry):
            self.summed(self.held.at[self.slot, t // 2, t % 2], self.from_y.at[t // 2, t % 2])
            return carry

        lax.fori_loop(0, 8, step, 0)
        self.plan.start(self.to_x)

    def after_x(self):
        z, x, y, c = self.at
        self.plan.arrived(self.to_x)

        def step(t, carry):
            self.summed(self.held.at[self.slot, t, x], self.from_x.at[t])
            return carry

        lax.fori_loop(0, 4, step, 0)
        for index in self.to_z:
            self.plan.start(index)

    def after_z(self):
        z, x, y, c = self.at
        for index in self.to_z:
            self.plan.arrived(index)
        value = self.held[self.slot, z, x].astype(F32)
        for j in range(3):
            value = value + self.from_z[j].astype(F32)
        self.done[...] = value.astype(self.slab.dtype)
        if self.slab.split:
            self.plan.start(self.share_y)
            self.plan.start(self.share_core)
            self.store().start()
        else:
            self.plan.start(self.to_y)

    def after_final(self):
        if self.slab.split:
            self.plan.arrived(self.share_y)
            self.plan.start(self.share_far)
        else:
            self.plan.arrived(self.to_y)
            self.plan.build(self.to_y).wait_send()
            self.summed(self.done, self.from_y.at[0, 0])
            self.plan.start(self.share_core)
            self.store().start()

    def end(self):
        self.plan.arrived(self.share_core)
        if self.slab.split:
            self.plan.arrived(self.share_far)
        self.store().wait()

    def finish_sends(self):
        done_early = () if self.slab.split else (self.to_y,)
        sends = self.to_core + [self.to_y, self.to_x] + self.to_z + [self.share_core]
        if self.slab.split:
            sends += [self.share_y, self.share_far]
        for index in sends:
            if index not in done_early:
                self.plan.build(index).wait_send()


STAGES = ("begin", "after_core", "after_y", "after_x", "after_z", "after_final", "end")

SLABS = (
    (0, Slab(96, FF // 4, True, 1)),
    (1, Slab(32, D, True, 0)),
    (1, Slab(128, D, False, 0, first=128)),
    (2, Slab(96, 3 * D // 2, False, 1)),
    (3, Slab(96, D // 2, False, 1)),
    (4, Slab(8, 128, False, 0, dtype=F32)),
)


def reduce_kernel(*refs):
    (gin_in, y_in), sources = refs[:2], refs[2:7]
    (gin_out, y_out), targets = refs[7:9], refs[9:14]
    scratch, (send, recv, own) = refs[14:-3], refs[-3:]
    z, x, y, c = place()
    blk = y * 2 + c
    greet(all_peers())
    plan = Plan(send, recv)
    share, span = gin_out.shape[0] // 4, gin_out.shape[1]
    kept, traded = [], []
    works = []
    for at, (number, slab) in enumerate(SLABS):
        part = scratch[6 * at : 6 * at + 6]
        works.append(
            Reduction(slab, sources[number], targets[number], part, plan, own, 2 + 3 * at)
        )
    for at, (src, dst) in enumerate(((gin_in, gin_out), (y_in, y_out))):
        mine = dst.at[pl.ds(blk * share, share)]
        kept.append(
            pltpu.make_async_copy(src.at[:, pl.ds(blk * span, span), :], mine, own.at[at])
        )
        kept[-1].start()
        for other in ((z, x, 1 - y, c), (z, x, 1 - y, 1 - c), (z, x, y, 1 - c)):
            their = other[2] * 2 + other[3]
            maker = lambda src=src, mine=mine, their=their, other=other: (
                src.at[:, pl.ds(their * span, span), :], mine, other,
            )
            traded.append(plan.add(maker))
    for stage in STAGES:
        for work in works:
            getattr(work, stage)()
        if stage == "after_y":
            for index in traded:
                plan.start(index)
    for index in traded:
        plan.arrived(index)
    for work in works:
        work.finish_sends()
    for index in traded:
        plan.build(index).wait_send()
    for made in kept:
        made.wait()


def reduce_all(grad_in, result, up, down, qkv, out, vec):
    share, length = grad_in.shape[:2]
    vmem = pl.BlockSpec(memory_space=pltpu.VMEM)
    hbm = pl.BlockSpec(memory_space=pl.ANY)
    shape = lambda a: jax.ShapeDtypeStruct(a.shape[2:], a.dtype)
    back = jax.ShapeDtypeStruct((share * 4, length // 4, D), BF16)
    grads = (up, down, qkv, out, vec)
    scratch = [s for _, slab in SLABS for s in slab.scratch()]
    wires = 6 + sum(slab.copies() for _, slab in SLABS)
    return pl.pallas_call(
        reduce_kernel,
        in_specs=[vmem] * 2 + [hbm] * 5,
        out_specs=[hbm] * 7,
        out_shape=[back, back] + [shape(a) for a in grads],
        scratch_shapes=scratch
        + [
            pltpu.SemaphoreType.DMA((wires,)),
            pltpu.SemaphoreType.DMA((wires,)),
            pltpu.SemaphoreType.DMA((2 + 3 * len(SLABS),)),
        ],
        compiler_params=pltpu.CompilerParams(
            collective_id=1, has_side_effects=True, vmem_limit_bytes=VMEM_ALL
        ),
        name="reduce_all",
    )(grad_in, result, *grads)


def local(*args):
    tables, lengths, cotangent, step_count = args[:4]
    masters, firsts, seconds = args[4:9], args[9:14], args[14:19]
    w_qkv, w_out, w_up, w_down, vectors = masters
    blocks = lax.axis_size("blk")
    shards = lax.axis_size("tab")
    table_count, local_len = tables.shape[:2]
    share = table_count // blocks
    tuned = shards == 8 and blocks == 4
    vec_pad = jnp.pad(vectors.astype(BF16).T, ((0, 4), (0, 128 - vectors.shape[0])))
    narrow = [w.astype(BF16) for w in (w_up, w_down, w_qkv, w_out)]
    if tuned:
        mine, cot, *wholes = gather_all(
            tables, cotangent, *[w[None] for w in narrow], vec_pad[None]
        )
    else:
        spread = partial(lax.all_to_all, axis_name="blk", split_axis=0, concat_axis=1, tiled=True)
        mine, cot = spread(tables), spread(cotangent)
        wholes = [lax.all_gather(w, "tab", axis=0) for w in narrow + [vec_pad]]
    full_up, full_down, full_qkv, full_out = [
        w.reshape(-1, w.shape[-1]) for w in wholes[:4]
    ]
    vec_f = wholes[4][:, :12, : vectors.shape[0]].transpose(1, 0, 2).reshape(12, D).astype(F32)
    my_lengths = lax.dynamic_slice(lengths, (lax.axis_index("blk") * share,), (share,))
    bias_up = vec_f[8:12].reshape(-1)
    bias_qkv = jnp.concatenate([vec_f[0], jnp.zeros((D,), F32), vec_f[1]])

    rows = mine.reshape(-1, D)
    qkv = (jnp.dot(rows, full_qkv, preferred_element_type=F32) + bias_qkv).astype(BF16)
    mixed, logs = attention_forward(my_lengths, qkv, share)
    attn_out = jnp.dot(mixed, full_out, preferred_element_type=F32) + vec_f[2]
    normed_one, norm_one_back = jax.vjp(
        layer_norm, rows.astype(F32) + attn_out, vec_f[4], vec_f[5]
    )
    normed_b = normed_one.astype(BF16)
    hidden = jnp.dot(normed_b, full_up, preferred_element_type=F32) + bias_up
    below = 0.5 * (1.0 + lax.erf(hidden * 0.5**0.5))
    active_b = (hidden * below).astype(BF16)
    slope = below + hidden * jnp.exp(-0.5 * hidden * hidden) * (2.0 * math.pi) ** -0.5
    active_b, slope = lax.optimization_barrier((active_b, slope.astype(BF16)))
    branch = jnp.dot(active_b, full_down, preferred_element_type=F32) + vec_f[3]
    result, norm_two_back = jax.vjp(layer_norm, normed_one + branch, vec_f[6], vec_f[7])
    result = result.astype(BF16).reshape(mine.shape)
    grad_two, grad_g2, grad_c2 = norm_two_back(cot.reshape(-1, D).astype(F32))
    grad_b2 = jnp.sum(grad_two, axis=0)
    branch_b = grad_two.astype(BF16)
    gw_down = inner(active_b, branch_b).astype(BF16)
    grad_hidden = back_mul(branch_b, full_down) * slope.astype(F32)
    grad_b1 = jnp.sum(grad_hidden, axis=0)
    hidden_b = grad_hidden.astype(BF16)
    gw_up = inner(normed_b, hidden_b).astype(BF16)
    grad_one, grad_g1, grad_c1 = norm_one_back(grad_two + back_mul(hidden_b, full_up))
    grad_bo = jnp.sum(grad_one, axis=0)
    attn_b = grad_one.astype(BF16)
    gw_out = inner(mixed, attn_b).astype(BF16)
    grad_mixed = back_mul(attn_b, full_out).astype(BF16)
    grad_three, sums = attention_backward(my_lengths, qkv, mixed, logs, grad_mixed, share)
    sums = jnp.sum(sums[:, :, :2], axis=0)
    grad_bq, grad_bv = sums[:, 0].reshape(-1), sums[:, 1].reshape(-1)
    grad_qkv = jnp.concatenate([grad_three[i] for i in range(3)], axis=1)
    gw_qkv = inner(rows, grad_qkv).astype(BF16)
    grad_in = grad_one + back_mul(grad_qkv, full_qkv)
    grad_in = grad_in.astype(BF16).reshape(mine.shape)
    gw_vec = jnp.concatenate(
        [
            jnp.stack([grad_bq, grad_bv, grad_bo, grad_b2, grad_g1, grad_c1, grad_g2, grad_c2]),
            grad_b1.reshape(4, D),
        ]
    )
    owned = vectors.shape[0]
    if tuned:
        pads = ((0, 0), (0, 0), (0, 2), (0, 128 - owned))
        wide_vec = jnp.pad(gw_vec.reshape(2, 6, shards, owned).transpose(2, 0, 1, 3), pads)
        by_owner = lambda g: g.reshape(4, 2, -1, g.shape[-1])
        grad_input, output, *sums = reduce_all(
            grad_in, result, by_owner(gw_up), by_owner(gw_down), by_owner(gw_qkv),
            by_owner(gw_out), wide_vec.reshape(4, 2, 16, 128),
        )
        sum_vec = sums[4].reshape(2, 8, 128)[:, :6, :owned].reshape(12, owned).T
        shares = [s.astype(F32) for s in (sums[2], sums[3], sums[0], sums[1], sum_vec)]
    else:
        back = partial(lax.all_to_all, axis_name="blk", split_axis=1, concat_axis=0, tiled=True)
        grad_input, output = back(grad_in), back(result)

        def collect(grad):
            part = lax.psum_scatter(
                grad.reshape(shards, -1, grad.shape[-1]), "tab", scatter_dimension=0
            )
            return lax.psum(part.astype(BF16), "blk").astype(F32)

        shares = [collect(g) for g in (gw_qkv, gw_out, gw_up, gw_down)]
        shares.append(collect(gw_vec.T.astype(BF16)))
    grad_input = grad_input.astype(F32)
    step_float = step_count[0].astype(F32)
    results = [output, grad_input]
    for at in range(5):
        results.extend(
            adam(masters[at], shares[at], firsts[at], seconds[at], RATES[at], step_float)
        )
    return tuple(results)


def solution(mesh):
    tokens, flat, rows = P("tab", "blk", None), P("tab"), P("tab", None)
    return jax.shard_map(
        local,
        mesh=mesh,
        in_specs=(tokens, flat, tokens, P()) + (rows,) * 15,
        out_specs=(tokens, tokens) + (rows,) * 20,
        check_vma=False,
    )
```

```python
import math
from functools import partial

import jax
import jax.numpy as jnp
from jax import lax
from jax.experimental import pallas as pl
from jax.experimental.pallas import tpu as pltpu
from jax.sharding import PartitionSpec as P

D = 768
H = 12
HD = 64
LEN = 512
FF = 3072
PAIR = 2 * HD

EPS = 1e-06
NEGATIVE = -1e30
BETA_ONE = 0.9
BETA_TWO = 0.999
ADAM_EPS = 1e-08
DECAY = 0.01
RATES = (1.0, 15.0, 1.0, 0.5, 5.0)

F32 = jnp.float32
BF16 = jnp.bfloat16
MESH_ID = pl.DeviceIdType.MESH
VMEM_ALL = 64 * 1000 * 1024


def layer_norm(hidden, gain_vec, shift_vec):
    row_mean = jnp.mean(hidden, axis=-1, keepdims=True)
    centred = hidden - row_mean
    variance = jnp.mean(centred * centred, axis=-1, keepdims=True)
    return centred * lax.rsqrt(variance + EPS) * gain_vec + shift_vec


def inner(left, right):
    return lax.dot_general(left, right, (((0,), (0,)), ((), ())), preferred_element_type=F32)


def back_mul(left, right):
    return lax.dot_general(left, right, (((1,), (1,)), ((), ())), preferred_element_type=F32)


def adam(master, gradient, first_moment, second_moment, rate_now, step_float):
    moment_new = BETA_ONE * first_moment + (1.0 - BETA_ONE) * gradient
    square_new = BETA_TWO * second_moment + (1.0 - BETA_TWO) * gradient * gradient
    fix_one = 1.0 - jnp.power(BETA_ONE, step_float)
    fix_two = 1.0 - jnp.power(BETA_TWO, step_float)
    update = moment_new / fix_one / (jnp.sqrt(square_new / fix_two) + ADAM_EPS)
    master_new = master - rate_now * (update + DECAY * master)
    return (moment_new, square_new, master_new, master_new.astype(BF16))


def head_masks(dtype):
    lane = lax.broadcasted_iota(jnp.int32, (1, PAIR), 1)
    return [(lane < HD).astype(dtype), (lane >= HD).astype(dtype)]


def attn_fwd_kernel(len_ref, q_ref, k_ref, v_ref, o_ref, l_ref):
    live = len_ref[pl.program_id(0)]
    masks = head_masks(BF16)
    keys = k_ref[...]
    values = v_ref[...]
    rows = 256
    key_at = lax.broadcasted_iota(jnp.int32, (1, LEN), 1)
    bias = jnp.where(key_at < live, 0.0, NEGATIVE)
    lane = lax.broadcasted_iota(jnp.int32, (1, PAIR), 1)
    for start in range(0, LEN, rows):
        query = q_ref[pl.ds(start, rows), :] * jnp.asarray(HD ** (-0.5), BF16)
        mixed, logs = [], []
        for head in range(2):
            scores = back_mul(query * masks[head], keys) + bias
            top = jnp.max(scores, axis=-1, keepdims=True)
            raised = jnp.exp(scores - top)
            total = jnp.sum(raised, axis=-1, keepdims=True)
            probs = (raised * (1.0 / total)).astype(BF16)
            mixed.append(jnp.dot(probs, values, preferred_element_type=F32))
            logs.append(top + jnp.log(total))
        o_ref[pl.ds(start, rows), :] = jnp.where(lane < HD, mixed[0], mixed[1]).astype(BF16)
        both = jnp.where(lane < HD, logs[0], logs[1])
        flat = both.T
        l_ref[0, 0, 0:1, pl.ds(start, rows)] = flat[0:1, :]
        l_ref[0, 0, 1:2, pl.ds(start, rows)] = flat[HD : HD + 1, :]


def attention_forward(lengths, qkv, tables):
    pairs = H // 2
    spec = lambda part: pl.BlockSpec((LEN, PAIR), lambda t, h, n: (t, part * pairs + h))
    return pl.pallas_call(
        attn_fwd_kernel,
        grid_spec=pltpu.PrefetchScalarGridSpec(
            num_scalar_prefetch=1,
            grid=(tables, pairs),
            in_specs=[spec(0), spec(1), spec(2)],
            out_specs=[
                pl.BlockSpec((LEN, PAIR), lambda t, h, n: (t, h)),
                pl.BlockSpec((1, 1, 8, LEN), lambda t, h, n: (t, h, 0, 0)),
            ],
        ),
        out_shape=[
            jax.ShapeDtypeStruct((tables * LEN, D), BF16),
            jax.ShapeDtypeStruct((tables, pairs, 8, LEN), F32),
        ],
        name="attn_fwd",
    )(lengths, qkv, qkv, qkv)


def attn_bwd_kernel(len_ref, q_ref, k_ref, v_ref, o_ref, l_ref, do_ref, d_ref, sums_ref):
    live = len_ref[pl.program_id(0)]
    masks = head_masks(BF16)
    keys = k_ref[...]
    values = v_ref[...]
    query = q_ref[...] * jnp.asarray(HD ** (-0.5), BF16)
    grad_out = do_ref[...]
    dots = (grad_out.astype(F32) * o_ref[...].astype(F32)).T
    rows = 256
    q_masked = [query * m for m in masks]
    g_masked = [grad_out * m for m in masks]
    deltas = [jnp.sum(dots[h * HD : (h + 1) * HD, :], axis=0, keepdims=True) for h in range(2)]
    logs = [l_ref[0, 0, h : h + 1, :] for h in range(2)]
    grad_q = jnp.zeros((LEN, PAIR), F32)
    sum_v = jnp.zeros((1, PAIR), F32)
    for start in range(0, LEN, rows):
        part_k = keys[start : start + rows, :]
        part_v = values[start : start + rows, :]
        key_at = start + lax.broadcasted_iota(jnp.int32, (rows, 1), 0)
        bias = jnp.where(key_at < live, 0.0, NEGATIVE)
        grad_k = jnp.zeros((rows, PAIR), F32)
        grad_v = jnp.zeros((rows, PAIR), F32)
        for head in range(2):
            scores = back_mul(part_k, q_masked[head])
            probs = jnp.exp(scores + bias - logs[head])
            grad_probs = back_mul(part_v, g_masked[head])
            grad_s = (probs * (grad_probs - deltas[head])).astype(BF16)
            grad_v += jnp.dot(probs.astype(BF16), g_masked[head], preferred_element_type=F32)
            grad_k += jnp.dot(grad_s, q_masked[head], preferred_element_type=F32)
            grad_q += inner(grad_s, part_k * masks[head])
        d_ref[1, pl.ds(start, rows), :] = grad_k.astype(BF16)
        d_ref[2, pl.ds(start, rows), :] = grad_v.astype(BF16)
        sum_v += jnp.sum(grad_v, axis=0, keepdims=True)
    grad_q = grad_q * HD ** (-0.5)
    d_ref[0, :, :] = grad_q.astype(BF16)
    sums_ref[0, 0, 0:1, :] = jnp.sum(grad_q, axis=0, keepdims=True)
    sums_ref[0, 0, 1:2, :] = sum_v


def attention_backward(lengths, qkv, mixed, logs, grad_mixed, tables):
    pairs = H // 2
    spec = lambda part: pl.BlockSpec((LEN, PAIR), lambda t, h, n: (t, part * pairs + h))
    block = pl.BlockSpec((LEN, PAIR), lambda t, h, n: (t, h))
    return pl.pallas_call(
        attn_bwd_kernel,
        grid_spec=pltpu.PrefetchScalarGridSpec(
            num_scalar_prefetch=1,
            grid=(tables, pairs),
            in_specs=[
                spec(0),
                spec(1),
                spec(2),
                block,
                pl.BlockSpec((1, 1, 8, LEN), lambda t, h, n: (t, h, 0, 0)),
                block,
            ],
            out_specs=[
                pl.BlockSpec((3, LEN, PAIR), lambda t, h, n: (0, t, h)),
                pl.BlockSpec((1, 1, 8, PAIR), lambda t, h, n: (t, h, 0, 0)),
            ],
        ),
        out_shape=[
            jax.ShapeDtypeStruct((3, tables * LEN, D), BF16),
            jax.ShapeDtypeStruct((tables, pairs, 8, PAIR), F32),
        ],
        name="attn_bwd",
    )(lengths, qkv, qkv, qkv, mixed, logs, grad_mixed)


def place():
    tab, blk = lax.axis_index("tab"), lax.axis_index("blk")
    return tab // 2, tab % 2, blk // 2, blk % 2


def greet(peers):
    barrier = pltpu.get_barrier_semaphore()
    for z, x, y, c in peers:
        pl.semaphore_signal(
            barrier, inc=1, device_id=(z * 2 + x, y * 2 + c), device_id_type=MESH_ID
        )
    pl.semaphore_wait(barrier, len(peers))


def all_peers():
    z, x, y, c = place()
    z_peers = [((z + j) % 4, x, y, c) for j in range(1, 4)]
    rest = [(z, 1 - x, y, c), (z, x, 1 - y, c), (z, x, y, 1 - c), (z, x, 1 - y, 1 - c)]
    return z_peers + rest


def by_columns(width):
    return lambda ref, t, part: ref.at[t, :, pl.ds(pl.multiple_of(part * width, 128), width)]


def by_rows(height):
    return lambda ref, t, part: ref.at[t, pl.ds(pl.multiple_of(part * height, 16), height), :]


PIECES = (
    (by_columns(3 * D // 2), False),
    (by_columns(D // 2), False),
    (by_columns(FF // 4), True),
    (by_rows(FF // 16), False),
)
G_WIRES = 96
STEPS = 12


class Gather:
    def __init__(self, at, shard, whole, plan):
        piece, self.split = PIECES[at]
        z, x, y, c = place()
        tab = z * 2 + x
        part = y * 2 + c if self.split else c
        other = (1 - y) * 2 + c
        own = lambda: piece(shard, 0, part)
        self.plan = plan
        near = lambda j: (z + 4 - j) % 4 * 2 + x
        far = lambda j: (z + 4 - j) % 4 * 2 + 1 - x

        def send(at_tab, which, to, first=False):
            return plan.add(
                lambda: (
                    own() if first else piece(whole, at_tab, which),
                    piece(whole, at_tab, which),
                    to,
                )
            )

        side, over, across = (z, x, y, 1 - c), (z, x, 1 - y, c), (z, 1 - x, y, c)
        self.z = [send(tab, part, ((z + j) % 4, x, y, c), True) for j in range(1, 4)]
        self.x = [send(tab, part, across, True)]
        self.x += [send(near(j), part, across) for j in range(1, 4)]
        tabs = [near(j) for j in range(1, 4)] + [far(j) for j in range(4)]
        self.c = [send(t, part, side) for t in tabs]
        self.y = [send(t, part, over) for t in tabs] if self.split else []
        self.late = [send(t, other, side) for t in tabs] if self.split else []

    def send_z(self):
        for index in self.z:
            self.plan.start(index)

    def send_x(self):
        self.plan.start(self.x[0])

    def onward(self, at):
        if self.split:
            self.plan.start(self.y[at])
        self.plan.start(self.c[at])

    def task_z(self, j):
        self.plan.arrived(self.z[j - 1])
        self.plan.start(self.x[j])
        self.onward(j - 1)

    def task_x(self, j):
        self.plan.arrived(self.x[j])
        self.onward(3 + j)

    def task_y(self, at):
        self.plan.arrived(self.y[at])
        self.plan.start(self.late[at])

    def end(self):
        for index in self.c + self.late:
            self.plan.arrived(index)


def gather_kernel(
    len_ref, x_in, cot_in, qkv_in, out_in, up_in, down_in, vec_in,
    x_out, cot_out, qkv_out, out_out, up_out, down_out, vec_out, acts_out, mixed_out, logs_out,
    x_all, w_all, vec_all, acts, mixed, logs, send, recv, own,
):
    z, x, y, c = place()
    tab, blk = z * 2 + x, y * 2 + c
    share, span = x_in.shape[0] // 4, x_in.shape[1]
    mine = pl.ds(blk * share, share)
    slot = pl.ds(pl.multiple_of(blk * span, span), span)
    plan = Plan(send, recv)
    shards = (qkv_in, out_in, up_in, down_in)
    wholes = (w_all, out_out, up_out, down_out)
    works = [Gather(at, shards[at], wholes[at], plan) for at in range(4)]
    qkv, out, up, down = works

    def trade(src, dst):
        made = []
        for other in ((z, x, 1 - y, c), (z, x, 1 - y, 1 - c), (z, x, y, 1 - c)):
            their = other[2] * 2 + other[3]
            made.append(
                plan.add(
                    lambda their=their, other=other: (
                        src.at[pl.ds(their * share, share)], dst.at[:, slot, :], other,
                    )
                )
            )
        return made

    trade_x, trade_cot = trade(x_in, x_all), trade(cot_in, cot_out)
    vec_z = [
        plan.add(lambda j=j: (vec_in.at[0], vec_all.at[tab], ((z + j) % 4, x, y, c)))
        for j in range(1, 4)
    ]
    vec_x = [plan.add(lambda: (vec_in.at[0], vec_all.at[tab], (z, 1 - x, y, c)))]
    for j in range(1, 4):
        t = (z + 4 - j) % 4 * 2 + x
        vec_x.append(plan.add(lambda t=t: (vec_all.at[t], vec_all.at[t], (z, 1 - x, y, c))))
    keeps = [
        lambda: pltpu.make_async_copy(x_in.at[mine], x_all.at[:, slot, :], own.at[0]),
        lambda: pltpu.make_async_copy(qkv_in.at[0], w_all.at[tab], own.at[1]),
        lambda: pltpu.make_async_copy(vec_in.at[0], vec_all.at[tab], own.at[2]),
        lambda: pltpu.make_async_copy(cot_in.at[mine], cot_out.at[:, slot, :], own.at[3]),
        lambda: pltpu.make_async_copy(out_in.at[0], out_out.at[tab], own.at[4]),
        lambda: pltpu.make_async_copy(up_in.at[0], up_out.at[tab], own.at[5]),
        lambda: pltpu.make_async_copy(down_in.at[0], down_out.at[tab], own.at[6]),
    ]
    puts = [
        lambda: pltpu.make_async_copy(x_all, x_out, own.at[7]),
        lambda: pltpu.make_async_copy(w_all, qkv_out, own.at[8]),
        lambda: pltpu.make_async_copy(vec_all, vec_out, own.at[9]),
        lambda: pltpu.make_async_copy(acts, acts_out, own.at[10]),
        lambda: pltpu.make_async_copy(mixed, mixed_out, own.at[11]),
        lambda: pltpu.make_async_copy(logs, logs_out, own.at[12]),
    ]
    greet(all_peers())
    for index in vec_z + vec_x[:1]:
        plan.start(index)
    qkv.send_z()
    qkv.send_x()
    for index in trade_x:
        plan.start(index)
    for keep in keeps:
        keep().start()
    for work in (out, up, down):
        work.send_z()
    out.send_x()
    for index in trade_cot:
        plan.start(index)
    for j in range(1, 4):
        plan.arrived(vec_z[j - 1])
        plan.start(vec_x[j])
    for j in range(1, 4):
        qkv.task_z(j)
    up.send_x()
    down.send_x()
    for j in range(4):
        qkv.task_x(j)
    for index in vec_x:
        plan.arrived(index)
    for keep in keeps[:3]:
        keep().wait()
    for index in trade_x:
        plan.arrived(index)
    qkv.end()
    for put in puts[:3]:
        put().start()

    tile = 256
    rows = share * LEN
    spread = [vec_all[t, 0:16, :].astype(F32) for t in range(8)]
    vectors = spread[0]
    for t in range(1, 8):
        vectors = vectors + spread[t]
    for part in range(3):
        for col in range(0, D, tile):
            at = part * D + col
            weight = w_all[:, :, at : at + tile].reshape(D, tile)
            value = jnp.dot(x_all[...].reshape(rows, D), weight, preferred_element_type=F32)
            if part != 1:
                value = value + vectors[part // 2 : part // 2 + 1, col : col + tile]
            acts[:, at : at + tile] = value.astype(BF16)
    puts[3]().start()

    tasks = {
        0: [lambda j=j: out.task_z(j) for j in (1, 2, 3)],
        1: [lambda j=j: out.task_x(j) for j in range(4)],
        2: [lambda: up.task_z(1)],
        3: [lambda: up.task_z(2), lambda: up.task_z(3)],
        4: [lambda: up.task_x(0), lambda: up.task_x(1)],
        5: [lambda: up.task_x(2), lambda: up.task_x(3)],
        6: [lambda: up.task_y(0), lambda: up.task_y(1)],
        7: [lambda: up.task_y(2), lambda: down.task_z(1)],
        8: [lambda: up.task_y(3), lambda: down.task_x(0)],
        9: [lambda: up.task_y(4), lambda: down.task_z(2)],
        10: [lambda: up.task_y(5), lambda: down.task_x(1)],
        11: [lambda: up.task_y(6), lambda: down.task_z(3)],
        12: [lambda: down.task_x(2), lambda: down.task_x(3)],
    }

    def step(s, carry):
        for when, todo in tasks.items():
            if when < STEPS:

                @pl.when(s == when)
                def _(todo=todo):
                    for task in todo:
                        task()

        t, h = s // (STEPS // share), s % (STEPS // share)
        base = pl.multiple_of(t * LEN, LEN)
        cols = [pl.ds(pl.multiple_of(part * D + h * PAIR, PAIR), PAIR) for part in range(3)]
        attend(len_ref[t], acts, mixed, logs, t, h, base, cols)
        return carry

    lax.fori_loop(0, STEPS, step, 0)
    for put in puts[4:]:
        put().start()
    for task in tasks[STEPS]:
        task()
    for index in trade_cot:
        plan.arrived(index)
    for work in (out, up, down):
        work.end()
    plan.finish()
    for keep in keeps[3:]:
        keep().wait()
    for put in puts:
        put().wait()


def attend(live, acts, mixed_ref, logs_ref, t, h, base, cols):
    masks = head_masks(BF16)
    keys = acts[pl.ds(base, LEN), cols[1]]
    values = acts[pl.ds(base, LEN), cols[2]]
    rows = 256
    key_at = lax.broadcasted_iota(jnp.int32, (1, LEN), 1)
    bias = jnp.where(key_at < live, 0.0, NEGATIVE)
    lane = lax.broadcasted_iota(jnp.int32, (1, PAIR), 1)
    for start in range(0, LEN, rows):
        query = acts[pl.ds(base + start, rows), cols[0]] * jnp.asarray(HD ** (-0.5), BF16)
        mixed, logs = [], []
        for head in range(2):
            scores = back_mul(query * masks[head], keys) + bias
            top = jnp.max(scores, axis=-1, keepdims=True)
            raised = jnp.exp(scores - top)
            total = jnp.sum(raised, axis=-1, keepdims=True)
            probs = (raised * (1.0 / total)).astype(BF16)
            mixed.append(jnp.dot(probs, values, preferred_element_type=F32))
            logs.append(top + jnp.log(total))
        mixed_ref[pl.ds(base + start, rows), cols[0]] = jnp.where(
            lane < HD, mixed[0], mixed[1]
        ).astype(BF16)
        flat = jnp.where(lane < HD, logs[0], logs[1]).T
        logs_ref[t, h, 0:1, start : start + rows] = flat[0:1, :]
        logs_ref[t, h, 1:2, start : start + rows] = flat[HD : HD + 1, :]


def gather_all(lengths, tables, cotangent, qkv, out, up, down, vec):
    share, span = tables.shape[0] // 4, tables.shape[1] * 4
    vmem = pl.BlockSpec(memory_space=pltpu.VMEM)
    hbm = pl.BlockSpec(memory_space=pl.ANY)
    shape = lambda a: jax.ShapeDtypeStruct((8,) + a.shape[1:], BF16)
    rows = share * span
    logs = (share, STEPS // share, 8, LEN)
    return pl.pallas_call(
        gather_kernel,
        in_specs=[pl.BlockSpec(memory_space=pltpu.SMEM)] + [vmem] * 7,
        out_specs=[hbm] * 10,
        out_shape=[
            jax.ShapeDtypeStruct((share, span, D), BF16),
            jax.ShapeDtypeStruct((share, span, D), BF16),
            shape(qkv), shape(out), shape(up), shape(down), shape(vec),
            jax.ShapeDtypeStruct((rows, 3 * D), BF16),
            jax.ShapeDtypeStruct((rows, D), BF16),
            jax.ShapeDtypeStruct(logs, F32),
        ],
        scratch_shapes=[
            pltpu.VMEM((share, span, D), BF16),
            pltpu.VMEM((8,) + qkv.shape[1:], BF16),
            pltpu.VMEM((8,) + vec.shape[1:], BF16),
            pltpu.VMEM((rows, 3 * D), BF16),
            pltpu.VMEM((rows, D), BF16),
            pltpu.VMEM(logs, F32),
            pltpu.SemaphoreType.DMA((G_WIRES,)),
            pltpu.SemaphoreType.DMA((G_WIRES,)),
            pltpu.SemaphoreType.DMA((13,)),
        ],
        compiler_params=pltpu.CompilerParams(
            collective_id=0, has_side_effects=True, vmem_limit_bytes=VMEM_ALL
        ),
        name="gather_attend",
    )(lengths, tables, cotangent, qkv, out, up, down, vec)


class Plan:
    def __init__(self, send, recv):
        self.send, self.recv, self.makers = send, recv, []

    def add(self, maker):
        self.makers.append(maker)
        return len(self.makers) - 1

    def build(self, index):
        src, dst, (z, x, y, c) = self.makers[index]()
        return pltpu.make_async_remote_copy(
            src_ref=src,
            dst_ref=dst,
            send_sem=self.send.at[index],
            recv_sem=self.recv.at[index],
            device_id=(z * 2 + x, y * 2 + c),
            device_id_type=MESH_ID,
        )

    def start(self, index):
        self.build(index).start()

    def arrived(self, index):
        self.build(index).wait_recv()

    def finish(self):
        for index in range(len(self.makers)):
            self.build(index).wait_send()


class Slab:
    def __init__(self, rows, cols, split, axis, first=0, dtype=BF16):
        self.rows, self.cols, self.split, self.axis = rows, cols, split, axis
        self.first, self.dtype = first, dtype
        self.tile = 128 if axis == 1 else (16 if dtype == BF16 else 8)

    def cut(self, index):
        if self.axis == 1:
            return pl.ds(0, self.rows), pl.ds(
                pl.multiple_of(index * self.cols, self.tile), self.cols
            )
        start = pl.multiple_of(self.first + index * self.rows, self.tile)
        return pl.ds(start, self.rows), pl.ds(0, self.cols)

    def scratch(self):
        ways = 2 if self.split else 1
        vmem = lambda *lead: pltpu.VMEM(lead + (self.rows, self.cols), self.dtype)
        late = vmem(4, 2) if self.split else vmem(1, 1)
        return [vmem(ways, 4, 2), vmem(ways, 4, 2), late, vmem(4), vmem(3), vmem()]

    def copies(self):
        return (2 if self.split else 1) + 1 + 1 + 3 + 3


class Reduction:
    def __init__(self, slab, source, target, scratch, plan, own, own_at):
        self.slab, self.source, self.target, self.plan = slab, source, target, plan
        self.held, self.from_c, self.from_y, self.from_x, self.from_z, self.done = scratch
        self.own, self.own_at = own, own_at
        z, x, y, c = place()
        self.at = z, x, y, c
        self.slot = y if slab.split else 0
        side = (z, x, y, 1 - c)
        over = (z, x, 1 - y, c)

        def index_of(half, core):
            return half * 2 + core if slab.split else core

        def cut_all(ref, index):
            rows, cols = slab.cut(index)
            return ref.at[:, :, rows, cols]

        def cut_out(index):
            rows, cols = slab.cut(index)
            return target.at[rows, cols]

        ways = 2 if slab.split else 1
        self.loads = [
            lambda half=half: pltpu.make_async_copy(
                cut_all(source, index_of(half, c)), self.held.at[half], own.at[own_at + half]
            )
            for half in range(ways)
        ]
        self.to_core = [
            plan.add(
                lambda half=half: (
                    cut_all(source, index_of(half, 1 - c)), self.from_c.at[half], side,
                )
            )
            for half in range(ways)
        ]
        if slab.split:
            self.to_y = plan.add(lambda: (self.held.at[1 - y], self.from_y, over))
        else:
            self.to_y = plan.add(lambda: (self.done, self.from_y.at[0, 0], over))
        self.to_x = plan.add(
            lambda: (self.held.at[self.slot, :, 1 - x], self.from_x, (z, 1 - x, y, c))
        )
        self.to_z = [
            plan.add(
                lambda j=j: (
                    self.held.at[self.slot, (z + j) % 4, x],
                    self.from_z.at[j - 1],
                    ((z + j) % 4, x, y, c),
                )
            )
            for j in range(1, 4)
        ]
        mine = lambda: cut_out(index_of(y, c))
        self.store = lambda: pltpu.make_async_copy(self.done, mine(), own.at[own_at + 2])
        self.share_core = plan.add(lambda: (self.done, mine(), side))
        if slab.split:
            theirs = lambda: cut_out(index_of(1 - y, c))
            self.share_y = plan.add(lambda: (self.done, mine(), over))
            self.share_far = plan.add(lambda: (theirs(), theirs(), side))

    def begin(self):
        for load in self.loads:
            load().start()
        for index in self.to_core:
            self.plan.start(index)

    def summed(self, total, *others):
        value = total[...].astype(F32)
        for other in others:
            value = value + other[...].astype(F32)
        total[...] = value.astype(self.slab.dtype)

    def after_core(self):
        for half, load in enumerate(self.loads):
            load().wait()
            self.plan.arrived(self.to_core[half])

        def step(t, carry):
            for half in range(len(self.loads)):
                self.summed(self.held.at[half, t // 2, t % 2], self.from_c.at[half, t // 2, t % 2])
            return carry

        lax.fori_loop(0, 8, step, 0)
        self.plan.start(self.to_y if self.slab.split else self.to_x)

    def after_y(self):
        if not self.slab.split:
            return
        self.plan.arrived(self.to_y)

        def step(t, carry):
            self.summed(self.held.at[self.slot, t // 2, t % 2], self.from_y.at[t // 2, t % 2])
            return carry

        lax.fori_loop(0, 8, step, 0)
        self.plan.start(self.to_x)

    def after_x(self):
        z, x, y, c = self.at
        self.plan.arrived(self.to_x)

        def step(t, carry):
            self.summed(self.held.at[self.slot, t, x], self.from_x.at[t])
            return carry

        lax.fori_loop(0, 4, step, 0)
        for index in self.to_z:
            self.plan.start(index)

    def after_z(self):
        z, x, y, c = self.at
        for index in self.to_z:
            self.plan.arrived(index)
        value = self.held[self.slot, z, x].astype(F32)
        for j in range(3):
            value = value + self.from_z[j].astype(F32)
        self.done[...] = value.astype(self.slab.dtype)
        if self.slab.split:
            self.plan.start(self.share_y)
            self.plan.start(self.share_core)
            self.store().start()
        else:
            self.plan.start(self.to_y)

    def after_final(self):
        if self.slab.split:
            self.plan.arrived(self.share_y)
            self.plan.start(self.share_far)
        else:
            self.plan.arrived(self.to_y)
            self.plan.build(self.to_y).wait_send()
            self.summed(self.done, self.from_y.at[0, 0])
            self.plan.start(self.share_core)
            self.store().start()

    def end(self):
        self.plan.arrived(self.share_core)
        if self.slab.split:
            self.plan.arrived(self.share_far)
        self.store().wait()

    def finish_sends(self):
        done_early = () if self.slab.split else (self.to_y,)
        sends = self.to_core + [self.to_y, self.to_x] + self.to_z + [self.share_core]
        if self.slab.split:
            sends += [self.share_y, self.share_far]
        for index in sends:
            if index not in done_early:
                self.plan.build(index).wait_send()


STAGES = ("begin", "after_core", "after_y", "after_x", "after_z", "after_final", "end")

SLABS = (
    (0, Slab(96, FF // 4, True, 1)),
    (1, Slab(32, D, True, 0)),
    (1, Slab(128, D, False, 0, first=128)),
    (2, Slab(96, 3 * D // 2, False, 1)),
    (3, Slab(96, D // 2, False, 1)),
    (4, Slab(8, 128, False, 0, dtype=F32)),
)


def reduce_kernel(*refs):
    (gin_in, y_in), sources = refs[:2], refs[2:7]
    (gin_out, y_out), targets = refs[7:9], refs[9:14]
    scratch, (send, recv, own) = refs[14:-3], refs[-3:]
    z, x, y, c = place()
    blk = y * 2 + c
    greet(all_peers())
    plan = Plan(send, recv)
    share, span = gin_out.shape[0] // 4, gin_out.shape[1]
    kept, traded = [], []
    works = []
    for at, (number, slab) in enumerate(SLABS):
        part = scratch[6 * at : 6 * at + 6]
        works.append(
            Reduction(slab, sources[number], targets[number], part, plan, own, 2 + 3 * at)
        )
    for at, (src, dst) in enumerate(((gin_in, gin_out), (y_in, y_out))):
        mine = dst.at[pl.ds(blk * share, share)]
        kept.append(
            pltpu.make_async_copy(src.at[:, pl.ds(blk * span, span), :], mine, own.at[at])
        )
        kept[-1].start()
        for other in ((z, x, 1 - y, c), (z, x, 1 - y, 1 - c), (z, x, y, 1 - c)):
            their = other[2] * 2 + other[3]
            maker = lambda src=src, mine=mine, their=their, other=other: (
                src.at[:, pl.ds(their * span, span), :], mine, other,
            )
            traded.append(plan.add(maker))
    for stage in STAGES:
        for work in works:
            getattr(work, stage)()
        if stage == "after_y":
            for index in traded:
                plan.start(index)
    for index in traded:
        plan.arrived(index)
    for work in works:
        work.finish_sends()
    for index in traded:
        plan.build(index).wait_send()
    for made in kept:
        made.wait()


def reduce_all(grad_in, result, up, down, qkv, out, vec):
    share, length = grad_in.shape[:2]
    vmem = pl.BlockSpec(memory_space=pltpu.VMEM)
    hbm = pl.BlockSpec(memory_space=pl.ANY)
    shape = lambda a: jax.ShapeDtypeStruct(a.shape[2:], a.dtype)
    back = jax.ShapeDtypeStruct((share * 4, length // 4, D), BF16)
    grads = (up, down, qkv, out, vec)
    scratch = [s for _, slab in SLABS for s in slab.scratch()]
    wires = 6 + sum(slab.copies() for _, slab in SLABS)
    return pl.pallas_call(
        reduce_kernel,
        in_specs=[vmem] * 2 + [hbm] * 5,
        out_specs=[hbm] * 7,
        out_shape=[back, back] + [shape(a) for a in grads],
        scratch_shapes=scratch
        + [
            pltpu.SemaphoreType.DMA((wires,)),
            pltpu.SemaphoreType.DMA((wires,)),
            pltpu.SemaphoreType.DMA((2 + 3 * len(SLABS),)),
        ],
        compiler_params=pltpu.CompilerParams(
            collective_id=1, has_side_effects=True, vmem_limit_bytes=VMEM_ALL
        ),
        name="reduce_all",
    )(grad_in, result, *grads)


def local(*args):
    tables, lengths, cotangent, step_count = args[:4]
    masters, firsts, seconds = args[4:9], args[9:14], args[14:19]
    w_qkv, w_out, w_up, w_down, vectors = masters
    blocks = lax.axis_size("blk")
    shards = lax.axis_size("tab")
    table_count, local_len = tables.shape[:2]
    share = table_count // blocks
    tuned = shards == 8 and blocks == 4
    owned = vectors.shape[0]
    vec_own = jnp.pad(vectors.astype(BF16).T, ((0, 4), (0, 0)))
    narrow = [w.astype(BF16) for w in (w_qkv, w_out, w_up, w_down)]
    my_lengths = lax.dynamic_slice(lengths, (lax.axis_index("blk") * share,), (share,))
    if tuned:
        at_own = (0, lax.axis_index("tab") * owned)
        vec_wide = lax.dynamic_update_slice(jnp.zeros((16, D), BF16), vec_own, at_own)
        mine, cot, *wholes, qkv, mixed, logs = gather_all(
            my_lengths, tables, cotangent, *[w[None] for w in narrow], vec_wide[None]
        )
        vec_f = jnp.sum(wholes[4].astype(F32), axis=0)[:12]
    else:
        spread = partial(lax.all_to_all, axis_name="blk", split_axis=0, concat_axis=1, tiled=True)
        mine, cot = spread(tables), spread(cotangent)
        wholes = [lax.all_gather(w, "tab", axis=0) for w in narrow + [vec_own]]
        vec_f = wholes[4][:, :12].transpose(1, 0, 2).reshape(12, D).astype(F32)
    full_qkv, full_out, full_up, full_down = [
        w.reshape(-1, w.shape[-1]) for w in wholes[:4]
    ]
    bias_up = vec_f[8:12].reshape(-1)
    rows = mine.reshape(-1, D)
    if not tuned:
        bias_qkv = jnp.concatenate([vec_f[0], jnp.zeros((D,), F32), vec_f[1]])
        qkv = (jnp.dot(rows, full_qkv, preferred_element_type=F32) + bias_qkv).astype(BF16)
        mixed, logs = attention_forward(my_lengths, qkv, share)
    attn_out = jnp.dot(mixed, full_out, preferred_element_type=F32) + vec_f[2]
    normed_one, norm_one_back = jax.vjp(
        layer_norm, rows.astype(F32) + attn_out, vec_f[4], vec_f[5]
    )
    normed_b = normed_one.astype(BF16)
    hidden = jnp.dot(normed_b, full_up, preferred_element_type=F32) + bias_up
    below = 0.5 * (1.0 + lax.erf(hidden * 0.5**0.5))
    active_b = (hidden * below).astype(BF16)
    slope = below + hidden * jnp.exp(-0.5 * hidden * hidden) * (2.0 * math.pi) ** -0.5
    active_b, slope = lax.optimization_barrier((active_b, slope.astype(BF16)))
    branch = jnp.dot(active_b, full_down, preferred_element_type=F32) + vec_f[3]
    result, norm_two_back = jax.vjp(layer_norm, normed_one + branch, vec_f[6], vec_f[7])
    result = result.astype(BF16).reshape(mine.shape)
    grad_two, grad_g2, grad_c2 = norm_two_back(cot.reshape(-1, D).astype(F32))
    grad_b2 = jnp.sum(grad_two, axis=0)
    branch_b = grad_two.astype(BF16)
    gw_down = inner(active_b, branch_b).astype(BF16)
    grad_hidden = back_mul(branch_b, full_down) * slope.astype(F32)
    grad_b1 = jnp.sum(grad_hidden, axis=0)
    hidden_b = grad_hidden.astype(BF16)
    gw_up = inner(normed_b, hidden_b).astype(BF16)
    grad_one, grad_g1, grad_c1 = norm_one_back(grad_two + back_mul(hidden_b, full_up))
    grad_bo = jnp.sum(grad_one, axis=0)
    attn_b = grad_one.astype(BF16)
    gw_out = inner(mixed, attn_b).astype(BF16)
    grad_mixed = back_mul(attn_b, full_out).astype(BF16)
    grad_three, sums = attention_backward(my_lengths, qkv, mixed, logs, grad_mixed, share)
    sums = jnp.sum(sums[:, :, :2], axis=0)
    grad_bq, grad_bv = sums[:, 0].reshape(-1), sums[:, 1].reshape(-1)
    grad_qkv = jnp.concatenate([grad_three[i] for i in range(3)], axis=1)
    gw_qkv = inner(rows, grad_qkv).astype(BF16)
    grad_in = grad_one + back_mul(grad_qkv, full_qkv)
    grad_in = grad_in.astype(BF16).reshape(mine.shape)
    gw_vec = jnp.concatenate(
        [
            jnp.stack([grad_bq, grad_bv, grad_bo, grad_b2, grad_g1, grad_c1, grad_g2, grad_c2]),
            grad_b1.reshape(4, D),
        ]
    )
    if tuned:
        pads = ((0, 0), (0, 0), (0, 2), (0, 128 - owned))
        wide_vec = jnp.pad(gw_vec.reshape(2, 6, shards, owned).transpose(2, 0, 1, 3), pads)
        by_owner = lambda g: g.reshape(4, 2, -1, g.shape[-1])
        grad_input, output, *sums = reduce_all(
            grad_in, result, by_owner(gw_up), by_owner(gw_down), by_owner(gw_qkv),
            by_owner(gw_out), wide_vec.reshape(4, 2, 16, 128),
        )
        sum_vec = sums[4].reshape(2, 8, 128)[:, :6, :owned].reshape(12, owned).T
        shares = [s.astype(F32) for s in (sums[2], sums[3], sums[0], sums[1], sum_vec)]
    else:
        back = partial(lax.all_to_all, axis_name="blk", split_axis=1, concat_axis=0, tiled=True)
        grad_input, output = back(grad_in), back(result)

        def collect(grad):
            part = lax.psum_scatter(
                grad.reshape(shards, -1, grad.shape[-1]), "tab", scatter_dimension=0
            )
            return lax.psum(part.astype(BF16), "blk").astype(F32)

        shares = [collect(g) for g in (gw_qkv, gw_out, gw_up, gw_down)]
        shares.append(collect(gw_vec.T.astype(BF16)))
    grad_input = grad_input.astype(F32)
    step_float = step_count[0].astype(F32)
    results = [output, grad_input]
    for at in range(5):
        results.extend(
            adam(masters[at], shares[at], firsts[at], seconds[at], RATES[at], step_float)
        )
    return tuple(results)


def solution(mesh):
    tokens, flat, rows = P("tab", "blk", None), P("tab"), P("tab", None)
    return jax.shard_map(
        local,
        mesh=mesh,
        in_specs=(tokens, flat, tokens, P()) + (rows,) * 15,
        out_specs=(tokens, tokens) + (rows,) * 20,
        check_vma=False,
    )
```

```python
import math
from functools import partial

import jax
import jax.numpy as jnp
from jax import lax
from jax.experimental import pallas as pl
from jax.experimental.pallas import tpu as pltpu
from jax.sharding import PartitionSpec as P

D = 768
H = 12
HD = 64
LEN = 512
FF = 3072
PAIR = 2 * HD

EPS = 1e-06
NEGATIVE = -1e30
BETA_ONE = 0.9
BETA_TWO = 0.999
ADAM_EPS = 1e-08
DECAY = 0.01
RATES = (1.0, 15.0, 1.0, 0.5, 5.0)

F32 = jnp.float32
BF16 = jnp.bfloat16
MESH_ID = pl.DeviceIdType.MESH
VMEM_ALL = 64 * 1000 * 1024


def layer_norm(hidden, gain_vec, shift_vec):
    row_mean = jnp.mean(hidden, axis=-1, keepdims=True)
    centred = hidden - row_mean
    variance = jnp.mean(centred * centred, axis=-1, keepdims=True)
    return centred * lax.rsqrt(variance + EPS) * gain_vec + shift_vec


def inner(left, right):
    return lax.dot_general(left, right, (((0,), (0,)), ((), ())), preferred_element_type=F32)


def back_mul(left, right):
    return lax.dot_general(left, right, (((1,), (1,)), ((), ())), preferred_element_type=F32)


def adam(master, gradient, first_moment, second_moment, rate_now, step_float):
    moment_new = BETA_ONE * first_moment + (1.0 - BETA_ONE) * gradient
    square_new = BETA_TWO * second_moment + (1.0 - BETA_TWO) * gradient * gradient
    fix_one = 1.0 - jnp.power(BETA_ONE, step_float)
    fix_two = 1.0 - jnp.power(BETA_TWO, step_float)
    update = moment_new / fix_one / (jnp.sqrt(square_new / fix_two) + ADAM_EPS)
    master_new = master - rate_now * (update + DECAY * master)
    return (moment_new, square_new, master_new, master_new.astype(BF16))


def head_masks(dtype):
    lane = lax.broadcasted_iota(jnp.int32, (1, PAIR), 1)
    return [(lane < HD).astype(dtype), (lane >= HD).astype(dtype)]


def attn_fwd_kernel(len_ref, q_ref, k_ref, v_ref, o_ref, l_ref):
    live = len_ref[pl.program_id(0)]
    masks = head_masks(BF16)
    keys = k_ref[...]
    values = v_ref[...]
    rows = 256
    key_at = lax.broadcasted_iota(jnp.int32, (1, LEN), 1)
    bias = jnp.where(key_at < live, 0.0, NEGATIVE)
    lane = lax.broadcasted_iota(jnp.int32, (1, PAIR), 1)
    for start in range(0, LEN, rows):
        query = q_ref[pl.ds(start, rows), :] * jnp.asarray(HD ** (-0.5), BF16)
        mixed, logs = [], []
        for head in range(2):
            scores = back_mul(query * masks[head], keys) + bias
            top = jnp.max(scores, axis=-1, keepdims=True)
            raised = jnp.exp(scores - top)
            total = jnp.sum(raised, axis=-1, keepdims=True)
            probs = (raised * (1.0 / total)).astype(BF16)
            mixed.append(jnp.dot(probs, values, preferred_element_type=F32))
            logs.append(top + jnp.log(total))
        o_ref[pl.ds(start, rows), :] = jnp.where(lane < HD, mixed[0], mixed[1]).astype(BF16)
        both = jnp.where(lane < HD, logs[0], logs[1])
        flat = both.T
        l_ref[0, 0, 0:1, pl.ds(start, rows)] = flat[0:1, :]
        l_ref[0, 0, 1:2, pl.ds(start, rows)] = flat[HD : HD + 1, :]


def attention_forward(lengths, qkv, tables):
    pairs = H // 2
    spec = lambda part: pl.BlockSpec((LEN, PAIR), lambda t, h, n: (t, part * pairs + h))
    return pl.pallas_call(
        attn_fwd_kernel,
        grid_spec=pltpu.PrefetchScalarGridSpec(
            num_scalar_prefetch=1,
            grid=(tables, pairs),
            in_specs=[spec(0), spec(1), spec(2)],
            out_specs=[
                pl.BlockSpec((LEN, PAIR), lambda t, h, n: (t, h)),
                pl.BlockSpec((1, 1, 8, LEN), lambda t, h, n: (t, h, 0, 0)),
            ],
        ),
        out_shape=[
            jax.ShapeDtypeStruct((tables * LEN, D), BF16),
            jax.ShapeDtypeStruct((tables, pairs, 8, LEN), F32),
        ],
        name="attn_fwd",
    )(lengths, qkv, qkv, qkv)


def attn_bwd_kernel(len_ref, q_ref, k_ref, v_ref, o_ref, l_ref, do_ref, d_ref, sums_ref):
    live = len_ref[pl.program_id(0)]
    masks = head_masks(BF16)
    keys = k_ref[...]
    values = v_ref[...]
    query = q_ref[...] * jnp.asarray(HD ** (-0.5), BF16)
    grad_out = do_ref[...]
    dots = (grad_out.astype(F32) * o_ref[...].astype(F32)).T
    rows = 256
    q_masked = [query * m for m in masks]
    g_masked = [grad_out * m for m in masks]
    deltas = [jnp.sum(dots[h * HD : (h + 1) * HD, :], axis=0, keepdims=True) for h in range(2)]
    logs = [l_ref[0, 0, h : h + 1, :] for h in range(2)]
    grad_q = jnp.zeros((LEN, PAIR), F32)
    sum_v = jnp.zeros((1, PAIR), F32)
    for start in range(0, LEN, rows):
        part_k = keys[start : start + rows, :]
        part_v = values[start : start + rows, :]
        key_at = start + lax.broadcasted_iota(jnp.int32, (rows, 1), 0)
        bias = jnp.where(key_at < live, 0.0, NEGATIVE)
        grad_k = jnp.zeros((rows, PAIR), F32)
        grad_v = jnp.zeros((rows, PAIR), F32)
        for head in range(2):
            scores = back_mul(part_k, q_masked[head])
            probs = jnp.exp(scores + bias - logs[head])
            grad_probs = back_mul(part_v, g_masked[head])
            grad_s = (probs * (grad_probs - deltas[head])).astype(BF16)
            grad_v += jnp.dot(probs.astype(BF16), g_masked[head], preferred_element_type=F32)
            grad_k += jnp.dot(grad_s, q_masked[head], preferred_element_type=F32)
            grad_q += inner(grad_s, part_k * masks[head])
        d_ref[1, pl.ds(start, rows), :] = grad_k.astype(BF16)
        d_ref[2, pl.ds(start, rows), :] = grad_v.astype(BF16)
        sum_v += jnp.sum(grad_v, axis=0, keepdims=True)
    grad_q = grad_q * HD ** (-0.5)
    d_ref[0, :, :] = grad_q.astype(BF16)
    sums_ref[0, 0, 0:1, :] = jnp.sum(grad_q, axis=0, keepdims=True)
    sums_ref[0, 0, 1:2, :] = sum_v


def attention_backward(lengths, qkv, mixed, logs, grad_mixed, tables):
    pairs = H // 2
    spec = lambda part: pl.BlockSpec((LEN, PAIR), lambda t, h, n: (t, part * pairs + h))
    block = pl.BlockSpec((LEN, PAIR), lambda t, h, n: (t, h))
    return pl.pallas_call(
        attn_bwd_kernel,
        grid_spec=pltpu.PrefetchScalarGridSpec(
            num_scalar_prefetch=1,
            grid=(tables, pairs),
            in_specs=[
                spec(0),
                spec(1),
                spec(2),
                block,
                pl.BlockSpec((1, 1, 8, LEN), lambda t, h, n: (t, h, 0, 0)),
                block,
            ],
            out_specs=[
                pl.BlockSpec((3, LEN, PAIR), lambda t, h, n: (0, t, h)),
                pl.BlockSpec((1, 1, 8, PAIR), lambda t, h, n: (t, h, 0, 0)),
            ],
        ),
        out_shape=[
            jax.ShapeDtypeStruct((3, tables * LEN, D), BF16),
            jax.ShapeDtypeStruct((tables, pairs, 8, PAIR), F32),
        ],
        name="attn_bwd",
    )(lengths, qkv, qkv, qkv, mixed, logs, grad_mixed)


def place():
    tab, blk = lax.axis_index("tab"), lax.axis_index("blk")
    return tab // 2, tab % 2, blk // 2, blk % 2


def greet(peers):
    barrier = pltpu.get_barrier_semaphore()
    for z, x, y, c in peers:
        pl.semaphore_signal(
            barrier, inc=1, device_id=(z * 2 + x, y * 2 + c), device_id_type=MESH_ID
        )
    pl.semaphore_wait(barrier, len(peers))


def all_peers():
    z, x, y, c = place()
    z_peers = [((z + j) % 4, x, y, c) for j in range(1, 4)]
    rest = [(z, 1 - x, y, c), (z, x, 1 - y, c), (z, x, y, 1 - c), (z, x, 1 - y, 1 - c)]
    return z_peers + rest


def by_columns(width):
    return lambda ref, t, part: ref.at[t, :, pl.ds(pl.multiple_of(part * width, 128), width)]


def by_rows(height):
    return lambda ref, t, part: ref.at[t, pl.ds(pl.multiple_of(part * height, 16), height), :]


PIECES = (
    (by_columns(3 * D // 2), False),
    (by_columns(D // 2), False),
    (by_columns(FF // 4), True),
    (by_rows(FF // 16), False),
)
G_WIRES = 96
STEPS = 12


class Gather:
    def __init__(self, at, shard, whole, plan):
        piece, self.split = PIECES[at]
        z, x, y, c = place()
        tab = z * 2 + x
        part = y * 2 + c if self.split else c
        other = (1 - y) * 2 + c
        own = lambda: piece(shard, 0, part)
        self.plan = plan
        near = lambda j: (z + 4 - j) % 4 * 2 + x
        far = lambda j: (z + 4 - j) % 4 * 2 + 1 - x

        def send(at_tab, which, to, first=False):
            return plan.add(
                lambda: (
                    own() if first else piece(whole, at_tab, which),
                    piece(whole, at_tab, which),
                    to,
                )
            )

        side, over, across = (z, x, y, 1 - c), (z, x, 1 - y, c), (z, 1 - x, y, c)
        self.z = [send(tab, part, ((z + j) % 4, x, y, c), True) for j in range(1, 4)]
        self.x = [send(tab, part, across, True)]
        self.x += [send(near(j), part, across) for j in range(1, 4)]
        tabs = [near(j) for j in range(1, 4)] + [far(j) for j in range(4)]
        self.c = [send(t, part, side) for t in tabs]
        self.y = [send(t, part, over) for t in tabs] if self.split else []
        self.late = [send(t, other, side) for t in tabs] if self.split else []

    def send_z(self):
        for index in self.z:
            self.plan.start(index)

    def send_x(self):
        self.plan.start(self.x[0])

    def onward(self, at):
        if self.split:
            self.plan.start(self.y[at])
        self.plan.start(self.c[at])

    def task_z(self, j):
        self.plan.arrived(self.z[j - 1])
        self.plan.start(self.x[j])
        self.onward(j - 1)

    def task_x(self, j):
        self.plan.arrived(self.x[j])
        self.onward(3 + j)

    def task_y(self, at):
        self.plan.arrived(self.y[at])
        self.plan.start(self.late[at])

    def end(self):
        for index in self.c + self.late:
            self.plan.arrived(index)


def gather_kernel(
    len_ref, x_in, cot_in, qkv_in, out_in, up_in, down_in, vec_in,
    x_out, cot_out, qkv_out, out_out, up_out, down_out, vec_out, acts_out, mixed_out, logs_out,
    x_all, w_all, vec_all, acts, mixed, logs, send, recv, own,
):
    z, x, y, c = place()
    tab, blk = z * 2 + x, y * 2 + c
    share, span = x_in.shape[0] // 4, x_in.shape[1]
    mine = pl.ds(blk * share, share)
    slot = pl.ds(pl.multiple_of(blk * span, span), span)
    plan = Plan(send, recv)
    shards = (qkv_in, out_in, up_in, down_in)
    wholes = (w_all, out_out, up_out, down_out)
    works = [Gather(at, shards[at], wholes[at], plan) for at in range(4)]
    qkv, out, up, down = works

    def trade(src, dst):
        made = []
        for other in ((z, x, 1 - y, c), (z, x, 1 - y, 1 - c), (z, x, y, 1 - c)):
            their = other[2] * 2 + other[3]
            made.append(
                plan.add(
                    lambda their=their, other=other: (
                        src.at[pl.ds(their * share, share)], dst.at[:, slot, :], other,
                    )
                )
            )
        return made

    trade_x, trade_cot = trade(x_in, x_all), trade(cot_in, cot_out)
    vec_z = [
        plan.add(lambda j=j: (vec_in.at[0], vec_all.at[tab], ((z + j) % 4, x, y, c)))
        for j in range(1, 4)
    ]
    vec_x = [plan.add(lambda: (vec_in.at[0], vec_all.at[tab], (z, 1 - x, y, c)))]
    for j in range(1, 4):
        t = (z + 4 - j) % 4 * 2 + x
        vec_x.append(plan.add(lambda t=t: (vec_all.at[t], vec_all.at[t], (z, 1 - x, y, c))))
    keeps = [
        lambda: pltpu.make_async_copy(x_in.at[mine], x_all.at[:, slot, :], own.at[0]),
        lambda: pltpu.make_async_copy(qkv_in.at[0], w_all.at[tab], own.at[1]),
        lambda: pltpu.make_async_copy(vec_in.at[0], vec_all.at[tab], own.at[2]),
        lambda: pltpu.make_async_copy(cot_in.at[mine], cot_out.at[:, slot, :], own.at[3]),
        lambda: pltpu.make_async_copy(out_in.at[0], out_out.at[tab], own.at[4]),
        lambda: pltpu.make_async_copy(up_in.at[0], up_out.at[tab], own.at[5]),
        lambda: pltpu.make_async_copy(down_in.at[0], down_out.at[tab], own.at[6]),
    ]
    puts = [
        lambda: pltpu.make_async_copy(x_all, x_out, own.at[7]),
        lambda: pltpu.make_async_copy(w_all, qkv_out, own.at[8]),
        lambda: pltpu.make_async_copy(vec_all, vec_out, own.at[9]),
        lambda: pltpu.make_async_copy(acts, acts_out, own.at[10]),
        lambda: pltpu.make_async_copy(mixed, mixed_out, own.at[11]),
        lambda: pltpu.make_async_copy(logs, logs_out, own.at[12]),
    ]
    greet(all_peers())
    for index in vec_z + vec_x[:1]:
        plan.start(index)
    qkv.send_z()
    qkv.send_x()
    for index in trade_x:
        plan.start(index)
    for keep in keeps:
        keep().start()
    for work in (out, up, down):
        work.send_z()
    out.send_x()
    for index in trade_cot:
        plan.start(index)
    for j in range(1, 4):
        plan.arrived(vec_z[j - 1])
        plan.start(vec_x[j])
    for j in range(1, 4):
        qkv.task_z(j)
    up.send_x()
    down.send_x()
    for j in range(4):
        qkv.task_x(j)
    for index in vec_x:
        plan.arrived(index)
    for keep in keeps[:3]:
        keep().wait()
    for index in trade_x:
        plan.arrived(index)
    qkv.end()
    for put in puts[:3]:
        put().start()

    tile = 256
    rows = share * LEN
    spread = [vec_all[t, 0:16, :].astype(F32) for t in range(8)]
    vectors = spread[0]
    for t in range(1, 8):
        vectors = vectors + spread[t]
    for part in range(3):
        for col in range(0, D, tile):
            at = part * D + col
            weight = w_all[:, :, at : at + tile].reshape(D, tile)
            value = jnp.dot(x_all[...].reshape(rows, D), weight, preferred_element_type=F32)
            if part != 1:
                value = value + vectors[part // 2 : part // 2 + 1, col : col + tile]
            acts[:, at : at + tile] = value.astype(BF16)
    puts[3]().start()

    tasks = {
        0: [lambda j=j: out.task_z(j) for j in (1, 2, 3)],
        1: [lambda j=j: out.task_x(j) for j in range(4)],
        2: [lambda: up.task_z(1)],
        3: [lambda: up.task_z(2), lambda: up.task_z(3)],
        4: [lambda: up.task_x(0), lambda: up.task_x(1)],
        5: [lambda: up.task_x(2), lambda: up.task_x(3)],
        6: [lambda: up.task_y(0), lambda: up.task_y(1)],
        7: [lambda: up.task_y(2), lambda: down.task_z(1)],
        8: [lambda: up.task_y(3), lambda: down.task_x(0)],
        9: [lambda: up.task_y(4), lambda: down.task_z(2)],
        10: [lambda: up.task_y(5), lambda: down.task_x(1)],
        11: [lambda: up.task_y(6), lambda: down.task_z(3)],
        12: [lambda: down.task_x(2), lambda: down.task_x(3)],
    }

    def step(s, carry):
        for when, todo in tasks.items():
            if when < STEPS:

                @pl.when(s == when)
                def _(todo=todo):
                    for task in todo:
                        task()

        t, h = s // (STEPS // share), s % (STEPS // share)
        base = pl.multiple_of(t * LEN, LEN)
        cols = [pl.ds(pl.multiple_of(part * D + h * PAIR, PAIR), PAIR) for part in range(3)]
        attend(len_ref[t], acts, mixed, logs, t, h, base, cols)
        return carry

    lax.fori_loop(0, STEPS, step, 0)
    for put in puts[4:]:
        put().start()
    for task in tasks[STEPS]:
        task()
    for index in trade_cot:
        plan.arrived(index)
    for work in (out, up, down):
        work.end()
    plan.finish()
    for keep in keeps[3:]:
        keep().wait()
    for put in puts:
        put().wait()


def attend(live, acts, mixed_ref, logs_ref, t, h, base, cols):
    masks = head_masks(BF16)
    keys = acts[pl.ds(base, LEN), cols[1]]
    values = acts[pl.ds(base, LEN), cols[2]]
    rows = 256
    key_at = lax.broadcasted_iota(jnp.int32, (1, LEN), 1)
    bias = jnp.where(key_at < live, 0.0, NEGATIVE)
    lane = lax.broadcasted_iota(jnp.int32, (1, PAIR), 1)
    for start in range(0, LEN, rows):
        query = acts[pl.ds(base + start, rows), cols[0]] * jnp.asarray(HD ** (-0.5), BF16)
        mixed, logs = [], []
        for head in range(2):
            scores = back_mul(query * masks[head], keys) + bias
            top = jnp.max(scores, axis=-1, keepdims=True)
            raised = jnp.exp(scores - top)
            total = jnp.sum(raised, axis=-1, keepdims=True)
            probs = (raised * (1.0 / total)).astype(BF16)
            mixed.append(jnp.dot(probs, values, preferred_element_type=F32))
            logs.append(top + jnp.log(total))
        mixed_ref[pl.ds(base + start, rows), cols[0]] = jnp.where(
            lane < HD, mixed[0], mixed[1]
        ).astype(BF16)
        flat = jnp.where(lane < HD, logs[0], logs[1]).T
        logs_ref[t, h, 0:1, start : start + rows] = flat[0:1, :]
        logs_ref[t, h, 1:2, start : start + rows] = flat[HD : HD + 1, :]


def gather_all(lengths, tables, cotangent, qkv, out, up, down, vec):
    share, span = tables.shape[0] // 4, tables.shape[1] * 4
    vmem = pl.BlockSpec(memory_space=pltpu.VMEM)
    hbm = pl.BlockSpec(memory_space=pl.ANY)
    shape = lambda a: jax.ShapeDtypeStruct((8,) + a.shape[1:], BF16)
    rows = share * span
    logs = (share, STEPS // share, 8, LEN)
    return pl.pallas_call(
        gather_kernel,
        in_specs=[pl.BlockSpec(memory_space=pltpu.SMEM)] + [vmem] * 7,
        out_specs=[hbm] * 10,
        out_shape=[
            jax.ShapeDtypeStruct((share, span, D), BF16),
            jax.ShapeDtypeStruct((share, span, D), BF16),
            shape(qkv), shape(out), shape(up), shape(down), shape(vec),
            jax.ShapeDtypeStruct((rows, 3 * D), BF16),
            jax.ShapeDtypeStruct((rows, D), BF16),
            jax.ShapeDtypeStruct(logs, F32),
        ],
        scratch_shapes=[
            pltpu.VMEM((share, span, D), BF16),
            pltpu.VMEM((8,) + qkv.shape[1:], BF16),
            pltpu.VMEM((8,) + vec.shape[1:], BF16),
            pltpu.VMEM((rows, 3 * D), BF16),
            pltpu.VMEM((rows, D), BF16),
            pltpu.VMEM(logs, F32),
            pltpu.SemaphoreType.DMA((G_WIRES,)),
            pltpu.SemaphoreType.DMA((G_WIRES,)),
            pltpu.SemaphoreType.DMA((13,)),
        ],
        compiler_params=pltpu.CompilerParams(
            collective_id=0, has_side_effects=True, vmem_limit_bytes=VMEM_ALL
        ),
        name="gather_attend",
    )(lengths, tables, cotangent, qkv, out, up, down, vec)


class Plan:
    def __init__(self, send, recv):
        self.send, self.recv, self.makers = send, recv, []

    def add(self, maker):
        self.makers.append(maker)
        return len(self.makers) - 1

    def build(self, index):
        src, dst, (z, x, y, c) = self.makers[index]()
        return pltpu.make_async_remote_copy(
            src_ref=src,
            dst_ref=dst,
            send_sem=self.send.at[index],
            recv_sem=self.recv.at[index],
            device_id=(z * 2 + x, y * 2 + c),
            device_id_type=MESH_ID,
        )

    def start(self, index):
        self.build(index).start()

    def arrived(self, index):
        self.build(index).wait_recv()

    def finish(self):
        for index in range(len(self.makers)):
            self.build(index).wait_send()


class Slab:
    def __init__(self, rows, cols, split, axis, first=0, dtype=BF16):
        self.rows, self.cols, self.split, self.axis = rows, cols, split, axis
        self.first, self.dtype = first, dtype
        self.tile = 128 if axis == 1 else (16 if dtype == BF16 else 8)

    def cut(self, index):
        size = self.cols if self.axis == 1 else self.rows
        part = pl.ds(pl.multiple_of(self.first + index * size, self.tile), size)
        if self.axis == 1:
            return pl.ds(0, self.rows), part
        return part, pl.ds(0, self.cols)

    def scratch(self):
        ways = 2 if self.split else 1
        vmem = lambda *lead: pltpu.VMEM(lead + (self.rows, self.cols), self.dtype)
        late = vmem(4, 2) if self.split else vmem(1, 1)
        return [vmem(ways, 4, 2), vmem(ways, 4, 2), late, vmem(4), vmem(3), vmem()]

    def copies(self):
        return (2 if self.split else 1) + 1 + 1 + 3 + 3


class Reduction:
    def __init__(self, slab, source, target, scratch, plan, own, own_at):
        self.slab, self.source, self.target, self.plan = slab, source, target, plan
        self.held, self.from_c, self.from_y, self.from_x, self.from_z, self.done = scratch
        self.own, self.own_at = own, own_at
        z, x, y, c = place()
        self.at = z, x, y, c
        self.slot = y if slab.split else 0
        side = (z, x, y, 1 - c)
        over = (z, x, 1 - y, c)

        def index_of(half, core):
            return half * 2 + core if slab.split else core

        def cut_all(ref, index):
            rows, cols = slab.cut(index)
            return ref.at[:, :, rows, cols]

        def cut_out(index):
            rows, cols = slab.cut(index)
            return target.at[rows, cols]

        ways = 2 if slab.split else 1
        self.loads = [
            lambda half=half: pltpu.make_async_copy(
                cut_all(source, index_of(half, c)), self.held.at[half], own.at[own_at + half]
            )
            for half in range(ways)
        ]
        self.to_core = [
            plan.add(
                lambda half=half: (
                    cut_all(source, index_of(half, 1 - c)), self.from_c.at[half], side,
                )
            )
            for half in range(ways)
        ]
        if slab.split:
            self.to_y = plan.add(lambda: (self.held.at[1 - y], self.from_y, over))
        else:
            self.to_y = plan.add(lambda: (self.done, self.from_y.at[0, 0], over))
        self.to_x = plan.add(
            lambda: (self.held.at[self.slot, :, 1 - x], self.from_x, (z, 1 - x, y, c))
        )
        self.to_z = [
            plan.add(
                lambda j=j: (
                    self.held.at[self.slot, (z + j) % 4, x],
                    self.from_z.at[j - 1],
                    ((z + j) % 4, x, y, c),
                )
            )
            for j in range(1, 4)
        ]
        mine = lambda: cut_out(index_of(y, c))
        self.store = lambda: pltpu.make_async_copy(self.done, mine(), own.at[own_at + 2])
        self.share_core = plan.add(lambda: (self.done, mine(), side))
        if slab.split:
            theirs = lambda: cut_out(index_of(1 - y, c))
            self.share_y = plan.add(lambda: (self.done, mine(), over))
            self.share_far = plan.add(lambda: (theirs(), theirs(), side))

    def begin(self):
        for load in self.loads:
            load().start()
        for index in self.to_core:
            self.plan.start(index)

    def summed(self, total, *others):
        value = total[...].astype(F32)
        for other in others:
            value = value + other[...].astype(F32)
        total[...] = value.astype(self.slab.dtype)

    def after_core(self):
        for half, load in enumerate(self.loads):
            load().wait()
            self.plan.arrived(self.to_core[half])

        def step(t, carry):
            for half in range(len(self.loads)):
                self.summed(self.held.at[half, t // 2, t % 2], self.from_c.at[half, t // 2, t % 2])
            return carry

        lax.fori_loop(0, 8, step, 0)
        self.plan.start(self.to_y if self.slab.split else self.to_x)

    def after_y(self):
        if not self.slab.split:
            return
        self.plan.arrived(self.to_y)

        def step(t, carry):
            self.summed(self.held.at[self.slot, t // 2, t % 2], self.from_y.at[t // 2, t % 2])
            return carry

        lax.fori_loop(0, 8, step, 0)
        self.plan.start(self.to_x)

    def after_x(self):
        z, x, y, c = self.at
        self.plan.arrived(self.to_x)

        def step(t, carry):
            self.summed(self.held.at[self.slot, t, x], self.from_x.at[t])
            return carry

        lax.fori_loop(0, 4, step, 0)
        for index in self.to_z:
            self.plan.start(index)

    def after_z(self):
        z, x, y, c = self.at
        for index in self.to_z:
            self.plan.arrived(index)
        value = self.held[self.slot, z, x].astype(F32)
        for j in range(3):
            value = value + self.from_z[j].astype(F32)
        self.done[...] = value.astype(self.slab.dtype)
        if self.slab.split:
            self.plan.start(self.share_y)
            self.plan.start(self.share_core)
            self.store().start()
        else:
            self.plan.start(self.to_y)

    def after_final(self):
        if self.slab.split:
            self.plan.arrived(self.share_y)
            self.plan.start(self.share_far)
        else:
            self.plan.arrived(self.to_y)
            self.plan.build(self.to_y).wait_send()
            self.summed(self.done, self.from_y.at[0, 0])
            self.plan.start(self.share_core)
            self.store().start()

    def end(self):
        self.plan.arrived(self.share_core)
        if self.slab.split:
            self.plan.arrived(self.share_far)
        self.store().wait()

    def finish_sends(self):
        done_early = () if self.slab.split else (self.to_y,)
        sends = self.to_core + [self.to_y, self.to_x] + self.to_z + [self.share_core]
        if self.slab.split:
            sends += [self.share_y, self.share_far]
        for index in sends:
            if index not in done_early:
                self.plan.build(index).wait_send()


SLABS = {
    "down_y": (1, Slab(64, D, True, 0)),
    "up_low": (0, Slab(96, D, False, 1)),
    "down": (1, Slab(64, D, False, 0, first=256)),
    "up_high": (0, Slab(96, D, False, 1, first=2 * D)),
    "out": (3, Slab(96, D // 2, False, 1)),
    "v": (2, Slab(96, D // 2, False, 1, first=2 * D)),
    "k": (2, Slab(96, D // 2, False, 1, first=D)),
    "q": (2, Slab(96, D // 2, False, 1)),
}


def attend_back(live, acts, mixed_ref, logs_ref, do_ref, d_ref, vec_ref, t, h, base, cols):
    masks = head_masks(BF16)
    rows_all = pl.ds(base, LEN)
    keys = acts[rows_all, cols[1]]
    values = acts[rows_all, cols[2]]
    query = acts[rows_all, cols[0]] * jnp.asarray(HD ** (-0.5), BF16)
    grad_out = do_ref[rows_all, cols[0]]
    dots = (grad_out.astype(F32) * mixed_ref[rows_all, cols[0]].astype(F32)).T
    rows = 256
    q_masked = [query * m for m in masks]
    g_masked = [grad_out * m for m in masks]
    deltas = [jnp.sum(dots[i * HD : (i + 1) * HD, :], axis=0, keepdims=True) for i in range(2)]
    logs = [logs_ref[t, h, i : i + 1, :] for i in range(2)]
    grad_q = jnp.zeros((LEN, PAIR), F32)
    sum_v = jnp.zeros((1, PAIR), F32)
    for start in range(0, LEN, rows):
        part_k = keys[start : start + rows, :]
        part_v = values[start : start + rows, :]
        key_at = start + lax.broadcasted_iota(jnp.int32, (rows, 1), 0)
        bias = jnp.where(key_at < live, 0.0, NEGATIVE)
        grad_k = jnp.zeros((rows, PAIR), F32)
        grad_v = jnp.zeros((rows, PAIR), F32)
        for head in range(2):
            scores = back_mul(part_k, q_masked[head])
            probs = jnp.exp(scores + bias - logs[head])
            grad_probs = back_mul(part_v, g_masked[head])
            grad_s = (probs * (grad_probs - deltas[head])).astype(BF16)
            grad_v += jnp.dot(probs.astype(BF16), g_masked[head], preferred_element_type=F32)
            grad_k += jnp.dot(grad_s, q_masked[head], preferred_element_type=F32)
            grad_q += inner(grad_s, part_k * masks[head])
        d_ref[pl.ds(base + start, rows), cols[1]] = grad_k.astype(BF16)
        d_ref[pl.ds(base + start, rows), cols[2]] = grad_v.astype(BF16)
        sum_v += jnp.sum(grad_v, axis=0, keepdims=True)
    grad_q = grad_q * HD ** (-0.5)
    d_ref[rows_all, cols[0]] = grad_q.astype(BF16)
    vec_ref[0:1, cols[0]] += jnp.sum(grad_q, axis=0, keepdims=True)
    vec_ref[1:2, cols[0]] += sum_v


N_LOADS = 7


def reduce_kernel(
    len_ref, acts_in, mixed_in, do_in, logs_in, x_in, w_in, one_in, y_in, vec_in,
    up_in, down_in, out_in,
    gin_out, y_out, up_out, down_out, qkv_out, out_out, vec_out,
    acts, mixed, do, logs, x_all, w_all, one, x_turned, d, gw, gin, vec, vec_from, *rest,
):
    scratch, (send, recv, own) = rest[:-3], rest[-3:]
    z, x, y, c = place()
    blk = y * 2 + c
    loads = [
        lambda at=at, src=src, dst=dst: pltpu.make_async_copy(src, dst, own.at[at])
        for at, (src, dst) in enumerate(
            (
                (acts_in, acts), (mixed_in, mixed), (do_in, do), (logs_in, logs),
                (x_in, x_all), (w_in, w_all), (one_in, one),
            )
        )
    ]
    for load in loads:
        load().start()
    greet(all_peers())
    plan = Plan(send, recv)
    share, span = gin_out.shape[0] // 4, gin_out.shape[1]
    sources, targets = (up_in, down_in, gw, out_in), (up_out, down_out, qkv_out, out_out)
    works = {}
    for at, (name, (number, slab)) in enumerate(SLABS.items()):
        part = scratch[6 * at : 6 * at + 6]
        works[name] = Reduction(
            slab, sources[number], targets[number], part, plan, own, N_LOADS + 2 + 3 * at
        )
    mine = pl.ds(blk * share, share)
    slot = pl.ds(pl.multiple_of(blk * span, span), span)
    kept = [
        lambda at=at, src=src, dst=dst: pltpu.make_async_copy(
            src.at[:, slot, :], dst.at[mine], own.at[N_LOADS + at]
        )
        for at, (src, dst) in enumerate(((gin, gin_out), (y_in, y_out)))
    ]

    def trade(src, dst):
        made = []
        for other in ((z, x, 1 - y, c), (z, x, 1 - y, 1 - c), (z, x, y, 1 - c)):
            their = other[2] * 2 + other[3]
            made.append(
                plan.add(
                    lambda their=their, other=other: (
                        src.at[:, pl.ds(pl.multiple_of(their * span, span), span), :],
                        dst.at[mine],
                        other,
                    )
                )
            )
        return made

    trade_g, trade_y = trade(gin, gin_out), trade(y_in, y_out)
    ways = [(z, x, y, 1 - c), (z, x, 1 - y, c), (z, 1 - x, y, c)]
    ways += [((z + j) % 4, x, y, c) for j in range(1, 4)]
    vec_sends = [
        plan.add(lambda at=at, to=to: (vec.at[min(at, 3)], vec_from.at[at], to))
        for at, to in enumerate(ways)
    ]

    def vec_task(at):
        if at == 0:
            plan.start(vec_sends[0])
            return
        plan.arrived(vec_sends[at - 1])
        vec[at] = vec[at - 1] + vec_from[at - 1]
        for index in vec_sends[at:] if at == 3 else vec_sends[at : at + 1]:
            plan.start(index)

    def vec_end():
        for index in vec_sends[3:]:
            plan.arrived(index)
        vec_out[...] = vec[3] + vec_from[3] + vec_from[4] + vec_from[5]

    def do_tasks(todo):
        for entry in todo:
            if entry[0] == "vec":
                vec_task(entry[1])
            elif entry[0] == "trade":
                for index in trade_y:
                    plan.start(index)
            else:
                getattr(works[entry[0]], entry[1])()

    vec[0] = vec_in[...]
    for name in ("down_y", "up_low", "down", "up_high", "out"):
        works[name].begin()
    kept[1]().start()
    for load in loads[:4]:
        load().wait()

    def step(s, carry):
        for when, todo in DURING.items():

            @pl.when(s == when)
            def _(todo=todo):
                do_tasks(todo)

        t, h = s // (STEPS // share), s % (STEPS // share)
        base = pl.multiple_of(t * LEN, LEN)
        cols = [pl.ds(pl.multiple_of(part * D + h * PAIR, PAIR), PAIR) for part in range(3)]
        attend_back(len_ref[t], acts, mixed, logs, do, d, vec.at[0], t, h, base, cols)
        return carry

    lax.fori_loop(0, STEPS, step, 0)
    do_tasks(AFTER["attention"])
    loads[4]().wait()
    rows = share * LEN
    x_turned[...] = x_all[...].T
    tile = 256
    for part, name in ((2, "v"), (1, "k"), (0, "q")):

        def grad_tile(i, carry, part=part):
            cols = pl.ds(pl.multiple_of(part * D + i * tile, tile), tile)
            value = jnp.dot(x_turned[...], d[:, cols], preferred_element_type=F32)
            gw[:, :, :, cols] = value.astype(BF16).reshape(4, 2, D // 8, tile)
            return carry

        lax.fori_loop(0, D // tile, grad_tile, 0)
        works[name].begin()
        do_tasks(AFTER[name])
    loads[5]().wait()
    loads[6]().wait()

    for i in range(D // tile):
        value = back_mul(d[...], w_all[pl.ds(i * tile, tile), :])
        value = value + one[:, i * tile : (i + 1) * tile]
        gin[:, :, i * tile : (i + 1) * tile] = value.astype(BF16).reshape(share, LEN, tile)
        do_tasks(AFTER[i])
    for index in trade_g:
        plan.start(index)
    kept[0]().start()
    do_tasks(AFTER["end"])
    vec_end()
    for work in works.values():
        work.end()
    for index in trade_g + trade_y:
        plan.arrived(index)
    for work in works.values():
        work.finish_sends()
    for index in trade_g + trade_y + vec_sends:
        plan.build(index).wait_send()
    for made in kept:
        made().wait()


DURING = {
    2: [("down_y", "after_core")],
    3: [("up_low", "after_core"), ("trade",)],
    4: [("down", "after_core")],
    5: [("up_high", "after_core")],
    6: [("out", "after_core")],
    10: [("down_y", "after_y"), ("up_low", "after_x")],
}
AFTER = {
    "attention": [("vec", 0)],
    "v": [("down", "after_x"), ("vec", 1)],
    "k": [("v", "after_core"), ("vec", 2)],
    "q": [("k", "after_core"), ("vec", 3), ("up_low", "after_z")],
    0: [("q", "after_core")],
    1: [("up_high", "after_x")],
    2: [("up_low", "after_final"), ("down", "after_z")],
    "end": [
        ("out", "after_x"),
        ("down_y", "after_x"),
        ("down", "after_final"),
        ("up_high", "after_z"),
        ("up_high", "after_final"),
        ("v", "after_x"),
        ("out", "after_z"),
        ("k", "after_x"),
        ("down_y", "after_z"),
        ("out", "after_final"),
        ("q", "after_x"),
        ("v", "after_z"),
        ("down_y", "after_final"),
        ("v", "after_final"),
        ("k", "after_z"),
        ("q", "after_z"),
        ("k", "after_final"),
        ("q", "after_final"),
    ],
}


def reduce_all(lengths, acts, mixed, do, logs, rows, whole, one, result, vec, up, down, out):
    share, length = result.shape[:2]
    vmem = pl.BlockSpec(memory_space=pltpu.VMEM)
    hbm = pl.BlockSpec(memory_space=pl.ANY)
    shape = lambda a: jax.ShapeDtypeStruct(a.shape[2:], a.dtype)
    back = jax.ShapeDtypeStruct((share * 4, length // 4, D), BF16)
    scratch = [s for _, slab in SLABS.values() for s in slab.scratch()]
    wires = 12 + sum(slab.copies() for _, slab in SLABS.values())
    like = lambda a: pltpu.VMEM(a.shape, a.dtype)
    return pl.pallas_call(
        reduce_kernel,
        in_specs=[pl.BlockSpec(memory_space=pltpu.SMEM)] + [hbm] * 7 + [vmem] * 2 + [hbm] * 3,
        out_specs=[hbm] * 6 + [vmem],
        out_shape=[
            back, back, shape(up), shape(down),
            jax.ShapeDtypeStruct((D // 8, 3 * D), BF16),
            shape(out),
            jax.ShapeDtypeStruct((16, D), F32),
        ],
        scratch_shapes=[like(a) for a in (acts, mixed, do, logs, rows, whole, one)]
        + [
            pltpu.VMEM(rows.shape[::-1], BF16),
            pltpu.VMEM(acts.shape, BF16),
            pltpu.VMEM((4, 2, D // 8, 3 * D), BF16),
            pltpu.VMEM((share, length, D), BF16),
            pltpu.VMEM((4, 16, D), F32),
            pltpu.VMEM((6, 16, D), F32),
        ]
        + scratch
        + [
            pltpu.SemaphoreType.DMA((wires,)),
            pltpu.SemaphoreType.DMA((wires,)),
            pltpu.SemaphoreType.DMA((N_LOADS + 2 + 3 * len(SLABS),)),
        ],
        compiler_params=pltpu.CompilerParams(
            collective_id=1, has_side_effects=True, vmem_limit_bytes=VMEM_ALL
        ),
        name="attend_reduce",
    )(lengths, acts, mixed, do, logs, rows, whole, one, result, vec, up, down, out)


def local(*args):
    tables, lengths, cotangent, step_count = args[:4]
    masters, firsts, seconds = args[4:9], args[9:14], args[14:19]
    w_qkv, w_out, w_up, w_down, vectors = masters
    blocks = lax.axis_size("blk")
    shards = lax.axis_size("tab")
    table_count, local_len = tables.shape[:2]
    share = table_count // blocks
    tuned = shards == 8 and blocks == 4
    owned = vectors.shape[0]
    vec_own = jnp.pad(vectors.astype(BF16).T, ((0, 4), (0, 0)))
    narrow = [w.astype(BF16) for w in (w_qkv, w_out, w_up, w_down)]
    my_lengths = lax.dynamic_slice(lengths, (lax.axis_index("blk") * share,), (share,))
    if tuned:
        at_own = (0, lax.axis_index("tab") * owned)
        vec_wide = lax.dynamic_update_slice(jnp.zeros((16, D), BF16), vec_own, at_own)
        mine, cot, *wholes, qkv, mixed, logs = gather_all(
            my_lengths, tables, cotangent, *[w[None] for w in narrow], vec_wide[None]
        )
        vec_f = jnp.sum(wholes[4].astype(F32), axis=0)[:12]
    else:
        spread = partial(lax.all_to_all, axis_name="blk", split_axis=0, concat_axis=1, tiled=True)
        mine, cot = spread(tables), spread(cotangent)
        wholes = [lax.all_gather(w, "tab", axis=0) for w in narrow + [vec_own]]
        vec_f = wholes[4][:, :12].transpose(1, 0, 2).reshape(12, D).astype(F32)
    full_qkv, full_out, full_up, full_down = [
        w.reshape(-1, w.shape[-1]) for w in wholes[:4]
    ]
    bias_up = vec_f[8:12].reshape(-1)
    rows = mine.reshape(-1, D)
    if not tuned:
        bias_qkv = jnp.concatenate([vec_f[0], jnp.zeros((D,), F32), vec_f[1]])
        qkv = (jnp.dot(rows, full_qkv, preferred_element_type=F32) + bias_qkv).astype(BF16)
        mixed, logs = attention_forward(my_lengths, qkv, share)
    attn_out = jnp.dot(mixed, full_out, preferred_element_type=F32) + vec_f[2]
    normed_one, norm_one_back = jax.vjp(
        layer_norm, rows.astype(F32) + attn_out, vec_f[4], vec_f[5]
    )
    normed_b = normed_one.astype(BF16)
    hidden = jnp.dot(normed_b, full_up, preferred_element_type=F32) + bias_up
    below = 0.5 * (1.0 + lax.erf(hidden * 0.5**0.5))
    active_b = (hidden * below).astype(BF16)
    slope = below + hidden * jnp.exp(-0.5 * hidden * hidden) * (2.0 * math.pi) ** -0.5
    active_b, slope = lax.optimization_barrier((active_b, slope.astype(BF16)))
    branch = jnp.dot(active_b, full_down, preferred_element_type=F32) + vec_f[3]
    result, norm_two_back = jax.vjp(layer_norm, normed_one + branch, vec_f[6], vec_f[7])
    result = result.astype(BF16).reshape(mine.shape)
    grad_two, grad_g2, grad_c2 = norm_two_back(cot.reshape(-1, D).astype(F32))
    grad_b2 = jnp.sum(grad_two, axis=0)
    branch_b = grad_two.astype(BF16)
    gw_down = inner(active_b, branch_b).astype(BF16)
    grad_hidden = back_mul(branch_b, full_down) * slope.astype(F32)
    grad_b1 = jnp.sum(grad_hidden, axis=0)
    hidden_b = grad_hidden.astype(BF16)
    gw_up = inner(normed_b, hidden_b).astype(BF16)
    grad_one, grad_g1, grad_c1 = norm_one_back(grad_two + back_mul(hidden_b, full_up))
    grad_bo = jnp.sum(grad_one, axis=0)
    attn_b = grad_one.astype(BF16)
    gw_out = inner(mixed, attn_b).astype(BF16)
    grad_mixed = back_mul(attn_b, full_out).astype(BF16)
    norm_rows = [grad_bo, grad_b2, grad_g1, grad_c1, grad_g2, grad_c2]
    if tuned:
        empty = jnp.zeros((2, D), F32)
        wide_vec = jnp.concatenate(
            [empty, jnp.stack(norm_rows), grad_b1.reshape(4, D), empty, empty]
        )
        by_owner = lambda g: g.reshape(4, 2, -1, g.shape[-1])
        grad_input, output, *sums = reduce_all(
            my_lengths, qkv, mixed, grad_mixed, logs, rows, full_qkv, grad_one, result,
            wide_vec, by_owner(gw_up), by_owner(gw_down), by_owner(gw_out),
        )
        at_own = (0, lax.axis_index("tab") * owned)
        sum_vec = lax.dynamic_slice(sums[4], at_own, (16, owned))[:12].T
        shares = [s.astype(F32) for s in (sums[2], sums[3], sums[0], sums[1], sum_vec)]
    else:
        grad_three, sums = attention_backward(my_lengths, qkv, mixed, logs, grad_mixed, share)
        sums = jnp.sum(sums[:, :, :2], axis=0)
        grad_bq, grad_bv = sums[:, 0].reshape(-1), sums[:, 1].reshape(-1)
        grad_qkv = jnp.concatenate([grad_three[i] for i in range(3)], axis=1)
        gw_qkv = inner(rows, grad_qkv).astype(BF16)
        grad_in = grad_one + back_mul(grad_qkv, full_qkv)
        grad_in = grad_in.astype(BF16).reshape(mine.shape)
        gw_vec = jnp.concatenate(
            [jnp.stack([grad_bq, grad_bv] + norm_rows), grad_b1.reshape(4, D)]
        )
        back = partial(lax.all_to_all, axis_name="blk", split_axis=1, concat_axis=0, tiled=True)
        grad_input, output = back(grad_in), back(result)

        def collect(grad):
            part = lax.psum_scatter(
                grad.reshape(shards, -1, grad.shape[-1]), "tab", scatter_dimension=0
            )
            return lax.psum(part.astype(BF16), "blk").astype(F32)

        shares = [collect(g) for g in (gw_qkv, gw_out, gw_up, gw_down)]
        shares.append(collect(gw_vec.T.astype(BF16)))
    grad_input = grad_input.astype(F32)
    step_float = step_count[0].astype(F32)
    results = [output, grad_input]
    for at in range(5):
        results.extend(
            adam(masters[at], shares[at], firsts[at], seconds[at], RATES[at], step_float)
        )
    return tuple(results)


def solution(mesh):
    tokens, flat, rows = P("tab", "blk", None), P("tab"), P("tab", None)
    return jax.shard_map(
        local,
        mesh=mesh,
        in_specs=(tokens, flat, tokens, P()) + (rows,) * 15,
        out_specs=(tokens, tokens) + (rows,) * 20,
        check_vma=False,
    )
```

```python
import math
from functools import partial

import jax
import jax.numpy as jnp
from jax import lax
from jax.experimental import pallas as pl
from jax.experimental.pallas import tpu as pltpu
from jax.sharding import PartitionSpec as P

D = 768
H = 12
HD = 64
LEN = 512
FF = 3072
PAIR = 2 * HD

EPS = 1e-06
NEGATIVE = -1e30
BETA_ONE = 0.9
BETA_TWO = 0.999
ADAM_EPS = 1e-08
DECAY = 0.01
RATES = (1.0, 15.0, 1.0, 0.5, 5.0)

F32 = jnp.float32
BF16 = jnp.bfloat16
MESH_ID = pl.DeviceIdType.MESH
VMEM_ALL = 64 * 1000 * 1024


def layer_norm(hidden, gain_vec, shift_vec):
    row_mean = jnp.mean(hidden, axis=-1, keepdims=True)
    centred = hidden - row_mean
    variance = jnp.mean(centred * centred, axis=-1, keepdims=True)
    return centred * lax.rsqrt(variance + EPS) * gain_vec + shift_vec


def inner(left, right):
    return lax.dot_general(left, right, (((0,), (0,)), ((), ())), preferred_element_type=F32)


def back_mul(left, right):
    return lax.dot_general(left, right, (((1,), (1,)), ((), ())), preferred_element_type=F32)


def adam(master, gradient, first_moment, second_moment, rate_now, step_float):
    moment_new = BETA_ONE * first_moment + (1.0 - BETA_ONE) * gradient
    square_new = BETA_TWO * second_moment + (1.0 - BETA_TWO) * gradient * gradient
    fix_one = 1.0 - jnp.power(BETA_ONE, step_float)
    fix_two = 1.0 - jnp.power(BETA_TWO, step_float)
    update = moment_new / fix_one / (jnp.sqrt(square_new / fix_two) + ADAM_EPS)
    master_new = master - rate_now * (update + DECAY * master)
    return (moment_new, square_new, master_new, master_new.astype(BF16))


def head_masks(dtype):
    lane = lax.broadcasted_iota(jnp.int32, (1, PAIR), 1)
    return [(lane < HD).astype(dtype), (lane >= HD).astype(dtype)]


def attn_fwd_kernel(len_ref, q_ref, k_ref, v_ref, o_ref, l_ref):
    live = len_ref[pl.program_id(0)]
    masks = head_masks(BF16)
    keys = k_ref[...]
    values = v_ref[...]
    rows = 256
    key_at = lax.broadcasted_iota(jnp.int32, (1, LEN), 1)
    bias = jnp.where(key_at < live, 0.0, NEGATIVE)
    lane = lax.broadcasted_iota(jnp.int32, (1, PAIR), 1)
    for start in range(0, LEN, rows):
        query = q_ref[pl.ds(start, rows), :] * jnp.asarray(HD ** (-0.5), BF16)
        mixed, logs = [], []
        for head in range(2):
            scores = back_mul(query * masks[head], keys) + bias
            top = jnp.max(scores, axis=-1, keepdims=True)
            raised = jnp.exp(scores - top)
            total = jnp.sum(raised, axis=-1, keepdims=True)
            probs = (raised * (1.0 / total)).astype(BF16)
            mixed.append(jnp.dot(probs, values, preferred_element_type=F32))
            logs.append(top + jnp.log(total))
        o_ref[pl.ds(start, rows), :] = jnp.where(lane < HD, mixed[0], mixed[1]).astype(BF16)
        both = jnp.where(lane < HD, logs[0], logs[1])
        flat = both.T
        l_ref[0, 0, 0:1, pl.ds(start, rows)] = flat[0:1, :]
        l_ref[0, 0, 1:2, pl.ds(start, rows)] = flat[HD : HD + 1, :]


def attention_forward(lengths, qkv, tables):
    pairs = H // 2
    spec = lambda part: pl.BlockSpec((LEN, PAIR), lambda t, h, n: (t, part * pairs + h))
    return pl.pallas_call(
        attn_fwd_kernel,
        grid_spec=pltpu.PrefetchScalarGridSpec(
            num_scalar_prefetch=1,
            grid=(tables, pairs),
            in_specs=[spec(0), spec(1), spec(2)],
            out_specs=[
                pl.BlockSpec((LEN, PAIR), lambda t, h, n: (t, h)),
                pl.BlockSpec((1, 1, 8, LEN), lambda t, h, n: (t, h, 0, 0)),
            ],
        ),
        out_shape=[
            jax.ShapeDtypeStruct((tables * LEN, D), BF16),
            jax.ShapeDtypeStruct((tables, pairs, 8, LEN), F32),
        ],
        name="attn_fwd",
    )(lengths, qkv, qkv, qkv)


def attn_bwd_kernel(len_ref, q_ref, k_ref, v_ref, o_ref, l_ref, do_ref, d_ref, sums_ref):
    live = len_ref[pl.program_id(0)]
    masks = head_masks(BF16)
    keys = k_ref[...]
    values = v_ref[...]
    query = q_ref[...] * jnp.asarray(HD ** (-0.5), BF16)
    grad_out = do_ref[...]
    dots = (grad_out.astype(F32) * o_ref[...].astype(F32)).T
    rows = 256
    q_masked = [query * m for m in masks]
    g_masked = [grad_out * m for m in masks]
    deltas = [jnp.sum(dots[h * HD : (h + 1) * HD, :], axis=0, keepdims=True) for h in range(2)]
    logs = [l_ref[0, 0, h : h + 1, :] for h in range(2)]
    grad_q = jnp.zeros((LEN, PAIR), F32)
    sum_v = jnp.zeros((1, PAIR), F32)
    for start in range(0, LEN, rows):
        part_k = keys[start : start + rows, :]
        part_v = values[start : start + rows, :]
        key_at = start + lax.broadcasted_iota(jnp.int32, (rows, 1), 0)
        bias = jnp.where(key_at < live, 0.0, NEGATIVE)
        grad_k = jnp.zeros((rows, PAIR), F32)
        grad_v = jnp.zeros((rows, PAIR), F32)
        for head in range(2):
            scores = back_mul(part_k, q_masked[head])
            probs = jnp.exp(scores + bias - logs[head])
            grad_probs = back_mul(part_v, g_masked[head])
            grad_s = (probs * (grad_probs - deltas[head])).astype(BF16)
            grad_v += jnp.dot(probs.astype(BF16), g_masked[head], preferred_element_type=F32)
            grad_k += jnp.dot(grad_s, q_masked[head], preferred_element_type=F32)
            grad_q += inner(grad_s, part_k * masks[head])
        d_ref[1, pl.ds(start, rows), :] = grad_k.astype(BF16)
        d_ref[2, pl.ds(start, rows), :] = grad_v.astype(BF16)
        sum_v += jnp.sum(grad_v, axis=0, keepdims=True)
    grad_q = grad_q * HD ** (-0.5)
    d_ref[0, :, :] = grad_q.astype(BF16)
    sums_ref[0, 0, 0:1, :] = jnp.sum(grad_q, axis=0, keepdims=True)
    sums_ref[0, 0, 1:2, :] = sum_v


def attention_backward(lengths, qkv, mixed, logs, grad_mixed, tables):
    pairs = H // 2
    spec = lambda part: pl.BlockSpec((LEN, PAIR), lambda t, h, n: (t, part * pairs + h))
    block = pl.BlockSpec((LEN, PAIR), lambda t, h, n: (t, h))
    return pl.pallas_call(
        attn_bwd_kernel,
        grid_spec=pltpu.PrefetchScalarGridSpec(
            num_scalar_prefetch=1,
            grid=(tables, pairs),
            in_specs=[
                spec(0),
                spec(1),
                spec(2),
                block,
                pl.BlockSpec((1, 1, 8, LEN), lambda t, h, n: (t, h, 0, 0)),
                block,
            ],
            out_specs=[
                pl.BlockSpec((3, LEN, PAIR), lambda t, h, n: (0, t, h)),
                pl.BlockSpec((1, 1, 8, PAIR), lambda t, h, n: (t, h, 0, 0)),
            ],
        ),
        out_shape=[
            jax.ShapeDtypeStruct((3, tables * LEN, D), BF16),
            jax.ShapeDtypeStruct((tables, pairs, 8, PAIR), F32),
        ],
        name="attn_bwd",
    )(lengths, qkv, qkv, qkv, mixed, logs, grad_mixed)


def place():
    tab, blk = lax.axis_index("tab"), lax.axis_index("blk")
    return tab // 2, tab % 2, blk // 2, blk % 2


def z_line():
    z = place()[0]
    inner = (z + 1) // 2 % 2
    near = inner * (z - 1) * 3 + (1 - inner) * (1 + z // 3)
    second = inner * (3 - z) + (1 - inner) * (3 - near)
    third = inner * (3 - near) + (1 - inner) * (3 - z)
    return inner, near, (near, second, third)


def greet(peers):
    barrier = pltpu.get_barrier_semaphore()
    for z, x, y, c in peers:
        pl.semaphore_signal(
            barrier, inc=1, device_id=(z * 2 + x, y * 2 + c), device_id_type=MESH_ID
        )
    pl.semaphore_wait(barrier, len(peers))


def all_peers():
    z, x, y, c = place()
    z_peers = [((z + j) % 4, x, y, c) for j in range(1, 4)]
    rest = [(z, 1 - x, y, c), (z, x, 1 - y, c), (z, x, y, 1 - c), (z, x, 1 - y, 1 - c)]
    return z_peers + rest


def by_columns(width):
    return lambda ref, t, part: ref.at[t, :, pl.ds(pl.multiple_of(part * width, 128), width)]


def by_rows(height):
    return lambda ref, t, part: ref.at[t, pl.ds(pl.multiple_of(part * height, 16), height), :]


PIECES = (
    (by_columns(3 * D // 2), False),
    (by_columns(D // 2), False),
    (by_columns(FF // 4), True),
    (by_rows(FF // 16), False),
)
G_WIRES = 96
STEPS = 12


class Gather:
    def __init__(self, at, shard, whole, plan):
        piece, self.split = PIECES[at]
        z, x, y, c = place()
        tab = z * 2 + x
        part = y * 2 + c if self.split else c
        other = (1 - y) * 2 + c
        own = lambda: piece(shard, 0, part)
        self.plan = plan
        self.middle, outer, order = z_line()
        near = lambda j: order[j - 1] * 2 + x
        far = lambda j: order[j - 1] * 2 + 1 - x if j else z * 2 + 1 - x

        def send(at_tab, which, to, first=False, inner=False):
            return plan.add(
                lambda: (
                    own() if first else piece(whole, at_tab, which),
                    piece(whole, at_tab, which),
                    to,
                ),
                inner,
            )

        side, over, across = (z, x, y, 1 - c), (z, x, 1 - y, c), (z, 1 - x, y, c)
        to_outer, to_inner = (outer, x, y, c), (3 - z, x, y, c)
        self.own_near = send(tab, part, to_outer, True)
        self.own_inner = send(tab, part, to_inner, True, inner=True)
        self.passed = [
            send(near(j), part, to_inner if j == 1 else to_outer, inner=True) for j in range(1, 4)
        ]
        self.x = [send(tab, part, across, True)]
        self.x += [send(near(j), part, across) for j in range(1, 4)]
        tabs = [near(j) for j in range(1, 4)] + [far(j) for j in range(4)]
        self.c = [send(t, part, side) for t in tabs]
        self.y = [send(t, part, over) for t in tabs] if self.split else []
        self.late = [send(t, other, side) for t in tabs] if self.split else []

    def send_z(self):
        self.plan.start(self.own_near)

        @pl.when(self.middle == 1)
        def _():
            self.plan.start(self.own_inner)

    def send_x(self):
        self.plan.start(self.x[0])

    def onward(self, at):
        if self.split:
            self.plan.start(self.y[at])
        self.plan.start(self.c[at])

    def task_z(self, j):
        if j == 1:
            self.plan.arrived(self.own_near)
        else:

            @pl.when(self.middle == 0)
            def _():
                self.plan.arrived(self.passed[j - 1])

        @pl.when(self.middle == 1)
        def _():
            if j > 1:
                self.plan.arrived(self.own_inner if j == 2 else self.passed[0])
            self.plan.start(self.passed[j - 1])

        self.plan.start(self.x[j])
        self.onward(j - 1)

    def task_x(self, j):
        self.plan.arrived(self.x[j])
        self.onward(3 + j)

    def task_y(self, at):
        self.plan.arrived(self.y[at])
        self.plan.start(self.late[at])

    def end(self):
        for index in self.c + self.late:
            self.plan.arrived(index)


def gather_kernel(
    len_ref, x_in, cot_in, qkv_wide, out_wide, up_wide, down_wide, vec_in,
    x_out, cot_out, qkv_out, out_out, up_out, down_out, vec_out, acts_out, mixed_out, logs_out,
    qkv_in, out_in, up_in, down_in, x_all, w_all, vec_all, acts, mixed, logs, send, recv, own,
):
    z, x, y, c = place()
    tab, blk = z * 2 + x, y * 2 + c
    share, span = x_in.shape[0] // 4, x_in.shape[1]
    mine = pl.ds(blk * share, share)
    slot = pl.ds(pl.multiple_of(blk * span, span), span)
    plan = Plan(send, recv)
    shards = (qkv_in, out_in, up_in, down_in)
    wholes = (w_all, out_out, up_out, down_out)
    works = [Gather(at, shards[at], wholes[at], plan) for at in range(4)]
    qkv, out, up, down = works

    def trade(src, dst):
        made = []
        for other in ((z, x, 1 - y, c), (z, x, 1 - y, 1 - c), (z, x, y, 1 - c)):
            their = other[2] * 2 + other[3]
            made.append(
                plan.add(
                    lambda their=their, other=other: (
                        src.at[pl.ds(their * share, share)], dst.at[:, slot, :], other,
                    )
                )
            )
        return made

    trade_x, trade_cot = trade(x_in, x_all), trade(cot_in, cot_out)
    vec_z = [
        plan.add(lambda j=j: (vec_in.at[0], vec_all.at[tab], ((z + j) % 4, x, y, c)))
        for j in range(1, 4)
    ]
    vec_x = [plan.add(lambda: (vec_in.at[0], vec_all.at[tab], (z, 1 - x, y, c)))]
    for j in range(1, 4):
        t = (z + 4 - j) % 4 * 2 + x
        vec_x.append(plan.add(lambda t=t: (vec_all.at[t], vec_all.at[t], (z, 1 - x, y, c))))
    keeps = [
        lambda: pltpu.make_async_copy(x_in.at[mine], x_all.at[:, slot, :], own.at[0]),
        lambda: pltpu.make_async_copy(qkv_in.at[0], w_all.at[tab], own.at[1]),
        lambda: pltpu.make_async_copy(vec_in.at[0], vec_all.at[tab], own.at[2]),
        lambda: pltpu.make_async_copy(cot_in.at[mine], cot_out.at[:, slot, :], own.at[3]),
        lambda: pltpu.make_async_copy(out_in.at[0], out_out.at[tab], own.at[4]),
        lambda: pltpu.make_async_copy(up_in.at[0], up_out.at[tab], own.at[5]),
        lambda: pltpu.make_async_copy(down_in.at[0], down_out.at[tab], own.at[6]),
    ]
    puts = [
        lambda: pltpu.make_async_copy(x_all, x_out, own.at[7]),
        lambda: pltpu.make_async_copy(w_all, qkv_out, own.at[8]),
        lambda: pltpu.make_async_copy(vec_all, vec_out, own.at[9]),
        lambda: pltpu.make_async_copy(acts, acts_out, own.at[10]),
        lambda: pltpu.make_async_copy(mixed, mixed_out, own.at[11]),
        lambda: pltpu.make_async_copy(logs, logs_out, own.at[12]),
    ]
    for wide, narrow in zip((qkv_wide, out_wide, up_wide, down_wide), shards):
        narrow[0] = wide[...].astype(BF16)
    greet(all_peers())
    for index in vec_z + vec_x[:1]:
        plan.start(index)
    qkv.send_z()
    qkv.send_x()
    for index in trade_x:
        plan.start(index)
    for keep in keeps:
        keep().start()
    for work in (out, up, down):
        work.send_z()
    out.send_x()
    for index in trade_cot:
        plan.start(index)
    for j in range(1, 4):
        plan.arrived(vec_z[j - 1])
        plan.start(vec_x[j])
    for j in range(1, 4):
        qkv.task_z(j)
    up.send_x()
    down.send_x()
    for j in range(4):
        qkv.task_x(j)
    for index in vec_x:
        plan.arrived(index)
    for keep in keeps[:3]:
        keep().wait()
    for index in trade_x:
        plan.arrived(index)
    qkv.end()
    for put in puts[:3]:
        put().start()

    tile = 256
    rows = share * LEN
    spread = [vec_all[t, 0:16, :].astype(F32) for t in range(8)]
    vectors = spread[0]
    for t in range(1, 8):
        vectors = vectors + spread[t]
    for part in range(3):
        for col in range(0, D, tile):
            at = part * D + col
            weight = w_all[:, :, at : at + tile].reshape(D, tile)
            value = jnp.dot(x_all[...].reshape(rows, D), weight, preferred_element_type=F32)
            if part != 1:
                value = value + vectors[part // 2 : part // 2 + 1, col : col + tile]
            acts[:, at : at + tile] = value.astype(BF16)
    puts[3]().start()

    tasks = {
        0: [lambda j=j: out.task_z(j) for j in (1, 2, 3)],
        1: [lambda: up.task_z(1), lambda: up.task_z(2)],
        2: [lambda j=j: out.task_x(j) for j in range(4)] + [lambda: up.task_z(3)],
        3: [lambda: up.task_x(0)],
        4: [lambda: down.task_z(1)],
        5: [lambda: down.task_z(2), lambda: up.task_x(1)],
        6: [lambda: down.task_x(0), lambda: up.task_x(2)],
        7: [lambda: down.task_z(3)],
        8: [lambda: up.task_x(3), lambda: up.task_y(0)],
        9: [lambda: up.task_y(1), lambda: down.task_x(1)],
        10: [lambda: up.task_y(2), lambda: up.task_y(3)],
        11: [lambda: up.task_y(4), lambda: down.task_x(2)],
        12: [lambda: up.task_y(5), lambda: up.task_y(6), lambda: down.task_x(3)],
    }

    def step(s, carry):
        for when, todo in tasks.items():
            if when < STEPS:

                @pl.when(s == when)
                def _(todo=todo):
                    for task in todo:
                        task()

        t, h = s // (STEPS // share), s % (STEPS // share)
        base = pl.multiple_of(t * LEN, LEN)
        cols = [pl.ds(pl.multiple_of(part * D + h * PAIR, PAIR), PAIR) for part in range(3)]
        attend(len_ref[t], acts, mixed, logs, t, h, base, cols)
        return carry

    lax.fori_loop(0, STEPS, step, 0)
    for put in puts[4:]:
        put().start()
    for task in tasks[STEPS]:
        task()
    for index in trade_cot:
        plan.arrived(index)
    for work in (out, up, down):
        work.end()
    plan.finish(z_line()[0])
    for keep in keeps[3:]:
        keep().wait()
    for put in puts:
        put().wait()


def attend(live, acts, mixed_ref, logs_ref, t, h, base, cols):
    masks = head_masks(BF16)
    keys = acts[pl.ds(base, LEN), cols[1]]
    values = acts[pl.ds(base, LEN), cols[2]]
    rows = 256
    key_at = lax.broadcasted_iota(jnp.int32, (1, LEN), 1)
    bias = jnp.where(key_at < live, 0.0, NEGATIVE)
    lane = lax.broadcasted_iota(jnp.int32, (1, PAIR), 1)
    for start in range(0, LEN, rows):
        query = acts[pl.ds(base + start, rows), cols[0]] * jnp.asarray(HD ** (-0.5), BF16)
        mixed, logs = [], []
        for head in range(2):
            scores = back_mul(query * masks[head], keys) + bias
            top = jnp.max(scores, axis=-1, keepdims=True)
            raised = jnp.exp(scores - top)
            total = jnp.sum(raised, axis=-1, keepdims=True)
            probs = (raised * (1.0 / total)).astype(BF16)
            mixed.append(jnp.dot(probs, values, preferred_element_type=F32))
            logs.append(top + jnp.log(total))
        mixed_ref[pl.ds(base + start, rows), cols[0]] = jnp.where(
            lane < HD, mixed[0], mixed[1]
        ).astype(BF16)
        flat = jnp.where(lane < HD, logs[0], logs[1]).T
        logs_ref[t, h, 0:1, start : start + rows] = flat[0:1, :]
        logs_ref[t, h, 1:2, start : start + rows] = flat[HD : HD + 1, :]


def gather_all(lengths, tables, cotangent, qkv, out, up, down, vec):
    share, span = tables.shape[0] // 4, tables.shape[1] * 4
    vmem = pl.BlockSpec(memory_space=pltpu.VMEM)
    hbm = pl.BlockSpec(memory_space=pl.ANY)
    shape = lambda a: jax.ShapeDtypeStruct((8,) + a.shape[-2:], BF16)
    rows = share * span
    logs = (share, STEPS // share, 8, LEN)
    return pl.pallas_call(
        gather_kernel,
        in_specs=[pl.BlockSpec(memory_space=pltpu.SMEM)] + [vmem] * 7,
        out_specs=[hbm] * 10,
        out_shape=[
            jax.ShapeDtypeStruct((share, span, D), BF16),
            jax.ShapeDtypeStruct((share, span, D), BF16),
            shape(qkv), shape(out), shape(up), shape(down), shape(vec),
            jax.ShapeDtypeStruct((rows, 3 * D), BF16),
            jax.ShapeDtypeStruct((rows, D), BF16),
            jax.ShapeDtypeStruct(logs, F32),
        ],
        scratch_shapes=[
            *[pltpu.VMEM((1,) + w.shape, BF16) for w in (qkv, out, up, down)],
            pltpu.VMEM((share, span, D), BF16),
            pltpu.VMEM((8,) + qkv.shape, BF16),
            pltpu.VMEM((8,) + vec.shape[1:], BF16),
            pltpu.VMEM((rows, 3 * D), BF16),
            pltpu.VMEM((rows, D), BF16),
            pltpu.VMEM(logs, F32),
            pltpu.SemaphoreType.DMA((G_WIRES,)),
            pltpu.SemaphoreType.DMA((G_WIRES,)),
            pltpu.SemaphoreType.DMA((13,)),
        ],
        compiler_params=pltpu.CompilerParams(
            collective_id=0, has_side_effects=True, vmem_limit_bytes=VMEM_ALL
        ),
        name="gather_attend",
    )(lengths, tables, cotangent, qkv, out, up, down, vec)


class Plan:
    def __init__(self, send, recv):
        self.send, self.recv, self.makers, self.inner = send, recv, [], []

    def add(self, maker, inner=False):
        self.makers.append(maker)
        if inner:
            self.inner.append(len(self.makers) - 1)
        return len(self.makers) - 1

    def build(self, index):
        src, dst, (z, x, y, c) = self.makers[index]()
        return pltpu.make_async_remote_copy(
            src_ref=src,
            dst_ref=dst,
            send_sem=self.send.at[index],
            recv_sem=self.recv.at[index],
            device_id=(z * 2 + x, y * 2 + c),
            device_id_type=MESH_ID,
        )

    def start(self, index):
        self.build(index).start()

    def arrived(self, index):
        self.build(index).wait_recv()

    def finish(self, inner):
        for index in range(len(self.makers)):
            if index not in self.inner:
                self.build(index).wait_send()

        @pl.when(inner == 1)
        def _():
            for index in self.inner:
                self.build(index).wait_send()


class Slab:
    def __init__(self, rows, cols, split, axis, first=0, dtype=BF16):
        self.rows, self.cols, self.split, self.axis = rows, cols, split, axis
        self.first, self.dtype = first, dtype
        self.tile = 128 if axis == 1 else (16 if dtype == BF16 else 8)

    def cut(self, index):
        size = self.cols if self.axis == 1 else self.rows
        part = pl.ds(pl.multiple_of(self.first + index * size, self.tile), size)
        if self.axis == 1:
            return pl.ds(0, self.rows), part
        return part, pl.ds(0, self.cols)

    def scratch(self):
        ways = 2 if self.split else 1
        vmem = lambda *lead: pltpu.VMEM(lead + (self.rows, self.cols), self.dtype)
        late = vmem(4, 2) if self.split else vmem(1, 1)
        return [vmem(ways, 4, 2), vmem(ways, 4, 2), late, vmem(4), vmem(5), vmem()]

    def copies(self):
        return (2 if self.split else 1) + 1 + 1 + 4 + 3


class Reduction:
    def __init__(self, slab, source, target, scratch, plan, own, own_at):
        self.slab, self.source, self.target, self.plan = slab, source, target, plan
        self.held, self.from_c, self.from_y, self.from_x, self.from_z, self.done = scratch
        self.own, self.own_at = own, own_at
        z, x, y, c = place()
        self.at = z, x, y, c
        self.slot = y if slab.split else 0
        side = (z, x, y, 1 - c)
        over = (z, x, 1 - y, c)

        def index_of(half, core):
            return half * 2 + core if slab.split else core

        def cut_all(ref, index):
            rows, cols = slab.cut(index)
            return ref.at[:, :, rows, cols]

        def cut_out(index):
            rows, cols = slab.cut(index)
            return target.at[rows, cols]

        ways = 2 if slab.split else 1
        self.loads = [
            lambda half=half: pltpu.make_async_copy(
                cut_all(source, index_of(half, c)), self.held.at[half], own.at[own_at + half]
            )
            for half in range(ways)
        ]
        self.to_core = [
            plan.add(
                lambda half=half: (
                    cut_all(source, index_of(half, 1 - c)), self.from_c.at[half], side,
                )
            )
            for half in range(ways)
        ]
        if slab.split:
            self.to_y = plan.add(lambda: (self.held.at[1 - y], self.from_y, over))
        else:
            self.to_y = plan.add(lambda: (self.done, self.from_y.at[0, 0], over))
        self.to_x = plan.add(
            lambda: (self.held.at[self.slot, :, 1 - x], self.from_x, (z, 1 - x, y, c))
        )
        self.middle, outer, _ = z_line()
        self.outer = outer
        self.inward = 2 - z // 2 * 2
        to_outer, to_inner = (outer, x, y, c), (3 - z, x, y, c)
        owned_by = lambda at: self.held.at[self.slot, at, x]
        beyond = lambda: self.held.at[self.slot, pl.ds(self.inward, 2), x]
        self.out_in = plan.add(lambda: (beyond(), self.from_z.at[pl.ds(0, 2)], to_outer))
        self.out_near = plan.add(lambda: (owned_by(outer), self.from_z.at[2], to_outer))
        self.in_in = plan.add(lambda: (beyond(), self.from_z.at[pl.ds(3, 2)], to_inner))
        self.in_out = plan.add(lambda: (owned_by(outer), self.from_z.at[0], to_outer))
        mine = lambda: cut_out(index_of(y, c))
        self.store = lambda: pltpu.make_async_copy(self.done, mine(), own.at[own_at + 2])
        self.share_core = plan.add(lambda: (self.done, mine(), side))
        if slab.split:
            theirs = lambda: cut_out(index_of(1 - y, c))
            self.share_y = plan.add(lambda: (self.done, mine(), over))
            self.share_far = plan.add(lambda: (theirs(), theirs(), side))

    def begin(self):
        for load in self.loads:
            load().start()
        for index in self.to_core:
            self.plan.start(index)

    def summed(self, total, *others):
        value = total[...].astype(F32)
        for other in others:
            value = value + other[...].astype(F32)
        total[...] = value.astype(self.slab.dtype)

    def after_core(self):
        for half, load in enumerate(self.loads):
            load().wait()
            self.plan.arrived(self.to_core[half])

        def step(t, carry):
            for half in range(len(self.loads)):
                self.summed(self.held.at[half, t // 2, t % 2], self.from_c.at[half, t // 2, t % 2])
            return carry

        lax.fori_loop(0, 8, step, 0)
        self.plan.start(self.to_y if self.slab.split else self.to_x)

    def after_y(self):
        if not self.slab.split:
            return
        self.plan.arrived(self.to_y)

        def step(t, carry):
            self.summed(self.held.at[self.slot, t // 2, t % 2], self.from_y.at[t // 2, t % 2])
            return carry

        lax.fori_loop(0, 8, step, 0)
        self.plan.start(self.to_x)

    def after_x(self):
        z, x, y, c = self.at
        self.plan.arrived(self.to_x)

        def step(t, carry):
            self.summed(self.held.at[self.slot, t, x], self.from_x.at[t])
            return carry

        lax.fori_loop(0, 4, step, 0)

        @pl.when(self.middle == 0)
        def _():
            self.plan.start(self.out_in)
            self.plan.start(self.out_near)

    def after_a(self):
        @pl.when(self.middle == 1)
        def _():
            self.plan.arrived(self.out_in)
            for at in range(2):
                total = self.held.at[self.slot, self.inward + at, self.at[1]]
                self.summed(total, self.from_z.at[at])
            self.plan.start(self.in_in)

    def after_b(self):
        @pl.when(self.middle == 1)
        def _():
            self.plan.arrived(self.in_in)
            at = 3 + self.outer - (2 - self.inward)
            total = self.held.at[self.slot, self.outer, self.at[1]]
            self.summed(total, self.from_z.at[at])
            self.plan.start(self.in_out)

    def after_z(self):
        z, x, y, c = self.at

        @pl.when(self.middle == 1)
        def _():
            self.plan.arrived(self.out_near)
            value = self.held[self.slot, z, x].astype(F32) + self.from_z[2].astype(F32)
            value = value + self.from_z[3 + z - (2 - self.inward)].astype(F32)
            self.done[...] = value.astype(self.slab.dtype)

        @pl.when(self.middle == 0)
        def _():
            self.plan.arrived(self.in_out)
            value = self.held[self.slot, z, x].astype(F32) + self.from_z[0].astype(F32)
            self.done[...] = value.astype(self.slab.dtype)

        if self.slab.split:
            self.plan.start(self.share_y)
            self.plan.start(self.share_core)
            self.store().start()
        else:
            self.plan.start(self.to_y)

    def after_final(self):
        if self.slab.split:
            self.plan.arrived(self.share_y)
            self.plan.start(self.share_far)
        else:
            self.plan.arrived(self.to_y)
            self.plan.build(self.to_y).wait_send()
            self.summed(self.done, self.from_y.at[0, 0])
            self.plan.start(self.share_core)
            self.store().start()

    def end(self):
        self.plan.arrived(self.share_core)
        if self.slab.split:
            self.plan.arrived(self.share_far)
        self.store().wait()

    def finish_sends(self):
        done_early = () if self.slab.split else (self.to_y,)
        sends = self.to_core + [self.to_y, self.to_x, self.share_core]
        if self.slab.split:
            sends += [self.share_y, self.share_far]
        for index in sends:
            if index not in done_early:
                self.plan.build(index).wait_send()

        @pl.when(self.middle == 1)
        def _():
            self.plan.build(self.in_in).wait_send()
            self.plan.build(self.in_out).wait_send()

        @pl.when(self.middle == 0)
        def _():
            self.plan.build(self.out_in).wait_send()
            self.plan.build(self.out_near).wait_send()


SLABS = {
    "down_y": (1, Slab(64, D, True, 0)),
    "up_low": (0, Slab(96, D, False, 1)),
    "down": (1, Slab(64, D, False, 0, first=256)),
    "up_high": (0, Slab(96, D, False, 1, first=2 * D)),
    "out": (3, Slab(96, D // 2, False, 1)),
    "v": (2, Slab(96, D // 2, False, 1, first=2 * D)),
    "k": (2, Slab(96, D // 2, False, 1, first=D)),
    "q": (2, Slab(96, D // 2, False, 1)),
}


def attend_back(live, acts, mixed_ref, logs_ref, do_ref, d_ref, vec_ref, t, h, base, cols):
    masks = head_masks(BF16)
    rows_all = pl.ds(base, LEN)
    keys = acts[rows_all, cols[1]]
    values = acts[rows_all, cols[2]]
    query = acts[rows_all, cols[0]] * jnp.asarray(HD ** (-0.5), BF16)
    grad_out = do_ref[rows_all, cols[0]]
    dots = (grad_out.astype(F32) * mixed_ref[rows_all, cols[0]].astype(F32)).T
    rows = 256
    q_masked = [query * m for m in masks]
    g_masked = [grad_out * m for m in masks]
    deltas = [jnp.sum(dots[i * HD : (i + 1) * HD, :], axis=0, keepdims=True) for i in range(2)]
    logs = [logs_ref[t, h, i : i + 1, :] for i in range(2)]
    grad_q = jnp.zeros((LEN, PAIR), F32)
    sum_v = jnp.zeros((1, PAIR), F32)
    for start in range(0, LEN, rows):
        part_k = keys[start : start + rows, :]
        part_v = values[start : start + rows, :]
        key_at = start + lax.broadcasted_iota(jnp.int32, (rows, 1), 0)
        bias = jnp.where(key_at < live, 0.0, NEGATIVE)
        grad_k = jnp.zeros((rows, PAIR), F32)
        grad_v = jnp.zeros((rows, PAIR), F32)
        for head in range(2):
            scores = back_mul(part_k, q_masked[head])
            probs = jnp.exp(scores + bias - logs[head])
            grad_probs = back_mul(part_v, g_masked[head])
            grad_s = (probs * (grad_probs - deltas[head])).astype(BF16)
            grad_v += jnp.dot(probs.astype(BF16), g_masked[head], preferred_element_type=F32)
            grad_k += jnp.dot(grad_s, q_masked[head], preferred_element_type=F32)
            grad_q += inner(grad_s, part_k * masks[head])
        d_ref[pl.ds(base + start, rows), cols[1]] = grad_k.astype(BF16)
        d_ref[pl.ds(base + start, rows), cols[2]] = grad_v.astype(BF16)
        sum_v += jnp.sum(grad_v, axis=0, keepdims=True)
    grad_q = grad_q * HD ** (-0.5)
    d_ref[rows_all, cols[0]] = grad_q.astype(BF16)
    vec_ref[0:1, cols[0]] += jnp.sum(grad_q, axis=0, keepdims=True)
    vec_ref[1:2, cols[0]] += sum_v


N_LOADS = 7


def reduce_kernel(
    len_ref, acts_in, mixed_in, do_in, logs_in, x_in, w_in, one_in, y_in, vec_in,
    up_in, down_in, out_in,
    gin_out, y_out, up_out, down_out, qkv_out, out_out, vec_out,
    acts, mixed, do, logs, x_all, w_all, one, x_turned, d, gw, gin, vec, vec_from, *rest,
):
    scratch, (send, recv, own) = rest[:-3], rest[-3:]
    z, x, y, c = place()
    blk = y * 2 + c
    loads = [
        lambda at=at, src=src, dst=dst: pltpu.make_async_copy(src, dst, own.at[at])
        for at, (src, dst) in enumerate(
            (
                (acts_in, acts), (mixed_in, mixed), (do_in, do), (logs_in, logs),
                (x_in, x_all), (w_in, w_all), (one_in, one),
            )
        )
    ]
    for load in loads:
        load().start()
    greet(all_peers())
    plan = Plan(send, recv)
    share, span = gin_out.shape[0] // 4, gin_out.shape[1]
    sources, targets = (up_in, down_in, gw, out_in), (up_out, down_out, qkv_out, out_out)
    works = {}
    for at, (name, (number, slab)) in enumerate(SLABS.items()):
        part = scratch[6 * at : 6 * at + 6]
        works[name] = Reduction(
            slab, sources[number], targets[number], part, plan, own, N_LOADS + 2 + 3 * at
        )
    mine = pl.ds(blk * share, share)
    slot = pl.ds(pl.multiple_of(blk * span, span), span)
    kept = [
        lambda at=at, src=src, dst=dst: pltpu.make_async_copy(
            src.at[:, slot, :], dst.at[mine], own.at[N_LOADS + at]
        )
        for at, (src, dst) in enumerate(((gin, gin_out), (y_in, y_out)))
    ]

    def trade(src, dst):
        made = []
        for other in ((z, x, 1 - y, c), (z, x, 1 - y, 1 - c), (z, x, y, 1 - c)):
            their = other[2] * 2 + other[3]
            made.append(
                plan.add(
                    lambda their=their, other=other: (
                        src.at[:, pl.ds(pl.multiple_of(their * span, span), span), :],
                        dst.at[mine],
                        other,
                    )
                )
            )
        return made

    trade_g, trade_y = trade(gin, gin_out), trade(y_in, y_out)
    ways = [(z, x, y, 1 - c), (z, x, 1 - y, c), (z, 1 - x, y, c)]
    ways += [((z + j) % 4, x, y, c) for j in range(1, 4)]
    vec_sends = [
        plan.add(lambda at=at, to=to: (vec.at[min(at, 3)], vec_from.at[at], to))
        for at, to in enumerate(ways)
    ]

    def vec_task(at):
        if at == 0:
            plan.start(vec_sends[0])
            return
        plan.arrived(vec_sends[at - 1])
        vec[at] = vec[at - 1] + vec_from[at - 1]
        for index in vec_sends[at:] if at == 3 else vec_sends[at : at + 1]:
            plan.start(index)

    def vec_end():
        for index in vec_sends[3:]:
            plan.arrived(index)
        vec_out[...] = vec[3] + vec_from[3] + vec_from[4] + vec_from[5]

    def do_tasks(todo):
        for entry in todo:
            if entry[0] == "vec":
                vec_task(entry[1])
            elif entry[0] == "trade":
                for index in trade_y:
                    plan.start(index)
            else:
                getattr(works[entry[0]], entry[1])()

    vec[0] = vec_in[...]
    for name in ("down_y", "up_low", "down", "up_high", "out"):
        works[name].begin()
    kept[1]().start()
    for load in loads[:4]:
        load().wait()

    def step(s, carry):
        for when, todo in DURING.items():

            @pl.when(s == when)
            def _(todo=todo):
                do_tasks(todo)

        t, h = s // (STEPS // share), s % (STEPS // share)
        base = pl.multiple_of(t * LEN, LEN)
        cols = [pl.ds(pl.multiple_of(part * D + h * PAIR, PAIR), PAIR) for part in range(3)]
        attend_back(len_ref[t], acts, mixed, logs, do, d, vec.at[0], t, h, base, cols)
        return carry

    lax.fori_loop(0, STEPS, step, 0)
    do_tasks(AFTER["attention"])
    loads[4]().wait()
    rows = share * LEN
    x_turned[...] = x_all[...].T
    tile = 256
    for part, name in ((2, "v"), (1, "k"), (0, "q")):

        def grad_tile(i, carry, part=part):
            cols = pl.ds(pl.multiple_of(part * D + i * tile, tile), tile)
            value = jnp.dot(x_turned[...], d[:, cols], preferred_element_type=F32)
            gw[:, :, :, cols] = value.astype(BF16).reshape(4, 2, D // 8, tile)
            return carry

        lax.fori_loop(0, D // tile, grad_tile, 0)
        works[name].begin()
        do_tasks(AFTER[name])
    loads[5]().wait()
    loads[6]().wait()

    for i in range(D // tile):
        value = back_mul(d[...], w_all[pl.ds(i * tile, tile), :])
        value = value + one[:, i * tile : (i + 1) * tile]
        gin[:, :, i * tile : (i + 1) * tile] = value.astype(BF16).reshape(share, LEN, tile)
        do_tasks(AFTER[i])
    for index in trade_g:
        plan.start(index)
    kept[0]().start()
    do_tasks(AFTER["end"])
    vec_end()
    for work in works.values():
        work.end()
    for index in trade_g + trade_y:
        plan.arrived(index)
    for work in works.values():
        work.finish_sends()
    for index in trade_g + trade_y + vec_sends:
        plan.build(index).wait_send()
    for made in kept:
        made().wait()


DURING = {
    0: [("down_y", "after_core")],
    1: [("up_low", "after_core"), ("trade",)],
    2: [("down", "after_core")],
    3: [("up_high", "after_core")],
    4: [("out", "after_core")],
    8: [("up_low", "after_x")],
    9: [("down_y", "after_y")],
    11: [("down", "after_x")],
}
AFTER = {
    "attention": [("vec", 0), ("up_low", "after_a")],
    "v": [("vec", 1)],
    "k": [("v", "after_core"), ("vec", 2)],
    "q": [("k", "after_core"), ("vec", 3), ("up_low", "after_b"), ("down", "after_a")],
    0: [("q", "after_core")],
    1: [("up_high", "after_x")],
    2: [("up_low", "after_z"), ("down", "after_b")],
    "end": [
        ("out", "after_x"),
        ("down", "after_z"),
        ("up_high", "after_a"),
        ("out", "after_a"),
        ("down_y", "after_x"),
        ("up_high", "after_b"),
        ("out", "after_b"),
        ("down_y", "after_a"),
        ("v", "after_x"),
        ("up_high", "after_z"),
        ("out", "after_z"),
        ("down_y", "after_b"),
        ("v", "after_a"),
        ("k", "after_x"),
        ("down_y", "after_z"),
        ("v", "after_b"),
        ("k", "after_a"),
        ("q", "after_x"),
        ("v", "after_z"),
        ("k", "after_b"),
        ("q", "after_a"),
        ("k", "after_z"),
        ("q", "after_b"),
        ("up_low", "after_final"),
        ("down", "after_final"),
        ("up_high", "after_final"),
        ("out", "after_final"),
        ("down_y", "after_final"),
        ("q", "after_z"),
        ("v", "after_final"),
        ("k", "after_final"),
        ("q", "after_final"),
    ],
}


def reduce_all(lengths, acts, mixed, do, logs, rows, whole, one, result, vec, up, down, out):
    share, length = result.shape[:2]
    vmem = pl.BlockSpec(memory_space=pltpu.VMEM)
    hbm = pl.BlockSpec(memory_space=pl.ANY)
    shape = lambda a: jax.ShapeDtypeStruct(a.shape[2:], a.dtype)
    back = jax.ShapeDtypeStruct((share * 4, length // 4, D), BF16)
    scratch = [s for _, slab in SLABS.values() for s in slab.scratch()]
    wires = 12 + sum(slab.copies() for _, slab in SLABS.values())
    like = lambda a: pltpu.VMEM(a.shape, a.dtype)
    return pl.pallas_call(
        reduce_kernel,
        in_specs=[pl.BlockSpec(memory_space=pltpu.SMEM)] + [hbm] * 7 + [vmem] * 2 + [hbm] * 3,
        out_specs=[hbm] * 6 + [vmem],
        out_shape=[
            back, back, shape(up), shape(down),
            jax.ShapeDtypeStruct((D // 8, 3 * D), BF16),
            shape(out),
            jax.ShapeDtypeStruct((16, D), F32),
        ],
        scratch_shapes=[like(a) for a in (acts, mixed, do, logs, rows, whole, one)]
        + [
            pltpu.VMEM(rows.shape[::-1], BF16),
            pltpu.VMEM(acts.shape, BF16),
            pltpu.VMEM((4, 2, D // 8, 3 * D), BF16),
            pltpu.VMEM((share, length, D), BF16),
            pltpu.VMEM((4, 16, D), F32),
            pltpu.VMEM((6, 16, D), F32),
        ]
        + scratch
        + [
            pltpu.SemaphoreType.DMA((wires,)),
            pltpu.SemaphoreType.DMA((wires,)),
            pltpu.SemaphoreType.DMA((N_LOADS + 2 + 3 * len(SLABS),)),
        ],
        compiler_params=pltpu.CompilerParams(
            collective_id=1, has_side_effects=True, vmem_limit_bytes=VMEM_ALL
        ),
        name="attend_reduce",
    )(lengths, acts, mixed, do, logs, rows, whole, one, result, vec, up, down, out)


def local(*args):
    tables, lengths, cotangent, step_count = args[:4]
    masters, firsts, seconds = args[4:9], args[9:14], args[14:19]
    w_qkv, w_out, w_up, w_down, vectors = masters
    blocks = lax.axis_size("blk")
    shards = lax.axis_size("tab")
    table_count, local_len = tables.shape[:2]
    share = table_count // blocks
    tuned = shards == 8 and blocks == 4
    owned = vectors.shape[0]
    vec_own = jnp.pad(vectors.astype(BF16).T, ((0, 4), (0, 0)))
    my_lengths = lax.dynamic_slice(lengths, (lax.axis_index("blk") * share,), (share,))
    if tuned:
        at_own = (0, lax.axis_index("tab") * owned)
        vec_wide = lax.dynamic_update_slice(jnp.zeros((16, D), BF16), vec_own, at_own)
        mine, cot, *wholes, qkv, mixed, logs = gather_all(
            my_lengths, tables, cotangent, w_qkv, w_out, w_up, w_down, vec_wide[None]
        )
        vec_f = jnp.sum(wholes[4].astype(F32), axis=0)[:12]
    else:
        spread = partial(lax.all_to_all, axis_name="blk", split_axis=0, concat_axis=1, tiled=True)
        mine, cot = spread(tables), spread(cotangent)
        narrow = [w.astype(BF16) for w in (w_qkv, w_out, w_up, w_down)]
        wholes = [lax.all_gather(w, "tab", axis=0) for w in narrow + [vec_own]]
        vec_f = wholes[4][:, :12].transpose(1, 0, 2).reshape(12, D).astype(F32)
    full_qkv, full_out, full_up, full_down = [
        w.reshape(-1, w.shape[-1]) for w in wholes[:4]
    ]
    bias_up = vec_f[8:12].reshape(-1)
    rows = mine.reshape(-1, D)
    if not tuned:
        bias_qkv = jnp.concatenate([vec_f[0], jnp.zeros((D,), F32), vec_f[1]])
        qkv = (jnp.dot(rows, full_qkv, preferred_element_type=F32) + bias_qkv).astype(BF16)
        mixed, logs = attention_forward(my_lengths, qkv, share)
    attn_out = jnp.dot(mixed, full_out, preferred_element_type=F32) + vec_f[2]
    normed_one, norm_one_back = jax.vjp(
        layer_norm, rows.astype(F32) + attn_out, vec_f[4], vec_f[5]
    )
    normed_b = normed_one.astype(BF16)
    hidden = jnp.dot(normed_b, full_up, preferred_element_type=F32) + bias_up
    below = 0.5 * (1.0 + lax.erf(hidden * 0.5**0.5))
    active_b = (hidden * below).astype(BF16)
    slope = below + hidden * jnp.exp(-0.5 * hidden * hidden) * (2.0 * math.pi) ** -0.5
    active_b, slope = lax.optimization_barrier((active_b, slope.astype(BF16)))
    branch = jnp.dot(active_b, full_down, preferred_element_type=F32) + vec_f[3]
    result, norm_two_back = jax.vjp(layer_norm, normed_one + branch, vec_f[6], vec_f[7])
    result = result.astype(BF16).reshape(mine.shape)
    grad_two, grad_g2, grad_c2 = norm_two_back(cot.reshape(-1, D).astype(F32))
    grad_b2 = jnp.sum(grad_two, axis=0)
    branch_b = grad_two.astype(BF16)
    gw_down = inner(active_b, branch_b).astype(BF16)
    grad_hidden = back_mul(branch_b, full_down) * slope.astype(F32)
    grad_b1 = jnp.sum(grad_hidden, axis=0)
    hidden_b = grad_hidden.astype(BF16)
    gw_up = inner(normed_b, hidden_b).astype(BF16)
    grad_one, grad_g1, grad_c1 = norm_one_back(grad_two + back_mul(hidden_b, full_up))
    grad_bo = jnp.sum(grad_one, axis=0)
    attn_b = grad_one.astype(BF16)
    gw_out = inner(mixed, attn_b).astype(BF16)
    grad_mixed = back_mul(attn_b, full_out).astype(BF16)
    norm_rows = [grad_bo, grad_b2, grad_g1, grad_c1, grad_g2, grad_c2]
    if tuned:
        empty = jnp.zeros((2, D), F32)
        wide_vec = jnp.concatenate(
            [empty, jnp.stack(norm_rows), grad_b1.reshape(4, D), empty, empty]
        )
        by_owner = lambda g: g.reshape(4, 2, -1, g.shape[-1])
        grad_input, output, *sums = reduce_all(
            my_lengths, qkv, mixed, grad_mixed, logs, rows, full_qkv, grad_one, result,
            wide_vec, by_owner(gw_up), by_owner(gw_down), by_owner(gw_out),
        )
        at_own = (0, lax.axis_index("tab") * owned)
        sum_vec = lax.dynamic_slice(sums[4], at_own, (16, owned))[:12].T
        shares = [s.astype(F32) for s in (sums[2], sums[3], sums[0], sums[1], sum_vec)]
    else:
        grad_three, sums = attention_backward(my_lengths, qkv, mixed, logs, grad_mixed, share)
        sums = jnp.sum(sums[:, :, :2], axis=0)
        grad_bq, grad_bv = sums[:, 0].reshape(-1), sums[:, 1].reshape(-1)
        grad_qkv = jnp.concatenate([grad_three[i] for i in range(3)], axis=1)
        gw_qkv = inner(rows, grad_qkv).astype(BF16)
        grad_in = grad_one + back_mul(grad_qkv, full_qkv)
        grad_in = grad_in.astype(BF16).reshape(mine.shape)
        gw_vec = jnp.concatenate(
            [jnp.stack([grad_bq, grad_bv] + norm_rows), grad_b1.reshape(4, D)]
        )
        back = partial(lax.all_to_all, axis_name="blk", split_axis=1, concat_axis=0, tiled=True)
        grad_input, output = back(grad_in), back(result)

        def collect(grad):
            part = lax.psum_scatter(
                grad.reshape(shards, -1, grad.shape[-1]), "tab", scatter_dimension=0
            )
            return lax.psum(part.astype(BF16), "blk").astype(F32)

        shares = [collect(g) for g in (gw_qkv, gw_out, gw_up, gw_down)]
        shares.append(collect(gw_vec.T.astype(BF16)))
    grad_input = grad_input.astype(F32)
    step_float = step_count[0].astype(F32)
    results = [output, grad_input]
    for at in range(5):
        results.extend(
            adam(masters[at], shares[at], firsts[at], seconds[at], RATES[at], step_float)
        )
    return tuple(results)


def solution(mesh):
    tokens, flat, rows = P("tab", "blk", None), P("tab"), P("tab", None)
    return jax.shard_map(
        local,
        mesh=mesh,
        in_specs=(tokens, flat, tokens, P()) + (rows,) * 15,
        out_specs=(tokens, tokens) + (rows,) * 20,
        check_vma=False,
    )
```

```python
import math
from functools import partial

import jax
import jax.numpy as jnp
from jax import lax
from jax.experimental import pallas as pl
from jax.experimental.pallas import tpu as pltpu
from jax.sharding import PartitionSpec as P

D = 768
H = 12
HD = 64
LEN = 512
FF = 3072
PAIR = 2 * HD

EPS = 1e-06
NEGATIVE = -1e30
BETA_ONE = 0.9
BETA_TWO = 0.999
ADAM_EPS = 1e-08
DECAY = 0.01
RATES = (1.0, 15.0, 1.0, 0.5, 5.0)

F32 = jnp.float32
BF16 = jnp.bfloat16
MESH_ID = pl.DeviceIdType.MESH
VMEM_ALL = 64 * 1000 * 1024


def layer_norm(hidden, gain_vec, shift_vec):
    row_mean = jnp.mean(hidden, axis=-1, keepdims=True)
    centred = hidden - row_mean
    variance = jnp.mean(centred * centred, axis=-1, keepdims=True)
    return centred * lax.rsqrt(variance + EPS) * gain_vec + shift_vec


def inner(left, right):
    return lax.dot_general(left, right, (((0,), (0,)), ((), ())), preferred_element_type=F32)


def back_mul(left, right):
    return lax.dot_general(left, right, (((1,), (1,)), ((), ())), preferred_element_type=F32)


def adam(master, gradient, first_moment, second_moment, rate_now, step_float):
    moment_new = BETA_ONE * first_moment + (1.0 - BETA_ONE) * gradient
    square_new = BETA_TWO * second_moment + (1.0 - BETA_TWO) * gradient * gradient
    fix_one = 1.0 - jnp.power(BETA_ONE, step_float)
    fix_two = 1.0 - jnp.power(BETA_TWO, step_float)
    update = moment_new / fix_one / (jnp.sqrt(square_new / fix_two) + ADAM_EPS)
    master_new = master - rate_now * (update + DECAY * master)
    return (moment_new, square_new, master_new, master_new.astype(BF16))


def head_masks(dtype):
    lane = lax.broadcasted_iota(jnp.int32, (1, PAIR), 1)
    return [(lane < HD).astype(dtype), (lane >= HD).astype(dtype)]


def attn_fwd_kernel(len_ref, q_ref, k_ref, v_ref, o_ref, l_ref):
    live = len_ref[pl.program_id(0)]
    masks = head_masks(BF16)
    keys = k_ref[...]
    values = v_ref[...]
    rows = 256
    key_at = lax.broadcasted_iota(jnp.int32, (1, LEN), 1)
    bias = jnp.where(key_at < live, 0.0, NEGATIVE)
    lane = lax.broadcasted_iota(jnp.int32, (1, PAIR), 1)
    for start in range(0, LEN, rows):
        query = q_ref[pl.ds(start, rows), :] * jnp.asarray(HD ** (-0.5), BF16)
        mixed, logs = [], []
        for head in range(2):
            scores = back_mul(query * masks[head], keys) + bias
            top = jnp.max(scores, axis=-1, keepdims=True)
            raised = jnp.exp(scores - top)
            total = jnp.sum(raised, axis=-1, keepdims=True)
            probs = (raised * (1.0 / total)).astype(BF16)
            mixed.append(jnp.dot(probs, values, preferred_element_type=F32))
            logs.append(top + jnp.log(total))
        o_ref[pl.ds(start, rows), :] = jnp.where(lane < HD, mixed[0], mixed[1]).astype(BF16)
        both = jnp.where(lane < HD, logs[0], logs[1])
        flat = both.T
        l_ref[0, 0, 0:1, pl.ds(start, rows)] = flat[0:1, :]
        l_ref[0, 0, 1:2, pl.ds(start, rows)] = flat[HD : HD + 1, :]


def attention_forward(lengths, qkv, tables):
    pairs = H // 2
    spec = lambda part: pl.BlockSpec((LEN, PAIR), lambda t, h, n: (t, part * pairs + h))
    return pl.pallas_call(
        attn_fwd_kernel,
        grid_spec=pltpu.PrefetchScalarGridSpec(
            num_scalar_prefetch=1,
            grid=(tables, pairs),
            in_specs=[spec(0), spec(1), spec(2)],
            out_specs=[
                pl.BlockSpec((LEN, PAIR), lambda t, h, n: (t, h)),
                pl.BlockSpec((1, 1, 8, LEN), lambda t, h, n: (t, h, 0, 0)),
            ],
        ),
        out_shape=[
            jax.ShapeDtypeStruct((tables * LEN, D), BF16),
            jax.ShapeDtypeStruct((tables, pairs, 8, LEN), F32),
        ],
        name="attn_fwd",
    )(lengths, qkv, qkv, qkv)


def attn_bwd_kernel(len_ref, q_ref, k_ref, v_ref, o_ref, l_ref, do_ref, d_ref, sums_ref):
    live = len_ref[pl.program_id(0)]
    masks = head_masks(BF16)
    keys = k_ref[...]
    values = v_ref[...]
    query = q_ref[...] * jnp.asarray(HD ** (-0.5), BF16)
    grad_out = do_ref[...]
    dots = (grad_out.astype(F32) * o_ref[...].astype(F32)).T
    rows = 256
    q_masked = [query * m for m in masks]
    g_masked = [grad_out * m for m in masks]
    deltas = [jnp.sum(dots[h * HD : (h + 1) * HD, :], axis=0, keepdims=True) for h in range(2)]
    logs = [l_ref[0, 0, h : h + 1, :] for h in range(2)]
    grad_q = jnp.zeros((LEN, PAIR), F32)
    sum_v = jnp.zeros((1, PAIR), F32)
    for start in range(0, LEN, rows):
        part_k = keys[start : start + rows, :]
        part_v = values[start : start + rows, :]
        key_at = start + lax.broadcasted_iota(jnp.int32, (rows, 1), 0)
        bias = jnp.where(key_at < live, 0.0, NEGATIVE)
        grad_k = jnp.zeros((rows, PAIR), F32)
        grad_v = jnp.zeros((rows, PAIR), F32)
        for head in range(2):
            scores = back_mul(part_k, q_masked[head])
            probs = jnp.exp(scores + bias - logs[head])
            grad_probs = back_mul(part_v, g_masked[head])
            grad_s = (probs * (grad_probs - deltas[head])).astype(BF16)
            grad_v += jnp.dot(probs.astype(BF16), g_masked[head], preferred_element_type=F32)
            grad_k += jnp.dot(grad_s, q_masked[head], preferred_element_type=F32)
            grad_q += inner(grad_s, part_k * masks[head])
        d_ref[1, pl.ds(start, rows), :] = grad_k.astype(BF16)
        d_ref[2, pl.ds(start, rows), :] = grad_v.astype(BF16)
        sum_v += jnp.sum(grad_v, axis=0, keepdims=True)
    grad_q = grad_q * HD ** (-0.5)
    d_ref[0, :, :] = grad_q.astype(BF16)
    sums_ref[0, 0, 0:1, :] = jnp.sum(grad_q, axis=0, keepdims=True)
    sums_ref[0, 0, 1:2, :] = sum_v


def attention_backward(lengths, qkv, mixed, logs, grad_mixed, tables):
    pairs = H // 2
    spec = lambda part: pl.BlockSpec((LEN, PAIR), lambda t, h, n: (t, part * pairs + h))
    block = pl.BlockSpec((LEN, PAIR), lambda t, h, n: (t, h))
    return pl.pallas_call(
        attn_bwd_kernel,
        grid_spec=pltpu.PrefetchScalarGridSpec(
            num_scalar_prefetch=1,
            grid=(tables, pairs),
            in_specs=[
                spec(0),
                spec(1),
                spec(2),
                block,
                pl.BlockSpec((1, 1, 8, LEN), lambda t, h, n: (t, h, 0, 0)),
                block,
            ],
            out_specs=[
                pl.BlockSpec((3, LEN, PAIR), lambda t, h, n: (0, t, h)),
                pl.BlockSpec((1, 1, 8, PAIR), lambda t, h, n: (t, h, 0, 0)),
            ],
        ),
        out_shape=[
            jax.ShapeDtypeStruct((3, tables * LEN, D), BF16),
            jax.ShapeDtypeStruct((tables, pairs, 8, PAIR), F32),
        ],
        name="attn_bwd",
    )(lengths, qkv, qkv, qkv, mixed, logs, grad_mixed)


def place():
    tab, blk = lax.axis_index("tab"), lax.axis_index("blk")
    return tab // 2, tab % 2, blk // 2, blk % 2


def z_line():
    z = place()[0]
    inner = (z + 1) // 2 % 2
    near = inner * (z - 1) * 3 + (1 - inner) * (1 + z // 3)
    second = inner * (3 - z) + (1 - inner) * (3 - near)
    third = inner * (3 - near) + (1 - inner) * (3 - z)
    return inner, near, (near, second, third)


def greet(peers):
    barrier = pltpu.get_barrier_semaphore()
    for z, x, y, c in peers:
        pl.semaphore_signal(
            barrier, inc=1, device_id=(z * 2 + x, y * 2 + c), device_id_type=MESH_ID
        )
    pl.semaphore_wait(barrier, len(peers))


def all_peers():
    z, x, y, c = place()
    z_peers = [((z + j) % 4, x, y, c) for j in range(1, 4)]
    rest = [(z, 1 - x, y, c), (z, x, 1 - y, c), (z, x, y, 1 - c), (z, x, 1 - y, 1 - c)]
    return z_peers + rest


def by_columns(width):
    return lambda ref, t, part: ref.at[t, :, pl.ds(pl.multiple_of(part * width, 128), width)]


def by_rows(height):
    return lambda ref, t, part: ref.at[t, pl.ds(pl.multiple_of(part * height, 16), height), :]


PIECES = (
    (by_columns(3 * D // 2), False),
    (by_columns(D // 2), False),
    (by_columns(FF // 4), True),
    (by_rows(FF // 16), False),
)
G_WIRES = 96
STEPS = 12


class Gather:
    def __init__(self, at, shard, whole, plan):
        piece, self.split = PIECES[at]
        z, x, y, c = place()
        tab = z * 2 + x
        part = y * 2 + c if self.split else c
        other = (1 - y) * 2 + c
        own = lambda: piece(shard, 0, part)
        self.plan = plan
        self.middle, outer, order = z_line()
        near = lambda j: order[j - 1] * 2 + x
        far = lambda j: order[j - 1] * 2 + 1 - x if j else z * 2 + 1 - x

        def send(at_tab, which, to, first=False, inner=False):
            return plan.add(
                lambda: (
                    own() if first else piece(whole, at_tab, which),
                    piece(whole, at_tab, which),
                    to,
                ),
                inner,
            )

        side, over, across = (z, x, y, 1 - c), (z, x, 1 - y, c), (z, 1 - x, y, c)
        to_outer, to_inner = (outer, x, y, c), (3 - z, x, y, c)
        self.own_near = send(tab, part, to_outer, True)
        self.own_inner = send(tab, part, to_inner, True, inner=True)
        self.passed = [
            send(near(j), part, to_inner if j == 1 else to_outer, inner=True) for j in range(1, 4)
        ]
        self.x = [send(tab, part, across, True)]
        self.x += [send(near(j), part, across) for j in range(1, 4)]
        tabs = [near(j) for j in range(1, 4)] + [far(j) for j in range(4)]
        self.c = [send(t, part, side) for t in tabs]
        self.y = [send(t, part, over) for t in tabs] if self.split else []
        self.late = [send(t, other, side) for t in tabs] if self.split else []

    def send_z(self):
        self.plan.start(self.own_near)

        @pl.when(self.middle == 1)
        def _():
            self.plan.start(self.own_inner)

    def send_x(self):
        self.plan.start(self.x[0])

    def onward(self, at):
        if self.split:
            self.plan.start(self.y[at])
        self.plan.start(self.c[at])

    def task_z(self, j):
        if j == 1:
            self.plan.arrived(self.own_near)
        else:

            @pl.when(self.middle == 0)
            def _():
                self.plan.arrived(self.passed[j - 1])

        @pl.when(self.middle == 1)
        def _():
            if j > 1:
                self.plan.arrived(self.own_inner if j == 2 else self.passed[0])
            self.plan.start(self.passed[j - 1])

        self.plan.start(self.x[j])
        self.onward(j - 1)

    def task_x(self, j):
        self.plan.arrived(self.x[j])
        self.onward(3 + j)

    def task_y(self, at):
        self.plan.arrived(self.y[at])
        self.plan.start(self.late[at])

    def end(self):
        for index in self.c + self.late:
            self.plan.arrived(index)


def gather_kernel(
    len_ref, x_in, cot_in, qkv_wide, out_wide, up_wide, down_wide, vec_in,
    x_out, cot_out, qkv_out, out_out, up_out, down_out, vec_out, acts_out, mixed_out, logs_out,
    qkv_in, out_in, up_in, down_in, x_all, w_all, vec_all, acts, mixed, logs, bias,
    send, recv, own,
):
    z, x, y, c = place()
    tab, blk = z * 2 + x, y * 2 + c
    share, span = x_in.shape[0] // 4, x_in.shape[1]
    mine = pl.ds(blk * share, share)
    slot = pl.ds(pl.multiple_of(blk * span, span), span)
    plan = Plan(send, recv)
    shards = (qkv_in, out_in, up_in, down_in)
    wholes = (w_all, out_out, up_out, down_out)
    works = [Gather(at, shards[at], wholes[at], plan) for at in range(4)]
    qkv, out, up, down = works

    def trade(src, dst):
        made = []
        for other in ((z, x, 1 - y, c), (z, x, 1 - y, 1 - c), (z, x, y, 1 - c)):
            their = other[2] * 2 + other[3]
            made.append(
                plan.add(
                    lambda their=their, other=other: (
                        src.at[pl.ds(their * share, share)], dst.at[:, slot, :], other,
                    )
                )
            )
        return made

    trade_x, trade_cot = trade(x_in, x_all), trade(cot_in, cot_out)
    vec_z = [
        plan.add(lambda j=j: (vec_in.at[0], vec_all.at[tab], ((z + j) % 4, x, y, c)))
        for j in range(1, 4)
    ]
    vec_x = [plan.add(lambda: (vec_in.at[0], vec_all.at[tab], (z, 1 - x, y, c)))]
    for j in range(1, 4):
        t = (z + 4 - j) % 4 * 2 + x
        vec_x.append(plan.add(lambda t=t: (vec_all.at[t], vec_all.at[t], (z, 1 - x, y, c))))
    keeps = [
        lambda: pltpu.make_async_copy(x_in.at[mine], x_all.at[:, slot, :], own.at[0]),
        lambda: pltpu.make_async_copy(qkv_in.at[0], w_all.at[tab], own.at[1]),
        lambda: pltpu.make_async_copy(vec_in.at[0], vec_all.at[tab], own.at[2]),
        lambda: pltpu.make_async_copy(cot_in.at[mine], cot_out.at[:, slot, :], own.at[3]),
        lambda: pltpu.make_async_copy(out_in.at[0], out_out.at[tab], own.at[4]),
        lambda: pltpu.make_async_copy(up_in.at[0], up_out.at[tab], own.at[5]),
        lambda: pltpu.make_async_copy(down_in.at[0], down_out.at[tab], own.at[6]),
    ]
    puts = [
        lambda: pltpu.make_async_copy(x_all, x_out, own.at[7]),
        lambda: pltpu.make_async_copy(w_all, qkv_out, own.at[8]),
        lambda: pltpu.make_async_copy(vec_all, vec_out, own.at[9]),
        lambda: pltpu.make_async_copy(acts, acts_out, own.at[10]),
        lambda: pltpu.make_async_copy(mixed, mixed_out, own.at[11]),
        lambda: pltpu.make_async_copy(logs, logs_out, own.at[12]),
    ]
    for wide, narrow in zip((qkv_wide, out_wide, up_wide, down_wide), shards):

        def rounded(i, carry, wide=wide, narrow=narrow):
            rows = pl.ds(pl.multiple_of(i * 16, 16), 16)
            narrow[0, rows, :] = wide[rows, :].astype(BF16)
            return carry

        lax.fori_loop(0, wide.shape[0] // 16, rounded, 0)
    greet(all_peers())
    for index in vec_z + vec_x[:1]:
        plan.start(index)
    qkv.send_z()
    qkv.send_x()
    for index in trade_x:
        plan.start(index)
    for keep in keeps:
        keep().start()
    for work in (out, up, down):
        work.send_z()
    out.send_x()
    for index in trade_cot:
        plan.start(index)
    for j in range(1, 4):
        plan.arrived(vec_z[j - 1])
        plan.start(vec_x[j])
    for j in range(1, 4):
        qkv.task_z(j)
    up.send_x()
    down.send_x()
    for j in range(4):
        qkv.task_x(j)
    for index in vec_x:
        plan.arrived(index)
    for keep in keeps[:3]:
        keep().wait()
    for index in trade_x:
        plan.arrived(index)
    qkv.end()
    for put in puts[:3]:
        put().start()

    tile = 256
    rows = share * LEN
    spread = [vec_all[t, 0:16, :].astype(F32) for t in range(8)]
    vectors = spread[0]
    for t in range(1, 8):
        vectors = vectors + spread[t]
    bias[:, 0:D] = vectors[0:1, :]
    bias[:, D : 2 * D] = jnp.zeros((1, D), F32)
    bias[:, 2 * D : 3 * D] = vectors[1:2, :]

    def project(i, carry):
        cols = pl.ds(pl.multiple_of(i * tile, tile), tile)
        weight = w_all[:, :, cols].reshape(D, tile)
        value = jnp.dot(x_all[...].reshape(rows, D), weight, preferred_element_type=F32)
        acts[:, cols] = (value + bias[:, cols]).astype(BF16)
        return carry

    lax.fori_loop(0, 3 * D // tile, project, 0)
    puts[3]().start()

    tasks = {
        0: [lambda j=j: out.task_z(j) for j in (1, 2, 3)],
        1: [lambda: up.task_z(1), lambda: up.task_z(2)],
        2: [lambda j=j: out.task_x(j) for j in range(4)] + [lambda: up.task_z(3)],
        3: [lambda: up.task_x(0)],
        4: [lambda: down.task_z(1)],
        5: [lambda: down.task_z(2), lambda: up.task_x(1)],
        6: [lambda: down.task_x(0), lambda: up.task_x(2)],
        7: [lambda: down.task_z(3)],
        8: [lambda: up.task_x(3), lambda: up.task_y(0)],
        9: [lambda: up.task_y(1), lambda: down.task_x(1)],
        10: [lambda: up.task_y(2), lambda: up.task_y(3)],
        11: [lambda: up.task_y(4), lambda: down.task_x(2)],
        12: [lambda: up.task_y(5), lambda: up.task_y(6), lambda: down.task_x(3)],
    }

    def step(s, carry):
        for when, todo in tasks.items():
            if when < STEPS:

                @pl.when(s == when)
                def _(todo=todo):
                    for task in todo:
                        task()

        t, h = s // (STEPS // share), s % (STEPS // share)
        base = pl.multiple_of(t * LEN, LEN)
        cols = [pl.ds(pl.multiple_of(part * D + h * PAIR, PAIR), PAIR) for part in range(3)]
        attend(len_ref[t], acts, mixed, logs, t, h, base, cols)
        return carry

    lax.fori_loop(0, STEPS, step, 0)
    for put in puts[4:]:
        put().start()
    for task in tasks[STEPS]:
        task()
    for index in trade_cot:
        plan.arrived(index)
    for work in (out, up, down):
        work.end()
    plan.finish(z_line()[0])
    for keep in keeps[3:]:
        keep().wait()
    for put in puts:
        put().wait()


def attend(live, acts, mixed_ref, logs_ref, t, h, base, cols):
    masks = head_masks(BF16)
    keys = acts[pl.ds(base, LEN), cols[1]]
    values = acts[pl.ds(base, LEN), cols[2]]
    rows = 256
    key_at = lax.broadcasted_iota(jnp.int32, (1, LEN), 1)
    bias = jnp.where(key_at < live, 0.0, NEGATIVE)
    lane = lax.broadcasted_iota(jnp.int32, (1, PAIR), 1)

    def half(i, carry):
        at = pl.ds(pl.multiple_of(base + i * rows, rows), rows)
        query = acts[at, cols[0]] * jnp.asarray(HD ** (-0.5), BF16)
        mixed, logs = [], []
        for head in range(2):
            scores = back_mul(query * masks[head], keys) + bias
            top = jnp.max(scores, axis=-1, keepdims=True)
            raised = jnp.exp(scores - top)
            total = jnp.sum(raised, axis=-1, keepdims=True)
            probs = (raised * (1.0 / total)).astype(BF16)
            mixed.append(jnp.dot(probs, values, preferred_element_type=F32))
            logs.append(top + jnp.log(total))
        mixed_ref[at, cols[0]] = jnp.where(lane < HD, mixed[0], mixed[1]).astype(BF16)
        flat = jnp.where(lane < HD, logs[0], logs[1]).T
        to = pl.ds(pl.multiple_of(i * rows, rows), rows)
        logs_ref[t, h, 0:1, to] = flat[0:1, :]
        logs_ref[t, h, 1:2, to] = flat[HD : HD + 1, :]
        return carry

    lax.fori_loop(0, LEN // rows, half, 0)


def gather_all(lengths, tables, cotangent, qkv, out, up, down, vec):
    share, span = tables.shape[0] // 4, tables.shape[1] * 4
    vmem = pl.BlockSpec(memory_space=pltpu.VMEM)
    hbm = pl.BlockSpec(memory_space=pl.ANY)
    shape = lambda a: jax.ShapeDtypeStruct((8,) + a.shape[-2:], BF16)
    rows = share * span
    logs = (share, STEPS // share, 8, LEN)
    return pl.pallas_call(
        gather_kernel,
        in_specs=[pl.BlockSpec(memory_space=pltpu.SMEM)] + [vmem] * 7,
        out_specs=[hbm] * 10,
        out_shape=[
            jax.ShapeDtypeStruct((share, span, D), BF16),
            jax.ShapeDtypeStruct((share, span, D), BF16),
            shape(qkv), shape(out), shape(up), shape(down), shape(vec),
            jax.ShapeDtypeStruct((rows, 3 * D), BF16),
            jax.ShapeDtypeStruct((rows, D), BF16),
            jax.ShapeDtypeStruct(logs, F32),
        ],
        scratch_shapes=[
            *[pltpu.VMEM((1,) + w.shape, BF16) for w in (qkv, out, up, down)],
            pltpu.VMEM((share, span, D), BF16),
            pltpu.VMEM((8,) + qkv.shape, BF16),
            pltpu.VMEM((8,) + vec.shape[1:], BF16),
            pltpu.VMEM((rows, 3 * D), BF16),
            pltpu.VMEM((rows, D), BF16),
            pltpu.VMEM(logs, F32),
            pltpu.VMEM((1, 3 * D), F32),
            pltpu.SemaphoreType.DMA((G_WIRES,)),
            pltpu.SemaphoreType.DMA((G_WIRES,)),
            pltpu.SemaphoreType.DMA((13,)),
        ],
        compiler_params=pltpu.CompilerParams(
            collective_id=0, has_side_effects=True, vmem_limit_bytes=VMEM_ALL
        ),
        name="gather_attend",
    )(lengths, tables, cotangent, qkv, out, up, down, vec)


class Plan:
    def __init__(self, send, recv):
        self.send, self.recv, self.makers, self.inner = send, recv, [], []

    def add(self, maker, inner=False):
        self.makers.append(maker)
        if inner:
            self.inner.append(len(self.makers) - 1)
        return len(self.makers) - 1

    def build(self, index):
        src, dst, (z, x, y, c) = self.makers[index]()
        return pltpu.make_async_remote_copy(
            src_ref=src,
            dst_ref=dst,
            send_sem=self.send.at[index],
            recv_sem=self.recv.at[index],
            device_id=(z * 2 + x, y * 2 + c),
            device_id_type=MESH_ID,
        )

    def start(self, index):
        self.build(index).start()

    def arrived(self, index):
        self.build(index).wait_recv()

    def finish(self, inner):
        for index in range(len(self.makers)):
            if index not in self.inner:
                self.build(index).wait_send()

        @pl.when(inner == 1)
        def _():
            for index in self.inner:
                self.build(index).wait_send()


class Slab:
    def __init__(self, rows, cols, split, axis, first=0, dtype=BF16):
        self.rows, self.cols, self.split, self.axis = rows, cols, split, axis
        self.first, self.dtype = first, dtype
        self.tile = 128 if axis == 1 else (16 if dtype == BF16 else 8)

    def cut(self, index):
        size = self.cols if self.axis == 1 else self.rows
        part = pl.ds(pl.multiple_of(self.first + index * size, self.tile), size)
        if self.axis == 1:
            return pl.ds(0, self.rows), part
        return part, pl.ds(0, self.cols)

    def scratch(self):
        ways = 2 if self.split else 1
        vmem = lambda *lead: pltpu.VMEM(lead + (self.rows, self.cols), self.dtype)
        late = vmem(4, 2) if self.split else vmem(1, 1)
        return [vmem(ways, 4, 2), vmem(ways, 4, 2), late, vmem(4), vmem(5), vmem()]

    def copies(self):
        return (2 if self.split else 1) + 1 + 1 + 4 + 3


class Reduction:
    def __init__(self, slab, source, target, scratch, plan, own, own_at):
        self.slab, self.source, self.target, self.plan = slab, source, target, plan
        self.held, self.from_c, self.from_y, self.from_x, self.from_z, self.done = scratch
        self.own, self.own_at = own, own_at
        z, x, y, c = place()
        self.at = z, x, y, c
        self.slot = y if slab.split else 0
        side = (z, x, y, 1 - c)
        over = (z, x, 1 - y, c)

        def index_of(half, core):
            return half * 2 + core if slab.split else core

        def cut_all(ref, index):
            rows, cols = slab.cut(index)
            return ref.at[:, :, rows, cols]

        def cut_out(index):
            rows, cols = slab.cut(index)
            return target.at[rows, cols]

        ways = 2 if slab.split else 1
        self.loads = [
            lambda half=half: pltpu.make_async_copy(
                cut_all(source, index_of(half, c)), self.held.at[half], own.at[own_at + half]
            )
            for half in range(ways)
        ]
        self.to_core = [
            plan.add(
                lambda half=half: (
                    cut_all(source, index_of(half, 1 - c)), self.from_c.at[half], side,
                )
            )
            for half in range(ways)
        ]
        if slab.split:
            self.to_y = plan.add(lambda: (self.held.at[1 - y], self.from_y, over))
        else:
            self.to_y = plan.add(lambda: (self.done, self.from_y.at[0, 0], over))
        self.to_x = plan.add(
            lambda: (self.held.at[self.slot, :, 1 - x], self.from_x, (z, 1 - x, y, c))
        )
        self.middle, outer, _ = z_line()
        self.outer = outer
        self.inward = 2 - z // 2 * 2
        to_outer, to_inner = (outer, x, y, c), (3 - z, x, y, c)
        owned_by = lambda at: self.held.at[self.slot, at, x]
        beyond = lambda: self.held.at[self.slot, pl.ds(self.inward, 2), x]
        self.out_in = plan.add(lambda: (beyond(), self.from_z.at[pl.ds(0, 2)], to_outer))
        self.out_near = plan.add(lambda: (owned_by(outer), self.from_z.at[2], to_outer))
        self.in_in = plan.add(lambda: (beyond(), self.from_z.at[pl.ds(3, 2)], to_inner))
        self.in_out = plan.add(lambda: (owned_by(outer), self.from_z.at[0], to_outer))
        mine = lambda: cut_out(index_of(y, c))
        self.store = lambda: pltpu.make_async_copy(self.done, mine(), own.at[own_at + 2])
        self.share_core = plan.add(lambda: (self.done, mine(), side))
        if slab.split:
            theirs = lambda: cut_out(index_of(1 - y, c))
            self.share_y = plan.add(lambda: (self.done, mine(), over))
            self.share_far = plan.add(lambda: (theirs(), theirs(), side))

    def begin(self):
        for load in self.loads:
            load().start()
        for index in self.to_core:
            self.plan.start(index)

    def summed(self, total, *others, into=None):
        into = total if into is None else into

        def step(i, carry):
            rows = pl.ds(pl.multiple_of(i * 16, 16), 16)
            value = total[rows, :].astype(F32)
            for other in others:
                value = value + other[rows, :].astype(F32)
            into[rows, :] = value.astype(self.slab.dtype)
            return carry

        lax.fori_loop(0, self.slab.rows // 16, step, 0)

    def after_core(self):
        for half, load in enumerate(self.loads):
            load().wait()
            self.plan.arrived(self.to_core[half])

        def step(t, carry):
            for half in range(len(self.loads)):
                self.summed(self.held.at[half, t // 2, t % 2], self.from_c.at[half, t // 2, t % 2])
            return carry

        lax.fori_loop(0, 8, step, 0)
        self.plan.start(self.to_y if self.slab.split else self.to_x)

    def after_y(self):
        if not self.slab.split:
            return
        self.plan.arrived(self.to_y)

        def step(t, carry):
            self.summed(self.held.at[self.slot, t // 2, t % 2], self.from_y.at[t // 2, t % 2])
            return carry

        lax.fori_loop(0, 8, step, 0)
        self.plan.start(self.to_x)

    def after_x(self):
        z, x, y, c = self.at
        self.plan.arrived(self.to_x)

        def step(t, carry):
            self.summed(self.held.at[self.slot, t, x], self.from_x.at[t])
            return carry

        lax.fori_loop(0, 4, step, 0)

        @pl.when(self.middle == 0)
        def _():
            self.plan.start(self.out_in)
            self.plan.start(self.out_near)

    def after_a(self):
        @pl.when(self.middle == 1)
        def _():
            self.plan.arrived(self.out_in)
            for at in range(2):
                total = self.held.at[self.slot, self.inward + at, self.at[1]]
                self.summed(total, self.from_z.at[at])
            self.plan.start(self.in_in)

    def after_b(self):
        @pl.when(self.middle == 1)
        def _():
            self.plan.arrived(self.in_in)
            at = 3 + self.outer - (2 - self.inward)
            total = self.held.at[self.slot, self.outer, self.at[1]]
            self.summed(total, self.from_z.at[at])
            self.plan.start(self.in_out)

    def after_z(self):
        z, x, y, c = self.at

        @pl.when(self.middle == 1)
        def _():
            self.plan.arrived(self.out_near)
            other = self.from_z.at[3 + z - (2 - self.inward)]
            own = self.held.at[self.slot, z, x]
            self.summed(own, self.from_z.at[2], other, into=self.done)

        @pl.when(self.middle == 0)
        def _():
            self.plan.arrived(self.in_out)
            self.summed(self.held.at[self.slot, z, x], self.from_z.at[0], into=self.done)

        if self.slab.split:
            self.plan.start(self.share_y)
            self.plan.start(self.share_core)
            self.store().start()
        else:
            self.plan.start(self.to_y)

    def after_final(self):
        if self.slab.split:
            self.plan.arrived(self.share_y)
            self.plan.start(self.share_far)
        else:
            self.plan.arrived(self.to_y)
            self.plan.build(self.to_y).wait_send()
            self.summed(self.done, self.from_y.at[0, 0])
            self.plan.start(self.share_core)
            self.store().start()

    def end(self):
        self.plan.arrived(self.share_core)
        if self.slab.split:
            self.plan.arrived(self.share_far)
        self.store().wait()

    def finish_sends(self):
        done_early = () if self.slab.split else (self.to_y,)
        sends = self.to_core + [self.to_y, self.to_x, self.share_core]
        if self.slab.split:
            sends += [self.share_y, self.share_far]
        for index in sends:
            if index not in done_early:
                self.plan.build(index).wait_send()

        @pl.when(self.middle == 1)
        def _():
            self.plan.build(self.in_in).wait_send()
            self.plan.build(self.in_out).wait_send()

        @pl.when(self.middle == 0)
        def _():
            self.plan.build(self.out_in).wait_send()
            self.plan.build(self.out_near).wait_send()


SLABS = {
    "down_y": (1, Slab(64, D, True, 0)),
    "up_low": (0, Slab(96, D // 2, True, 1)),
    "down": (1, Slab(64, D, False, 0, first=256)),
    "up_high": (0, Slab(96, D, False, 1, first=2 * D)),
    "out": (3, Slab(96, D // 2, False, 1)),
    "v": (2, Slab(96, D // 2, False, 1, first=2 * D)),
    "k": (2, Slab(96, D // 2, False, 1, first=D)),
    "q": (2, Slab(96, D // 2, False, 1)),
}


def attend_back(live, acts, mixed_ref, logs_ref, do_ref, d_ref, vec_ref, t, h, base, cols):
    masks = head_masks(BF16)
    rows_all = pl.ds(base, LEN)
    keys = acts[rows_all, cols[1]]
    values = acts[rows_all, cols[2]]
    query = acts[rows_all, cols[0]] * jnp.asarray(HD ** (-0.5), BF16)
    grad_out = do_ref[rows_all, cols[0]]
    dots = (grad_out.astype(F32) * mixed_ref[rows_all, cols[0]].astype(F32)).T
    rows = 256
    q_masked = [query * m for m in masks]
    g_masked = [grad_out * m for m in masks]
    deltas = [jnp.sum(dots[i * HD : (i + 1) * HD, :], axis=0, keepdims=True) for i in range(2)]
    logs = [logs_ref[t, h, i : i + 1, :] for i in range(2)]
    grad_q = jnp.zeros((LEN, PAIR), F32)
    sum_v = jnp.zeros((1, PAIR), F32)
    for start in range(0, LEN, rows):
        part_k = keys[start : start + rows, :]
        part_v = values[start : start + rows, :]
        key_at = start + lax.broadcasted_iota(jnp.int32, (rows, 1), 0)
        bias = jnp.where(key_at < live, 0.0, NEGATIVE)
        grad_k = jnp.zeros((rows, PAIR), F32)
        grad_v = jnp.zeros((rows, PAIR), F32)
        for head in range(2):
            scores = back_mul(part_k, q_masked[head])
            probs = jnp.exp(scores + bias - logs[head])
            grad_probs = back_mul(part_v, g_masked[head])
            grad_s = (probs * (grad_probs - deltas[head])).astype(BF16)
            grad_v += jnp.dot(probs.astype(BF16), g_masked[head], preferred_element_type=F32)
            grad_k += jnp.dot(grad_s, q_masked[head], preferred_element_type=F32)
            grad_q += inner(grad_s, part_k * masks[head])
        d_ref[pl.ds(base + start, rows), cols[1]] = grad_k.astype(BF16)
        d_ref[pl.ds(base + start, rows), cols[2]] = grad_v.astype(BF16)
        sum_v += jnp.sum(grad_v, axis=0, keepdims=True)
    grad_q = grad_q * HD ** (-0.5)
    d_ref[rows_all, cols[0]] = grad_q.astype(BF16)
    vec_ref[0:1, cols[0]] += jnp.sum(grad_q, axis=0, keepdims=True)
    vec_ref[1:2, cols[0]] += sum_v


N_LOADS = 7


def reduce_kernel(
    len_ref, acts_in, mixed_in, do_in, logs_in, x_in, w_in, one_in, y_in, vec_in,
    up_in, down_in, out_in,
    gin_out, y_out, up_out, down_out, qkv_out, out_out, vec_out,
    acts, mixed, do, logs, x_all, w_all, one, x_turned, d, gw, gin, vec, vec_from, *rest,
):
    scratch, (send, recv, own) = rest[:-3], rest[-3:]
    z, x, y, c = place()
    blk = y * 2 + c
    loads = [
        lambda at=at, src=src, dst=dst: pltpu.make_async_copy(src, dst, own.at[at])
        for at, (src, dst) in enumerate(
            (
                (acts_in, acts), (mixed_in, mixed), (do_in, do), (logs_in, logs),
                (x_in, x_all), (w_in, w_all), (one_in, one),
            )
        )
    ]
    for load in loads:
        load().start()
    greet(all_peers())
    plan = Plan(send, recv)
    share, span = gin_out.shape[0] // 4, gin_out.shape[1]
    sources, targets = (up_in, down_in, gw, out_in), (up_out, down_out, qkv_out, out_out)
    works = {}
    for at, (name, (number, slab)) in enumerate(SLABS.items()):
        part = scratch[6 * at : 6 * at + 6]
        works[name] = Reduction(
            slab, sources[number], targets[number], part, plan, own, N_LOADS + 2 + 3 * at
        )
    mine = pl.ds(blk * share, share)
    slot = pl.ds(pl.multiple_of(blk * span, span), span)
    kept = [
        lambda at=at, src=src, dst=dst: pltpu.make_async_copy(
            src.at[:, slot, :], dst.at[mine], own.at[N_LOADS + at]
        )
        for at, (src, dst) in enumerate(((gin, gin_out), (y_in, y_out)))
    ]

    def trade(src, dst):
        made = []
        for other in ((z, x, 1 - y, c), (z, x, 1 - y, 1 - c), (z, x, y, 1 - c)):
            their = other[2] * 2 + other[3]
            made.append(
                plan.add(
                    lambda their=their, other=other: (
                        src.at[:, pl.ds(pl.multiple_of(their * span, span), span), :],
                        dst.at[mine],
                        other,
                    )
                )
            )
        return made

    trade_g, trade_y = trade(gin, gin_out), trade(y_in, y_out)
    ways = [(z, x, y, 1 - c), (z, x, 1 - y, c), (z, 1 - x, y, c)]
    ways += [((z + j) % 4, x, y, c) for j in range(1, 4)]
    vec_sends = [
        plan.add(lambda at=at, to=to: (vec.at[min(at, 3)], vec_from.at[at], to))
        for at, to in enumerate(ways)
    ]

    def vec_task(at):
        if at == 0:
            plan.start(vec_sends[0])
            return
        plan.arrived(vec_sends[at - 1])
        vec[at] = vec[at - 1] + vec_from[at - 1]
        for index in vec_sends[at:] if at == 3 else vec_sends[at : at + 1]:
            plan.start(index)

    def vec_end():
        for index in vec_sends[3:]:
            plan.arrived(index)
        vec_out[...] = vec[3] + vec_from[3] + vec_from[4] + vec_from[5]

    def do_tasks(todo):
        for entry in todo:
            if entry[0] == "vec":
                vec_task(entry[1])
            elif entry[0] == "trade":
                for index in trade_y:
                    plan.start(index)
            else:
                getattr(works[entry[0]], entry[1])()

    vec[0] = vec_in[...]
    for name in ("down_y", "down", "up_low", "up_high", "out"):
        works[name].begin()
    kept[1]().start()
    for load in loads[:4]:
        load().wait()

    def step(s, carry):
        for when, todo in DURING.items():

            @pl.when(s == when)
            def _(todo=todo):
                do_tasks(todo)

        t, h = s // (STEPS // share), s % (STEPS // share)
        base = pl.multiple_of(t * LEN, LEN)
        cols = [pl.ds(pl.multiple_of(part * D + h * PAIR, PAIR), PAIR) for part in range(3)]
        attend_back(len_ref[t], acts, mixed, logs, do, d, vec.at[0], t, h, base, cols)
        return carry

    lax.fori_loop(0, STEPS, step, 0)
    do_tasks(AFTER["attention"])
    loads[4]().wait()
    rows = share * LEN
    x_turned[...] = x_all[...].T
    tile = 256
    tiles = D // tile

    def grad_tile(i, carry):
        at = (2 - i // tiles) * tiles + i % tiles
        cols = pl.ds(pl.multiple_of(at * tile, tile), tile)
        value = jnp.dot(x_turned[...], d[:, cols], preferred_element_type=F32)
        gw[:, :, :, cols] = value.astype(BF16).reshape(4, 2, D // 8, tile)
        for part, name in enumerate(("v", "k", "q")):

            @pl.when(i == part * tiles + tiles - 1)
            def _(name=name):
                works[name].begin()
                do_tasks(AFTER[name])

        return carry

    lax.fori_loop(0, 3 * tiles, grad_tile, 0)
    loads[5]().wait()
    loads[6]().wait()

    def token_tile(i, carry):
        cols = pl.ds(pl.multiple_of(i * tile, tile), tile)
        value = back_mul(d[...], w_all[cols, :]) + one[:, cols]
        gin[:, :, cols] = value.astype(BF16).reshape(share, LEN, tile)
        for when in range(D // tile):

            @pl.when(i == when)
            def _(when=when):
                do_tasks(AFTER[when])

        return carry

    lax.fori_loop(0, D // tile, token_tile, 0)
    for index in trade_g:
        plan.start(index)
    kept[0]().start()
    do_tasks(AFTER["end"])
    vec_end()
    for work in works.values():
        work.end()
    for index in trade_g + trade_y:
        plan.arrived(index)
    for work in works.values():
        work.finish_sends()
    for index in trade_g + trade_y + vec_sends:
        plan.build(index).wait_send()
    for made in kept:
        made().wait()


DURING = {
    0: [("down_y", "after_core")],
    1: [("down", "after_core"), ("up_low", "after_core")],
    2: [("up_high", "after_core")],
    3: [("out", "after_core"), ("trade",)],
    7: [("down", "after_x")],
    9: [("down_y", "after_y")],
    11: [("up_high", "after_x")],
}
AFTER = {
    "attention": [("vec", 0), ("down", "after_a")],
    "v": [("vec", 1), ("up_low", "after_y")],
    "k": [("v", "after_core"), ("vec", 2)],
    "q": [("k", "after_core"), ("vec", 3), ("out", "after_x"), ("down", "after_b")],
    0: [("q", "after_core"), ("up_high", "after_a")],
    1: [("down", "after_z"), ("down_y", "after_x")],
    2: [("up_high", "after_b")],
    "end": [
        ("out", "after_a"),
        ("up_low", "after_x"),
        ("down_y", "after_a"),
        ("out", "after_b"),
        ("up_high", "after_z"),
        ("down_y", "after_b"),
        ("up_low", "after_a"),
        ("v", "after_x"),
        ("out", "after_z"),
        ("down_y", "after_z"),
        ("up_low", "after_b"),
        ("v", "after_a"),
        ("k", "after_x"),
        ("up_low", "after_z"),
        ("v", "after_b"),
        ("k", "after_a"),
        ("q", "after_x"),
        ("v", "after_z"),
        ("k", "after_b"),
        ("q", "after_a"),
        ("k", "after_z"),
        ("q", "after_b"),
        ("down", "after_final"),
        ("up_high", "after_final"),
        ("out", "after_final"),
        ("down_y", "after_final"),
        ("up_low", "after_final"),
        ("q", "after_z"),
        ("v", "after_final"),
        ("k", "after_final"),
        ("q", "after_final"),
    ],
}


def reduce_all(lengths, acts, mixed, do, logs, rows, whole, one, result, vec, up, down, out):
    share, length = result.shape[:2]
    vmem = pl.BlockSpec(memory_space=pltpu.VMEM)
    hbm = pl.BlockSpec(memory_space=pl.ANY)
    shape = lambda a: jax.ShapeDtypeStruct(a.shape[2:], a.dtype)
    back = jax.ShapeDtypeStruct((share * 4, length // 4, D), BF16)
    scratch = [s for _, slab in SLABS.values() for s in slab.scratch()]
    wires = 12 + sum(slab.copies() for _, slab in SLABS.values())
    like = lambda a: pltpu.VMEM(a.shape, a.dtype)
    return pl.pallas_call(
        reduce_kernel,
        in_specs=[pl.BlockSpec(memory_space=pltpu.SMEM)] + [hbm] * 7 + [vmem] * 2 + [hbm] * 3,
        out_specs=[hbm] * 6 + [vmem],
        out_shape=[
            back, back, shape(up), shape(down),
            jax.ShapeDtypeStruct((D // 8, 3 * D), BF16),
            shape(out),
            jax.ShapeDtypeStruct((16, D), F32),
        ],
        scratch_shapes=[like(a) for a in (acts, mixed, do, logs, rows, whole, one)]
        + [
            pltpu.VMEM(rows.shape[::-1], BF16),
            pltpu.VMEM(acts.shape, BF16),
            pltpu.VMEM((4, 2, D // 8, 3 * D), BF16),
            pltpu.VMEM((share, length, D), BF16),
            pltpu.VMEM((4, 16, D), F32),
            pltpu.VMEM((6, 16, D), F32),
        ]
        + scratch
        + [
            pltpu.SemaphoreType.DMA((wires,)),
            pltpu.SemaphoreType.DMA((wires,)),
            pltpu.SemaphoreType.DMA((N_LOADS + 2 + 3 * len(SLABS),)),
        ],
        compiler_params=pltpu.CompilerParams(
            collective_id=1, has_side_effects=True, vmem_limit_bytes=VMEM_ALL
        ),
        name="attend_reduce",
    )(lengths, acts, mixed, do, logs, rows, whole, one, result, vec, up, down, out)


def local(*args):
    tables, lengths, cotangent, step_count = args[:4]
    masters, firsts, seconds = args[4:9], args[9:14], args[14:19]
    w_qkv, w_out, w_up, w_down, vectors = masters
    blocks = lax.axis_size("blk")
    shards = lax.axis_size("tab")
    table_count, local_len = tables.shape[:2]
    share = table_count // blocks
    tuned = shards == 8 and blocks == 4
    owned = vectors.shape[0]
    vec_own = jnp.pad(vectors.astype(BF16).T, ((0, 4), (0, 0)))
    my_lengths = lax.dynamic_slice(lengths, (lax.axis_index("blk") * share,), (share,))
    if tuned:
        at_own = (0, lax.axis_index("tab") * owned)
        vec_wide = lax.dynamic_update_slice(jnp.zeros((16, D), BF16), vec_own, at_own)
        mine, cot, *wholes, qkv, mixed, logs = gather_all(
            my_lengths, tables, cotangent, w_qkv, w_out, w_up, w_down, vec_wide[None]
        )
        vec_f = jnp.sum(wholes[4].astype(F32), axis=0)[:12]
    else:
        spread = partial(lax.all_to_all, axis_name="blk", split_axis=0, concat_axis=1, tiled=True)
        mine, cot = spread(tables), spread(cotangent)
        narrow = [w.astype(BF16) for w in (w_qkv, w_out, w_up, w_down)]
        wholes = [lax.all_gather(w, "tab", axis=0) for w in narrow + [vec_own]]
        vec_f = wholes[4][:, :12].transpose(1, 0, 2).reshape(12, D).astype(F32)
    full_qkv, full_out, full_up, full_down = [
        w.reshape(-1, w.shape[-1]) for w in wholes[:4]
    ]
    bias_up = vec_f[8:12].reshape(-1)
    rows = mine.reshape(-1, D)
    if not tuned:
        bias_qkv = jnp.concatenate([vec_f[0], jnp.zeros((D,), F32), vec_f[1]])
        qkv = (jnp.dot(rows, full_qkv, preferred_element_type=F32) + bias_qkv).astype(BF16)
        mixed, logs = attention_forward(my_lengths, qkv, share)
    attn_out = jnp.dot(mixed, full_out, preferred_element_type=F32) + vec_f[2]
    normed_one, norm_one_back = jax.vjp(
        layer_norm, rows.astype(F32) + attn_out, vec_f[4], vec_f[5]
    )
    normed_b = normed_one.astype(BF16)
    hidden = jnp.dot(normed_b, full_up, preferred_element_type=F32) + bias_up
    below = 0.5 * (1.0 + lax.erf(hidden * 0.5**0.5))
    active_b = (hidden * below).astype(BF16)
    slope = below + hidden * jnp.exp(-0.5 * hidden * hidden) * (2.0 * math.pi) ** -0.5
    active_b, slope = lax.optimization_barrier((active_b, slope.astype(BF16)))
    branch = jnp.dot(active_b, full_down, preferred_element_type=F32) + vec_f[3]
    result, norm_two_back = jax.vjp(layer_norm, normed_one + branch, vec_f[6], vec_f[7])
    result = result.astype(BF16).reshape(mine.shape)
    grad_two, grad_g2, grad_c2 = norm_two_back(cot.reshape(-1, D).astype(F32))
    grad_b2 = jnp.sum(grad_two, axis=0)
    branch_b = grad_two.astype(BF16)
    gw_down = inner(active_b, branch_b).astype(BF16)
    grad_hidden = back_mul(branch_b, full_down) * slope.astype(F32)
    grad_b1 = jnp.sum(grad_hidden, axis=0)
    hidden_b = grad_hidden.astype(BF16)
    gw_up = inner(normed_b, hidden_b).astype(BF16)
    grad_one, grad_g1, grad_c1 = norm_one_back(grad_two + back_mul(hidden_b, full_up))
    grad_bo = jnp.sum(grad_one, axis=0)
    attn_b = grad_one.astype(BF16)
    gw_out = inner(mixed, attn_b).astype(BF16)
    grad_mixed = back_mul(attn_b, full_out).astype(BF16)
    norm_rows = [grad_bo, grad_b2, grad_g1, grad_c1, grad_g2, grad_c2]
    if tuned:
        empty = jnp.zeros((2, D), F32)
        wide_vec = jnp.concatenate(
            [empty, jnp.stack(norm_rows), grad_b1.reshape(4, D), empty, empty]
        )
        by_owner = lambda g: g.reshape(4, 2, -1, g.shape[-1])
        grad_input, output, *sums = reduce_all(
            my_lengths, qkv, mixed, grad_mixed, logs, rows, full_qkv, grad_one, result,
            wide_vec, by_owner(gw_up), by_owner(gw_down), by_owner(gw_out),
        )
        at_own = (0, lax.axis_index("tab") * owned)
        sum_vec = lax.dynamic_slice(sums[4], at_own, (16, owned))[:12].T
        shares = [s.astype(F32) for s in (sums[2], sums[3], sums[0], sums[1], sum_vec)]
    else:
        grad_three, sums = attention_backward(my_lengths, qkv, mixed, logs, grad_mixed, share)
        sums = jnp.sum(sums[:, :, :2], axis=0)
        grad_bq, grad_bv = sums[:, 0].reshape(-1), sums[:, 1].reshape(-1)
        grad_qkv = jnp.concatenate([grad_three[i] for i in range(3)], axis=1)
        gw_qkv = inner(rows, grad_qkv).astype(BF16)
        grad_in = grad_one + back_mul(grad_qkv, full_qkv)
        grad_in = grad_in.astype(BF16).reshape(mine.shape)
        gw_vec = jnp.concatenate(
            [jnp.stack([grad_bq, grad_bv] + norm_rows), grad_b1.reshape(4, D)]
        )
        back = partial(lax.all_to_all, axis_name="blk", split_axis=1, concat_axis=0, tiled=True)
        grad_input, output = back(grad_in), back(result)

        def collect(grad):
            part = lax.psum_scatter(
                grad.reshape(shards, -1, grad.shape[-1]), "tab", scatter_dimension=0
            )
            return lax.psum(part.astype(BF16), "blk").astype(F32)

        shares = [collect(g) for g in (gw_qkv, gw_out, gw_up, gw_down)]
        shares.append(collect(gw_vec.T.astype(BF16)))
    grad_input = grad_input.astype(F32)
    step_float = step_count[0].astype(F32)
    results = [output, grad_input]
    for at in range(5):
        results.extend(
            adam(masters[at], shares[at], firsts[at], seconds[at], RATES[at], step_float)
        )
    return tuple(results)


def solution(mesh):
    tokens, flat, rows = P("tab", "blk", None), P("tab"), P("tab", None)
    return jax.shard_map(
        local,
        mesh=mesh,
        in_specs=(tokens, flat, tokens, P()) + (rows,) * 15,
        out_specs=(tokens, tokens) + (rows,) * 20,
        check_vma=False,
    )
```

```python
import math
from functools import partial

import jax
import jax.numpy as jnp
from jax import lax
from jax.experimental import pallas as pl
from jax.experimental.pallas import tpu as pltpu
from jax.sharding import PartitionSpec as P

D = 768
H = 12
HD = 64
LEN = 512
FF = 3072
PAIR = 2 * HD

EPS = 1e-06
NEGATIVE = -1e30
BETA_ONE = 0.9
BETA_TWO = 0.999
ADAM_EPS = 1e-08
DECAY = 0.01
RATES = (1.0, 15.0, 1.0, 0.5, 5.0)

F32 = jnp.float32
BF16 = jnp.bfloat16
MESH_ID = pl.DeviceIdType.MESH
VMEM_ALL = 64 * 1000 * 1024


def layer_norm(hidden, gain_vec, shift_vec):
    row_mean = jnp.mean(hidden, axis=-1, keepdims=True)
    centred = hidden - row_mean
    variance = jnp.mean(centred * centred, axis=-1, keepdims=True)
    return centred * lax.rsqrt(variance + EPS) * gain_vec + shift_vec


def inner(left, right):
    return lax.dot_general(left, right, (((0,), (0,)), ((), ())), preferred_element_type=F32)


def back_mul(left, right):
    return lax.dot_general(left, right, (((1,), (1,)), ((), ())), preferred_element_type=F32)


def adam(master, gradient, first_moment, second_moment, rate_now, step_float):
    moment_new = BETA_ONE * first_moment + (1.0 - BETA_ONE) * gradient
    square_new = BETA_TWO * second_moment + (1.0 - BETA_TWO) * gradient * gradient
    fix_one = 1.0 - jnp.power(BETA_ONE, step_float)
    fix_two = 1.0 - jnp.power(BETA_TWO, step_float)
    update = moment_new / fix_one / (jnp.sqrt(square_new / fix_two) + ADAM_EPS)
    master_new = master - rate_now * (update + DECAY * master)
    return (moment_new, square_new, master_new, master_new.astype(BF16))


def head_masks(dtype):
    lane = lax.broadcasted_iota(jnp.int32, (1, PAIR), 1)
    return [(lane < HD).astype(dtype), (lane >= HD).astype(dtype)]


def attn_fwd_kernel(len_ref, q_ref, k_ref, v_ref, o_ref, l_ref):
    live = len_ref[pl.program_id(0)]
    masks = head_masks(BF16)
    keys = k_ref[...]
    values = v_ref[...]
    rows = 256
    key_at = lax.broadcasted_iota(jnp.int32, (1, LEN), 1)
    bias = jnp.where(key_at < live, 0.0, NEGATIVE)
    lane = lax.broadcasted_iota(jnp.int32, (1, PAIR), 1)
    for start in range(0, LEN, rows):
        query = q_ref[pl.ds(start, rows), :] * jnp.asarray(HD ** (-0.5), BF16)
        mixed, logs = [], []
        for head in range(2):
            scores = back_mul(query * masks[head], keys) + bias
            top = jnp.max(scores, axis=-1, keepdims=True)
            raised = jnp.exp(scores - top)
            total = jnp.sum(raised, axis=-1, keepdims=True)
            probs = (raised * (1.0 / total)).astype(BF16)
            mixed.append(jnp.dot(probs, values, preferred_element_type=F32))
            logs.append(top + jnp.log(total))
        o_ref[pl.ds(start, rows), :] = jnp.where(lane < HD, mixed[0], mixed[1]).astype(BF16)
        both = jnp.where(lane < HD, logs[0], logs[1])
        flat = both.T
        l_ref[0, 0, 0:1, pl.ds(start, rows)] = flat[0:1, :]
        l_ref[0, 0, 1:2, pl.ds(start, rows)] = flat[HD : HD + 1, :]


def attention_forward(lengths, qkv, tables):
    pairs = H // 2
    spec = lambda part: pl.BlockSpec((LEN, PAIR), lambda t, h, n: (t, part * pairs + h))
    return pl.pallas_call(
        attn_fwd_kernel,
        grid_spec=pltpu.PrefetchScalarGridSpec(
            num_scalar_prefetch=1,
            grid=(tables, pairs),
            in_specs=[spec(0), spec(1), spec(2)],
            out_specs=[
                pl.BlockSpec((LEN, PAIR), lambda t, h, n: (t, h)),
                pl.BlockSpec((1, 1, 8, LEN), lambda t, h, n: (t, h, 0, 0)),
            ],
        ),
        out_shape=[
            jax.ShapeDtypeStruct((tables * LEN, D), BF16),
            jax.ShapeDtypeStruct((tables, pairs, 8, LEN), F32),
        ],
        name="attn_fwd",
    )(lengths, qkv, qkv, qkv)


def attn_bwd_kernel(len_ref, q_ref, k_ref, v_ref, o_ref, l_ref, do_ref, d_ref, sums_ref):
    live = len_ref[pl.program_id(0)]
    masks = head_masks(BF16)
    keys = k_ref[...]
    values = v_ref[...]
    query = q_ref[...] * jnp.asarray(HD ** (-0.5), BF16)
    grad_out = do_ref[...]
    dots = (grad_out.astype(F32) * o_ref[...].astype(F32)).T
    rows = 256
    q_masked = [query * m for m in masks]
    g_masked = [grad_out * m for m in masks]
    deltas = [jnp.sum(dots[h * HD : (h + 1) * HD, :], axis=0, keepdims=True) for h in range(2)]
    logs = [l_ref[0, 0, h : h + 1, :] for h in range(2)]
    grad_q = jnp.zeros((LEN, PAIR), F32)
    sum_v = jnp.zeros((1, PAIR), F32)
    for start in range(0, LEN, rows):
        part_k = keys[start : start + rows, :]
        part_v = values[start : start + rows, :]
        key_at = start + lax.broadcasted_iota(jnp.int32, (rows, 1), 0)
        bias = jnp.where(key_at < live, 0.0, NEGATIVE)
        grad_k = jnp.zeros((rows, PAIR), F32)
        grad_v = jnp.zeros((rows, PAIR), F32)
        for head in range(2):
            scores = back_mul(part_k, q_masked[head])
            probs = jnp.exp(scores + bias - logs[head])
            grad_probs = back_mul(part_v, g_masked[head])
            grad_s = (probs * (grad_probs - deltas[head])).astype(BF16)
            grad_v += jnp.dot(probs.astype(BF16), g_masked[head], preferred_element_type=F32)
            grad_k += jnp.dot(grad_s, q_masked[head], preferred_element_type=F32)
            grad_q += inner(grad_s, part_k * masks[head])
        d_ref[1, pl.ds(start, rows), :] = grad_k.astype(BF16)
        d_ref[2, pl.ds(start, rows), :] = grad_v.astype(BF16)
        sum_v += jnp.sum(grad_v, axis=0, keepdims=True)
    grad_q = grad_q * HD ** (-0.5)
    d_ref[0, :, :] = grad_q.astype(BF16)
    sums_ref[0, 0, 0:1, :] = jnp.sum(grad_q, axis=0, keepdims=True)
    sums_ref[0, 0, 1:2, :] = sum_v


def attention_backward(lengths, qkv, mixed, logs, grad_mixed, tables):
    pairs = H // 2
    spec = lambda part: pl.BlockSpec((LEN, PAIR), lambda t, h, n: (t, part * pairs + h))
    block = pl.BlockSpec((LEN, PAIR), lambda t, h, n: (t, h))
    return pl.pallas_call(
        attn_bwd_kernel,
        grid_spec=pltpu.PrefetchScalarGridSpec(
            num_scalar_prefetch=1,
            grid=(tables, pairs),
            in_specs=[
                spec(0),
                spec(1),
                spec(2),
                block,
                pl.BlockSpec((1, 1, 8, LEN), lambda t, h, n: (t, h, 0, 0)),
                block,
            ],
            out_specs=[
                pl.BlockSpec((3, LEN, PAIR), lambda t, h, n: (0, t, h)),
                pl.BlockSpec((1, 1, 8, PAIR), lambda t, h, n: (t, h, 0, 0)),
            ],
        ),
        out_shape=[
            jax.ShapeDtypeStruct((3, tables * LEN, D), BF16),
            jax.ShapeDtypeStruct((tables, pairs, 8, PAIR), F32),
        ],
        name="attn_bwd",
    )(lengths, qkv, qkv, qkv, mixed, logs, grad_mixed)


def place():
    tab, blk = lax.axis_index("tab"), lax.axis_index("blk")
    return tab // 2, tab % 2, blk // 2, blk % 2


def z_line():
    z = place()[0]
    inner = (z + 1) // 2 % 2
    near = inner * (z - 1) * 3 + (1 - inner) * (1 + z // 3)
    second = inner * (3 - z) + (1 - inner) * (3 - near)
    third = inner * (3 - near) + (1 - inner) * (3 - z)
    return inner, near, (near, second, third)


def greet(peers):
    barrier = pltpu.get_barrier_semaphore()
    for z, x, y, c in peers:
        pl.semaphore_signal(
            barrier, inc=1, device_id=(z * 2 + x, y * 2 + c), device_id_type=MESH_ID
        )
    pl.semaphore_wait(barrier, len(peers))


def all_peers():
    z, x, y, c = place()
    z_peers = [((z + j) % 4, x, y, c) for j in range(1, 4)]
    rest = [(z, 1 - x, y, c), (z, x, 1 - y, c), (z, x, y, 1 - c), (z, x, 1 - y, 1 - c)]
    return z_peers + rest


def by_columns(width):
    return lambda ref, t, part: ref.at[t, :, pl.ds(pl.multiple_of(part * width, 128), width)]


def by_rows(height):
    return lambda ref, t, part: ref.at[t, pl.ds(pl.multiple_of(part * height, 16), height), :]


PIECES = (
    (by_columns(3 * D // 2), False),
    (by_columns(D // 2), False),
    (by_columns(FF // 4), True),
    (by_rows(FF // 16), False),
)
G_WIRES = 96
STEPS = 12


class Gather:
    def __init__(self, at, shard, whole, plan):
        piece, self.split = PIECES[at]
        z, x, y, c = place()
        tab = z * 2 + x
        part = y * 2 + c if self.split else c
        other = (1 - y) * 2 + c
        own = lambda: piece(shard, 0, part)
        self.plan = plan
        self.middle, outer, order = z_line()
        near = lambda j: order[j - 1] * 2 + x
        far = lambda j: order[j - 1] * 2 + 1 - x if j else z * 2 + 1 - x

        def send(at_tab, which, to, first=False, inner=False):
            return plan.add(
                lambda: (
                    own() if first else piece(whole, at_tab, which),
                    piece(whole, at_tab, which),
                    to,
                ),
                inner,
            )

        side, over, across = (z, x, y, 1 - c), (z, x, 1 - y, c), (z, 1 - x, y, c)
        to_outer, to_inner = (outer, x, y, c), (3 - z, x, y, c)
        self.own_near = send(tab, part, to_outer, True)
        self.own_inner = send(tab, part, to_inner, True, inner=True)
        self.passed = [
            send(near(j), part, to_inner if j == 1 else to_outer, inner=True) for j in range(1, 4)
        ]
        self.x = [send(tab, part, across, True)]
        self.x += [send(near(j), part, across) for j in range(1, 4)]
        tabs = [near(j) for j in range(1, 4)] + [far(j) for j in range(4)]
        self.c = [send(t, part, side) for t in tabs]
        self.y = [send(t, part, over) for t in tabs] if self.split else []
        self.late = [send(t, other, side) for t in tabs] if self.split else []

    def send_z(self):
        self.plan.start(self.own_near)

        @pl.when(self.middle == 1)
        def _():
            self.plan.start(self.own_inner)

    def send_x(self):
        self.plan.start(self.x[0])

    def onward(self, at):
        if self.split:
            self.plan.start(self.y[at])
        self.plan.start(self.c[at])

    def task_z(self, j):
        if j == 1:
            self.plan.arrived(self.own_near)
        else:

            @pl.when(self.middle == 0)
            def _():
                self.plan.arrived(self.passed[j - 1])

        @pl.when(self.middle == 1)
        def _():
            if j > 1:
                self.plan.arrived(self.own_inner if j == 2 else self.passed[0])
            self.plan.start(self.passed[j - 1])

        self.plan.start(self.x[j])
        self.onward(j - 1)

    def task_x(self, j):
        self.plan.arrived(self.x[j])
        self.onward(3 + j)

    def task_y(self, at):
        self.plan.arrived(self.y[at])
        self.plan.start(self.late[at])

    def end(self):
        for index in self.c + self.late:
            self.plan.arrived(index)


def gather_kernel(
    len_ref, x_in, cot_in, qkv_wide, out_wide, up_wide, down_wide, vec_in,
    x_out, cot_out, qkv_out, out_out, up_out, down_out, vec_out, acts_out, mixed_out, logs_out,
    qkv_in, out_in, up_in, down_in, x_all, w_all, vec_all, acts, mixed, logs, bias,
    send, recv, own,
):
    z, x, y, c = place()
    tab, blk = z * 2 + x, y * 2 + c
    share, span = x_in.shape[0] // 4, x_in.shape[1]
    mine = pl.ds(blk * share, share)
    slot = pl.ds(pl.multiple_of(blk * span, span), span)
    plan = Plan(send, recv)
    shards = (qkv_in, out_in, up_in, down_in)
    wholes = (w_all, out_out, up_out, down_out)
    works = [Gather(at, shards[at], wholes[at], plan) for at in range(4)]
    qkv, out, up, down = works

    def trade(src, dst):
        made = []
        for other in ((z, x, 1 - y, c), (z, x, 1 - y, 1 - c), (z, x, y, 1 - c)):
            their = other[2] * 2 + other[3]
            made.append(
                plan.add(
                    lambda their=their, other=other: (
                        src.at[pl.ds(their * share, share)], dst.at[:, slot, :], other,
                    )
                )
            )
        return made

    trade_x, trade_cot = trade(x_in, x_all), trade(cot_in, cot_out)
    vec_z = [
        plan.add(lambda j=j: (vec_in.at[0], vec_all.at[tab], ((z + j) % 4, x, y, c)))
        for j in range(1, 4)
    ]
    vec_x = [plan.add(lambda: (vec_in.at[0], vec_all.at[tab], (z, 1 - x, y, c)))]
    for j in range(1, 4):
        t = (z + 4 - j) % 4 * 2 + x
        vec_x.append(plan.add(lambda t=t: (vec_all.at[t], vec_all.at[t], (z, 1 - x, y, c))))
    keeps = [
        lambda: pltpu.make_async_copy(x_in.at[mine], x_all.at[:, slot, :], own.at[0]),
        lambda: pltpu.make_async_copy(qkv_in.at[0], w_all.at[tab], own.at[1]),
        lambda: pltpu.make_async_copy(vec_in.at[0], vec_all.at[tab], own.at[2]),
        lambda: pltpu.make_async_copy(cot_in.at[mine], cot_out.at[:, slot, :], own.at[3]),
        lambda: pltpu.make_async_copy(out_in.at[0], out_out.at[tab], own.at[4]),
        lambda: pltpu.make_async_copy(up_in.at[0], up_out.at[tab], own.at[5]),
        lambda: pltpu.make_async_copy(down_in.at[0], down_out.at[tab], own.at[6]),
    ]
    puts = [
        lambda: pltpu.make_async_copy(x_all, x_out, own.at[7]),
        lambda: pltpu.make_async_copy(w_all, qkv_out, own.at[8]),
        lambda: pltpu.make_async_copy(vec_all, vec_out, own.at[9]),
        lambda: pltpu.make_async_copy(acts, acts_out, own.at[10]),
        lambda: pltpu.make_async_copy(mixed, mixed_out, own.at[11]),
        lambda: pltpu.make_async_copy(logs, logs_out, own.at[12]),
    ]
    for wide, narrow in zip((qkv_wide, out_wide, up_wide, down_wide), shards):

        def rounded(i, carry, wide=wide, narrow=narrow):
            rows = pl.ds(pl.multiple_of(i * 16, 16), 16)
            narrow[0, rows, :] = wide[rows, :].astype(BF16)
            return carry

        lax.fori_loop(0, wide.shape[0] // 16, rounded, 0)
    greet(all_peers())
    for index in vec_z + vec_x[:1]:
        plan.start(index)
    qkv.send_z()
    qkv.send_x()
    for index in trade_x:
        plan.start(index)
    for keep in keeps:
        keep().start()
    for work in (out, up, down):
        work.send_z()
    out.send_x()
    for index in trade_cot:
        plan.start(index)
    for j in range(1, 4):
        plan.arrived(vec_z[j - 1])
        plan.start(vec_x[j])
    for j in range(1, 4):
        qkv.task_z(j)
    up.send_x()
    down.send_x()
    for j in range(4):
        qkv.task_x(j)
    for index in vec_x:
        plan.arrived(index)
    for keep in keeps[:3]:
        keep().wait()
    for index in trade_x:
        plan.arrived(index)
    qkv.end()
    for put in puts[:3]:
        put().start()

    tile = 256
    rows = share * LEN
    spread = [vec_all[t, 0:16, :].astype(F32) for t in range(8)]
    vectors = spread[0]
    for t in range(1, 8):
        vectors = vectors + spread[t]
    bias[:, 0:D] = vectors[0:1, :]
    bias[:, D : 2 * D] = jnp.zeros((1, D), F32)
    bias[:, 2 * D : 3 * D] = vectors[1:2, :]

    def project(i, carry):
        cols = pl.ds(pl.multiple_of(i * tile, tile), tile)
        weight = w_all[:, :, cols].reshape(D, tile)

        def table(t, carry):
            value = jnp.dot(x_all[t], weight, preferred_element_type=F32) + bias[:, cols]
            acts[pl.ds(pl.multiple_of(t * LEN, LEN), LEN), cols] = value.astype(BF16)
            return carry

        return lax.fori_loop(0, share, table, carry)

    lax.fori_loop(0, 3 * D // tile, project, 0)
    puts[3]().start()

    tasks = {
        0: [lambda j=j: out.task_z(j) for j in (1, 2, 3)],
        1: [lambda: up.task_z(1), lambda: up.task_z(2)],
        2: [lambda j=j: out.task_x(j) for j in range(4)] + [lambda: up.task_z(3)],
        3: [lambda: up.task_x(0)],
        4: [lambda: down.task_z(1)],
        5: [lambda: down.task_z(2), lambda: up.task_x(1)],
        6: [lambda: down.task_x(0), lambda: up.task_x(2)],
        7: [lambda: down.task_z(3)],
        8: [lambda: up.task_x(3), lambda: up.task_y(0)],
        9: [lambda: up.task_y(1), lambda: down.task_x(1)],
        10: [lambda: up.task_y(2), lambda: up.task_y(3)],
        11: [lambda: up.task_y(4), lambda: down.task_x(2)],
        12: [lambda: up.task_y(5), lambda: up.task_y(6), lambda: down.task_x(3)],
    }

    def step(s, carry):
        for when, todo in tasks.items():
            if when < STEPS:

                @pl.when(s == when)
                def _(todo=todo):
                    for task in todo:
                        task()

        t, h = s // (STEPS // share), s % (STEPS // share)
        base = pl.multiple_of(t * LEN, LEN)
        cols = [pl.ds(pl.multiple_of(part * D + h * PAIR, PAIR), PAIR) for part in range(3)]
        attend(len_ref[t], acts, mixed, logs, t, h, base, cols)
        return carry

    lax.fori_loop(0, STEPS, step, 0)
    for put in puts[4:]:
        put().start()
    for task in tasks[STEPS]:
        task()
    for index in trade_cot:
        plan.arrived(index)
    for work in (out, up, down):
        work.end()
    plan.finish(z_line()[0])
    for keep in keeps[3:]:
        keep().wait()
    for put in puts:
        put().wait()


def attend(live, acts, mixed_ref, logs_ref, t, h, base, cols):
    masks = head_masks(BF16)
    keys = acts[pl.ds(base, LEN), cols[1]]
    values = acts[pl.ds(base, LEN), cols[2]]
    rows = 256
    key_at = lax.broadcasted_iota(jnp.int32, (1, LEN), 1)
    bias = jnp.where(key_at < live, 0.0, NEGATIVE)
    lane = lax.broadcasted_iota(jnp.int32, (1, PAIR), 1)

    def half(i, carry):
        at = pl.ds(pl.multiple_of(base + i * rows, rows), rows)
        query = acts[at, cols[0]] * jnp.asarray(HD ** (-0.5), BF16)
        mixed, logs = [], []
        for head in range(2):
            scores = back_mul(query * masks[head], keys) + bias
            top = jnp.max(scores, axis=-1, keepdims=True)
            raised = jnp.exp(scores - top)
            total = jnp.sum(raised, axis=-1, keepdims=True)
            probs = (raised * (1.0 / total)).astype(BF16)
            mixed.append(jnp.dot(probs, values, preferred_element_type=F32))
            logs.append(top + jnp.log(total))
        mixed_ref[at, cols[0]] = jnp.where(lane < HD, mixed[0], mixed[1]).astype(BF16)
        flat = jnp.where(lane < HD, logs[0], logs[1]).T
        to = pl.ds(pl.multiple_of(i * rows, rows), rows)
        logs_ref[t, h, 0:1, to] = flat[0:1, :]
        logs_ref[t, h, 1:2, to] = flat[HD : HD + 1, :]
        return carry

    lax.fori_loop(0, LEN // rows, half, 0)


def gather_all(lengths, tables, cotangent, qkv, out, up, down, vec):
    share, span = tables.shape[0] // 4, tables.shape[1] * 4
    vmem = pl.BlockSpec(memory_space=pltpu.VMEM)
    hbm = pl.BlockSpec(memory_space=pl.ANY)
    shape = lambda a: jax.ShapeDtypeStruct((8,) + a.shape[-2:], BF16)
    rows = share * span
    logs = (share, STEPS // share, 8, LEN)
    return pl.pallas_call(
        gather_kernel,
        in_specs=[pl.BlockSpec(memory_space=pltpu.SMEM)] + [vmem] * 7,
        out_specs=[hbm] * 10,
        out_shape=[
            jax.ShapeDtypeStruct((share, span, D), BF16),
            jax.ShapeDtypeStruct((share, span, D), BF16),
            shape(qkv), shape(out), shape(up), shape(down), shape(vec),
            jax.ShapeDtypeStruct((rows, 3 * D), BF16),
            jax.ShapeDtypeStruct((rows, D), BF16),
            jax.ShapeDtypeStruct(logs, F32),
        ],
        scratch_shapes=[
            *[pltpu.VMEM((1,) + w.shape, BF16) for w in (qkv, out, up, down)],
            pltpu.VMEM((share, span, D), BF16),
            pltpu.VMEM((8,) + qkv.shape, BF16),
            pltpu.VMEM((8,) + vec.shape[1:], BF16),
            pltpu.VMEM((rows, 3 * D), BF16),
            pltpu.VMEM((rows, D), BF16),
            pltpu.VMEM(logs, F32),
            pltpu.VMEM((1, 3 * D), F32),
            pltpu.SemaphoreType.DMA((G_WIRES,)),
            pltpu.SemaphoreType.DMA((G_WIRES,)),
            pltpu.SemaphoreType.DMA((13,)),
        ],
        compiler_params=pltpu.CompilerParams(
            collective_id=0, has_side_effects=True, vmem_limit_bytes=VMEM_ALL
        ),
        name="gather_attend",
    )(lengths, tables, cotangent, qkv, out, up, down, vec)


class Plan:
    def __init__(self, send, recv):
        self.send, self.recv, self.makers, self.inner = send, recv, [], []

    def add(self, maker, inner=False):
        self.makers.append(maker)
        if inner:
            self.inner.append(len(self.makers) - 1)
        return len(self.makers) - 1

    def build(self, index):
        src, dst, (z, x, y, c) = self.makers[index]()
        return pltpu.make_async_remote_copy(
            src_ref=src,
            dst_ref=dst,
            send_sem=self.send.at[index],
            recv_sem=self.recv.at[index],
            device_id=(z * 2 + x, y * 2 + c),
            device_id_type=MESH_ID,
        )

    def start(self, index):
        self.build(index).start()

    def arrived(self, index):
        self.build(index).wait_recv()

    def finish(self, inner):
        for index in range(len(self.makers)):
            if index not in self.inner:
                self.build(index).wait_send()

        @pl.when(inner == 1)
        def _():
            for index in self.inner:
                self.build(index).wait_send()


class Slab:
    def __init__(self, rows, cols, split, axis, first=0, dtype=BF16):
        self.rows, self.cols, self.split, self.axis = rows, cols, split, axis
        self.first, self.dtype = first, dtype
        self.tile = 128 if axis == 1 else (16 if dtype == BF16 else 8)

    def cut(self, index):
        size = self.cols if self.axis == 1 else self.rows
        part = pl.ds(pl.multiple_of(self.first + index * size, self.tile), size)
        if self.axis == 1:
            return pl.ds(0, self.rows), part
        return part, pl.ds(0, self.cols)

    def scratch(self):
        ways = 2 if self.split else 1
        vmem = lambda *lead: pltpu.VMEM(lead + (self.rows, self.cols), self.dtype)
        late = vmem(4, 2) if self.split else vmem(1, 1)
        return [vmem(ways, 4, 2), vmem(ways, 4, 2), late, vmem(4), vmem(5), vmem()]

    def copies(self):
        return (2 if self.split else 1) + 1 + 1 + 4 + 3


class Reduction:
    def __init__(self, slab, source, target, scratch, plan, own, own_at):
        self.slab, self.source, self.target, self.plan = slab, source, target, plan
        self.held, self.from_c, self.from_y, self.from_x, self.from_z, self.done = scratch
        self.own, self.own_at = own, own_at
        z, x, y, c = place()
        self.at = z, x, y, c
        self.slot = y if slab.split else 0
        side = (z, x, y, 1 - c)
        over = (z, x, 1 - y, c)

        def index_of(half, core):
            return half * 2 + core if slab.split else core

        def cut_all(ref, index):
            rows, cols = slab.cut(index)
            return ref.at[:, :, rows, cols]

        def cut_out(index):
            rows, cols = slab.cut(index)
            return target.at[rows, cols]

        ways = 2 if slab.split else 1
        self.loads = [
            lambda half=half: pltpu.make_async_copy(
                cut_all(source, index_of(half, c)), self.held.at[half], own.at[own_at + half]
            )
            for half in range(ways)
        ]
        self.to_core = [
            plan.add(
                lambda half=half: (
                    cut_all(source, index_of(half, 1 - c)), self.from_c.at[half], side,
                )
            )
            for half in range(ways)
        ]
        if slab.split:
            self.to_y = plan.add(lambda: (self.held.at[1 - y], self.from_y, over))
        else:
            self.to_y = plan.add(lambda: (self.done, self.from_y.at[0, 0], over))
        self.to_x = plan.add(
            lambda: (self.held.at[self.slot, :, 1 - x], self.from_x, (z, 1 - x, y, c))
        )
        self.middle, outer, _ = z_line()
        self.outer = outer
        self.inward = 2 - z // 2 * 2
        to_outer, to_inner = (outer, x, y, c), (3 - z, x, y, c)
        owned_by = lambda at: self.held.at[self.slot, at, x]
        beyond = lambda: self.held.at[self.slot, pl.ds(self.inward, 2), x]
        self.out_in = plan.add(lambda: (beyond(), self.from_z.at[pl.ds(0, 2)], to_outer))
        self.out_near = plan.add(lambda: (owned_by(outer), self.from_z.at[2], to_outer))
        self.in_in = plan.add(lambda: (beyond(), self.from_z.at[pl.ds(3, 2)], to_inner))
        self.in_out = plan.add(lambda: (owned_by(outer), self.from_z.at[0], to_outer))
        mine = lambda: cut_out(index_of(y, c))
        self.store = lambda: pltpu.make_async_copy(self.done, mine(), own.at[own_at + 2])
        self.share_core = plan.add(lambda: (self.done, mine(), side))
        if slab.split:
            theirs = lambda: cut_out(index_of(1 - y, c))
            self.share_y = plan.add(lambda: (self.done, mine(), over))
            self.share_far = plan.add(lambda: (theirs(), theirs(), side))

    def begin(self):
        for load in self.loads:
            load().start()
        for index in self.to_core:
            self.plan.start(index)

    def summed(self, total, *others, into=None):
        into = total if into is None else into

        def step(i, carry):
            rows = pl.ds(pl.multiple_of(i * 16, 16), 16)
            value = total[rows, :].astype(F32)
            for other in others:
                value = value + other[rows, :].astype(F32)
            into[rows, :] = value.astype(self.slab.dtype)
            return carry

        lax.fori_loop(0, self.slab.rows // 16, step, 0)

    def after_core(self):
        for half, load in enumerate(self.loads):
            load().wait()
            self.plan.arrived(self.to_core[half])

        def step(t, carry):
            for half in range(len(self.loads)):
                self.summed(self.held.at[half, t // 2, t % 2], self.from_c.at[half, t // 2, t % 2])
            return carry

        lax.fori_loop(0, 8, step, 0)
        self.plan.start(self.to_y if self.slab.split else self.to_x)

    def after_y(self):
        if not self.slab.split:
            return
        self.plan.arrived(self.to_y)

        def step(t, carry):
            self.summed(self.held.at[self.slot, t // 2, t % 2], self.from_y.at[t // 2, t % 2])
            return carry

        lax.fori_loop(0, 8, step, 0)
        self.plan.start(self.to_x)

    def after_x(self):
        z, x, y, c = self.at
        self.plan.arrived(self.to_x)

        def step(t, carry):
            self.summed(self.held.at[self.slot, t, x], self.from_x.at[t])
            return carry

        lax.fori_loop(0, 4, step, 0)

        @pl.when(self.middle == 0)
        def _():
            self.plan.start(self.out_in)
            self.plan.start(self.out_near)

    def after_a(self):
        @pl.when(self.middle == 1)
        def _():
            self.plan.arrived(self.out_in)
            for at in range(2):
                total = self.held.at[self.slot, self.inward + at, self.at[1]]
                self.summed(total, self.from_z.at[at])
            self.plan.start(self.in_in)

    def after_b(self):
        @pl.when(self.middle == 1)
        def _():
            self.plan.arrived(self.in_in)
            at = 3 + self.outer - (2 - self.inward)
            total = self.held.at[self.slot, self.outer, self.at[1]]
            self.summed(total, self.from_z.at[at])
            self.plan.start(self.in_out)

    def after_z(self):
        z, x, y, c = self.at

        @pl.when(self.middle == 1)
        def _():
            self.plan.arrived(self.out_near)
            other = self.from_z.at[3 + z - (2 - self.inward)]
            own = self.held.at[self.slot, z, x]
            self.summed(own, self.from_z.at[2], other, into=self.done)

        @pl.when(self.middle == 0)
        def _():
            self.plan.arrived(self.in_out)
            self.summed(self.held.at[self.slot, z, x], self.from_z.at[0], into=self.done)

        if self.slab.split:
            self.plan.start(self.share_y)
            self.plan.start(self.share_core)
            self.store().start()
        else:
            self.plan.start(self.to_y)

    def after_final(self):
        if self.slab.split:
            self.plan.arrived(self.share_y)
            self.plan.start(self.share_far)
        else:
            self.plan.arrived(self.to_y)
            self.plan.build(self.to_y).wait_send()
            self.summed(self.done, self.from_y.at[0, 0])
            self.plan.start(self.share_core)
            self.store().start()

    def end(self):
        self.plan.arrived(self.share_core)
        if self.slab.split:
            self.plan.arrived(self.share_far)
        self.store().wait()

    def finish_sends(self):
        done_early = () if self.slab.split else (self.to_y,)
        sends = self.to_core + [self.to_y, self.to_x, self.share_core]
        if self.slab.split:
            sends += [self.share_y, self.share_far]
        for index in sends:
            if index not in done_early:
                self.plan.build(index).wait_send()

        @pl.when(self.middle == 1)
        def _():
            self.plan.build(self.in_in).wait_send()
            self.plan.build(self.in_out).wait_send()

        @pl.when(self.middle == 0)
        def _():
            self.plan.build(self.out_in).wait_send()
            self.plan.build(self.out_near).wait_send()


SLABS = {
    "down_y": (1, Slab(64, D, True, 0)),
    "up_low": (0, Slab(96, D // 2, True, 1)),
    "down": (1, Slab(32, D, True, 0, first=256)),
    "up_high": (0, Slab(96, D, False, 1, first=2 * D)),
    "out": (3, Slab(96, D // 2, False, 1)),
    "v": (2, Slab(96, D // 2, False, 1, first=2 * D)),
    "k": (2, Slab(96, D // 2, False, 1, first=D)),
    "q": (2, Slab(96, D // 2, False, 1)),
}


def attend_back(live, acts, mixed_ref, logs_ref, do_ref, d_ref, vec_ref, t, h, base, cols):
    masks = head_masks(BF16)
    rows_all = pl.ds(base, LEN)
    keys = acts[rows_all, cols[1]]
    values = acts[rows_all, cols[2]]
    query = acts[rows_all, cols[0]] * jnp.asarray(HD ** (-0.5), BF16)
    grad_out = do_ref[rows_all, cols[0]]
    dots = (grad_out.astype(F32) * mixed_ref[rows_all, cols[0]].astype(F32)).T
    rows = 256
    q_masked = [query * m for m in masks]
    g_masked = [grad_out * m for m in masks]
    deltas = [jnp.sum(dots[i * HD : (i + 1) * HD, :], axis=0, keepdims=True) for i in range(2)]
    logs = [logs_ref[t, h, i : i + 1, :] for i in range(2)]
    grad_q = jnp.zeros((LEN, PAIR), F32)
    sum_v = jnp.zeros((1, PAIR), F32)
    for start in range(0, LEN, rows):
        part_k = keys[start : start + rows, :]
        part_v = values[start : start + rows, :]
        key_at = start + lax.broadcasted_iota(jnp.int32, (rows, 1), 0)
        bias = jnp.where(key_at < live, 0.0, NEGATIVE)
        grad_k = jnp.zeros((rows, PAIR), F32)
        grad_v = jnp.zeros((rows, PAIR), F32)
        for head in range(2):
            scores = back_mul(part_k, q_masked[head])
            probs = jnp.exp(scores + bias - logs[head])
            grad_probs = back_mul(part_v, g_masked[head])
            grad_s = (probs * (grad_probs - deltas[head])).astype(BF16)
            grad_v += jnp.dot(probs.astype(BF16), g_masked[head], preferred_element_type=F32)
            grad_k += jnp.dot(grad_s, q_masked[head], preferred_element_type=F32)
            grad_q += inner(grad_s, part_k * masks[head])
        d_ref[pl.ds(base + start, rows), cols[1]] = grad_k.astype(BF16)
        d_ref[pl.ds(base + start, rows), cols[2]] = grad_v.astype(BF16)
        sum_v += jnp.sum(grad_v, axis=0, keepdims=True)
    grad_q = grad_q * HD ** (-0.5)
    d_ref[rows_all, cols[0]] = grad_q.astype(BF16)
    vec_ref[0:1, cols[0]] += jnp.sum(grad_q, axis=0, keepdims=True)
    vec_ref[1:2, cols[0]] += sum_v


N_LOADS = 7


def reduce_kernel(
    len_ref, acts_in, mixed_in, do_in, logs_in, x_in, w_in, one_in, vec_in,
    up_in, down_in, out_in,
    gin_out, up_out, down_out, qkv_out, out_out, vec_out,
    acts, mixed, do, logs, x_all, w_all, one, x_turned, d, gw, gin, vec, vec_from, *rest,
):
    scratch, (send, recv, own) = rest[:-3], rest[-3:]
    z, x, y, c = place()
    blk = y * 2 + c
    loads = [
        lambda at=at, src=src, dst=dst: pltpu.make_async_copy(src, dst, own.at[at])
        for at, (src, dst) in enumerate(
            (
                (acts_in, acts), (mixed_in, mixed), (do_in, do), (logs_in, logs),
                (x_in, x_all), (w_in, w_all), (one_in, one),
            )
        )
    ]
    for load in loads:
        load().start()
    greet(all_peers())
    plan = Plan(send, recv)
    share, span = gin_out.shape[0] // 4, gin_out.shape[1]
    sources, targets = (up_in, down_in, gw, out_in), (up_out, down_out, qkv_out, out_out)
    works = {}
    for at, (name, (number, slab)) in enumerate(SLABS.items()):
        part = scratch[6 * at : 6 * at + 6]
        works[name] = Reduction(
            slab, sources[number], targets[number], part, plan, own, N_LOADS + 2 + 3 * at
        )
    mine = pl.ds(blk * share, share)
    slot = pl.ds(pl.multiple_of(blk * span, span), span)
    kept = [
        lambda at=at, src=src, dst=dst: pltpu.make_async_copy(
            src.at[:, slot, :], dst.at[mine], own.at[N_LOADS + at]
        )
        for at, (src, dst) in enumerate(((gin, gin_out),))
    ]

    def trade(src, dst):
        made = []
        for other in ((z, x, 1 - y, c), (z, x, 1 - y, 1 - c), (z, x, y, 1 - c)):
            their = other[2] * 2 + other[3]
            made.append(
                plan.add(
                    lambda their=their, other=other: (
                        src.at[:, pl.ds(pl.multiple_of(their * span, span), span), :],
                        dst.at[mine],
                        other,
                    )
                )
            )
        return made

    trade_g = trade(gin, gin_out)
    ways = [(z, x, y, 1 - c), (z, x, 1 - y, c), (z, 1 - x, y, c)]
    ways += [((z + j) % 4, x, y, c) for j in range(1, 4)]
    vec_sends = [
        plan.add(lambda at=at, to=to: (vec.at[min(at, 3)], vec_from.at[at], to))
        for at, to in enumerate(ways)
    ]

    def vec_task(at):
        if at == 0:
            plan.start(vec_sends[0])
            return
        plan.arrived(vec_sends[at - 1])
        vec[at] = vec[at - 1] + vec_from[at - 1]
        for index in vec_sends[at:] if at == 3 else vec_sends[at : at + 1]:
            plan.start(index)

    def vec_end():
        for index in vec_sends[3:]:
            plan.arrived(index)
        vec_out[...] = vec[3] + vec_from[3] + vec_from[4] + vec_from[5]

    def do_tasks(todo):
        for entry in todo:
            if entry[0] == "vec":
                vec_task(entry[1])
            else:
                getattr(works[entry[0]], entry[1])()

    vec[0] = vec_in[...]
    for name in ("up_high", "up_low", "down_y", "down", "out"):
        works[name].begin()
    for load in loads[:4]:
        load().wait()

    def step(s, carry):
        for when, todo in DURING.items():

            @pl.when(s == when)
            def _(todo=todo):
                do_tasks(todo)

        t, h = s // (STEPS // share), s % (STEPS // share)
        base = pl.multiple_of(t * LEN, LEN)
        cols = [pl.ds(pl.multiple_of(part * D + h * PAIR, PAIR), PAIR) for part in range(3)]
        attend_back(len_ref[t], acts, mixed, logs, do, d, vec.at[0], t, h, base, cols)
        return carry

    lax.fori_loop(0, STEPS, step, 0)
    do_tasks(AFTER["attention"])
    loads[4]().wait()
    rows = share * LEN

    def turn(i, carry):
        part = pl.ds(pl.multiple_of(i * 128, 128), 128)
        x_turned[:, part] = x_all[part, :].T
        return carry

    lax.fori_loop(0, rows // 128, turn, 0)
    tile = 256
    tiles = D // tile

    def grad_tile(i, carry):
        at = (2 - i // tiles) * tiles + i % tiles
        cols = pl.ds(pl.multiple_of(at * tile, tile), tile)

        def owners(t, carry):
            left = x_turned[pl.ds(pl.multiple_of(t * (D // 2), D // 2), D // 2), :]
            value = jnp.dot(left, d[:, cols], preferred_element_type=F32)
            gw[pl.ds(t * 2, 2), :, :, cols] = value.astype(BF16).reshape(2, 2, D // 8, tile)
            return carry

        lax.fori_loop(0, 2, owners, 0)
        for part, name in enumerate(("v", "k", "q")):

            @pl.when(i == part * tiles + tiles - 1)
            def _(name=name):
                works[name].begin()
                do_tasks(AFTER[name])

        return carry

    lax.fori_loop(0, 3 * tiles, grad_tile, 0)
    loads[5]().wait()
    loads[6]().wait()

    def token_tile(i, carry):
        cols = pl.ds(pl.multiple_of(i * tile, tile), tile)

        def table(t, carry):
            at = pl.ds(pl.multiple_of(t * LEN, LEN), LEN)
            value = back_mul(d[at, :], w_all[cols, :]) + one[at, cols]
            gin[t, :, cols] = value.astype(BF16)
            return carry

        lax.fori_loop(0, share, table, 0)
        for when in range(D // tile):

            @pl.when(i == when)
            def _(when=when):
                do_tasks(AFTER[when])

        return carry

    lax.fori_loop(0, D // tile, token_tile, 0)
    for index in trade_g:
        plan.start(index)
    kept[0]().start()
    do_tasks(AFTER["end"])
    vec_end()
    for work in works.values():
        work.end()
    for index in trade_g:
        plan.arrived(index)
    for work in works.values():
        work.finish_sends()
    for index in trade_g + vec_sends:
        plan.build(index).wait_send()
    for made in kept:
        made().wait()


DURING = {
    0: [("up_high", "after_core")],
    1: [("up_low", "after_core")],
    2: [("down_y", "after_core")],
    3: [("down", "after_core")],
    4: [("out", "after_core")],
    7: [("up_low", "after_y")],
    8: [("up_high", "after_x")],
    11: [("out", "after_x")],
}
AFTER = {
    "attention": [("vec", 0), ("up_high", "after_a"), ("up_low", "after_x")],
    "v": [("vec", 1)],
    "k": [("v", "after_core"), ("vec", 2), ("down_y", "after_y"), ("out", "after_a")],
    "q": [("k", "after_core"), ("vec", 3), ("up_high", "after_b"), ("up_low", "after_a")],
    0: [("q", "after_core"), ("out", "after_b")],
    1: [("down", "after_y"), ("up_high", "after_z")],
    2: [("down_y", "after_x"), ("up_low", "after_b"), ("out", "after_z")],
    "end": [
        ("v", "after_x"),
        ("down_y", "after_a"),
        ("up_low", "after_z"),
        ("k", "after_x"),
        ("v", "after_a"),
        ("down_y", "after_b"),
        ("q", "after_x"),
        ("k", "after_a"),
        ("v", "after_b"),
        ("down_y", "after_z"),
        ("down", "after_x"),
        ("v", "after_z"),
        ("q", "after_a"),
        ("k", "after_b"),
        ("down", "after_a"),
        ("k", "after_z"),
        ("q", "after_b"),
        ("down", "after_b"),
        ("up_high", "after_final"),
        ("out", "after_final"),
        ("down_y", "after_final"),
        ("up_low", "after_final"),
        ("q", "after_z"),
        ("v", "after_final"),
        ("k", "after_final"),
        ("q", "after_final"),
        ("down", "after_z"),
        ("down", "after_final"),
    ],
}


def reduce_all(lengths, acts, mixed, do, logs, rows, whole, one, vec, up, down, out):
    share, length = acts.shape[0] // LEN, LEN
    vmem = pl.BlockSpec(memory_space=pltpu.VMEM)
    hbm = pl.BlockSpec(memory_space=pl.ANY)
    shape = lambda a: jax.ShapeDtypeStruct(a.shape[2:], a.dtype)
    back = jax.ShapeDtypeStruct((share * 4, length // 4, D), BF16)
    scratch = [s for _, slab in SLABS.values() for s in slab.scratch()]
    wires = 12 + sum(slab.copies() for _, slab in SLABS.values())
    like = lambda a: pltpu.VMEM(a.shape, a.dtype)
    return pl.pallas_call(
        reduce_kernel,
        in_specs=[pl.BlockSpec(memory_space=pltpu.SMEM)] + [hbm] * 7 + [vmem] + [hbm] * 3,
        out_specs=[hbm] * 5 + [vmem],
        out_shape=[
            back, shape(up), shape(down),
            jax.ShapeDtypeStruct((D // 8, 3 * D), BF16),
            shape(out),
            jax.ShapeDtypeStruct((16, D), F32),
        ],
        scratch_shapes=[like(a) for a in (acts, mixed, do, logs, rows, whole, one)]
        + [
            pltpu.VMEM(rows.shape[::-1], BF16),
            pltpu.VMEM(acts.shape, BF16),
            pltpu.VMEM((4, 2, D // 8, 3 * D), BF16),
            pltpu.VMEM((share, length, D), BF16),
            pltpu.VMEM((4, 16, D), F32),
            pltpu.VMEM((6, 16, D), F32),
        ]
        + scratch
        + [
            pltpu.SemaphoreType.DMA((wires,)),
            pltpu.SemaphoreType.DMA((wires,)),
            pltpu.SemaphoreType.DMA((N_LOADS + 2 + 3 * len(SLABS),)),
        ],
        compiler_params=pltpu.CompilerParams(
            collective_id=1, has_side_effects=True, vmem_limit_bytes=VMEM_ALL
        ),
        name="attend_reduce",
    )(lengths, acts, mixed, do, logs, rows, whole, one, vec, up, down, out)


def send_back(result, share):
    blk, span = lax.axis_index("blk"), result.shape[1] // 4
    piece = lambda at: lax.dynamic_slice_in_dim(result, at * span, span, axis=1)
    output = jnp.zeros((4 * share, span, D), BF16)
    output = lax.dynamic_update_slice_in_dim(output, piece(blk), blk * share, axis=0)
    for k in (1, 2, 3):
        other = blk ^ k
        got = lax.ppermute(piece(other), "blk", [(b, b ^ k) for b in range(4)])
        output = lax.dynamic_update_slice_in_dim(output, got, other * share, axis=0)
    return output


def local(*args):
    tables, lengths, cotangent, step_count = args[:4]
    masters, firsts, seconds = args[4:9], args[9:14], args[14:19]
    w_qkv, w_out, w_up, w_down, vectors = masters
    blocks = lax.axis_size("blk")
    shards = lax.axis_size("tab")
    table_count, local_len = tables.shape[:2]
    share = table_count // blocks
    tuned = shards == 8 and blocks == 4
    owned = vectors.shape[0]
    vec_own = jnp.pad(vectors.astype(BF16).T, ((0, 4), (0, 0)))
    my_lengths = lax.dynamic_slice(lengths, (lax.axis_index("blk") * share,), (share,))
    if tuned:
        at_own = (0, lax.axis_index("tab") * owned)
        vec_wide = lax.dynamic_update_slice(jnp.zeros((16, D), BF16), vec_own, at_own)
        mine, cot, *wholes, qkv, mixed, logs = gather_all(
            my_lengths, tables, cotangent, w_qkv, w_out, w_up, w_down, vec_wide[None]
        )
        vec_f = jnp.sum(wholes[4].astype(F32), axis=0)[:12]
    else:
        spread = partial(lax.all_to_all, axis_name="blk", split_axis=0, concat_axis=1, tiled=True)
        mine, cot = spread(tables), spread(cotangent)
        narrow = [w.astype(BF16) for w in (w_qkv, w_out, w_up, w_down)]
        wholes = [lax.all_gather(w, "tab", axis=0) for w in narrow + [vec_own]]
        vec_f = wholes[4][:, :12].transpose(1, 0, 2).reshape(12, D).astype(F32)
    full_qkv, full_out, full_up, full_down = [
        w.reshape(-1, w.shape[-1]) for w in wholes[:4]
    ]
    bias_up = vec_f[8:12].reshape(-1)
    rows = mine.reshape(-1, D)
    if not tuned:
        bias_qkv = jnp.concatenate([vec_f[0], jnp.zeros((D,), F32), vec_f[1]])
        qkv = (jnp.dot(rows, full_qkv, preferred_element_type=F32) + bias_qkv).astype(BF16)
        mixed, logs = attention_forward(my_lengths, qkv, share)
    attn_out = jnp.dot(mixed, full_out, preferred_element_type=F32) + vec_f[2]
    normed_one, norm_one_back = jax.vjp(
        layer_norm, rows.astype(F32) + attn_out, vec_f[4], vec_f[5]
    )
    normed_b = normed_one.astype(BF16)
    hidden = jnp.dot(normed_b, full_up, preferred_element_type=F32) + bias_up
    below = 0.5 * (1.0 + lax.erf(hidden * 0.5**0.5))
    active_b = (hidden * below).astype(BF16)
    slope = below + hidden * jnp.exp(-0.5 * hidden * hidden) * (2.0 * math.pi) ** -0.5
    active_b, slope = lax.optimization_barrier((active_b, slope.astype(BF16)))
    branch = jnp.dot(active_b, full_down, preferred_element_type=F32) + vec_f[3]
    result, norm_two_back = jax.vjp(layer_norm, normed_one + branch, vec_f[6], vec_f[7])
    result = result.astype(BF16).reshape(mine.shape)
    grad_two, grad_g2, grad_c2 = norm_two_back(cot.reshape(-1, D).astype(F32))
    grad_b2 = jnp.sum(grad_two, axis=0)
    branch_b = grad_two.astype(BF16)
    gw_down = inner(active_b, branch_b).astype(BF16)
    grad_hidden = back_mul(branch_b, full_down) * slope.astype(F32)
    grad_b1 = jnp.sum(grad_hidden, axis=0)
    hidden_b = grad_hidden.astype(BF16)
    gw_up = inner(normed_b, hidden_b).astype(BF16)
    grad_one, grad_g1, grad_c1 = norm_one_back(grad_two + back_mul(hidden_b, full_up))
    grad_bo = jnp.sum(grad_one, axis=0)
    attn_b = grad_one.astype(BF16)
    gw_out = inner(mixed, attn_b).astype(BF16)
    grad_mixed = back_mul(attn_b, full_out).astype(BF16)
    norm_rows = [grad_bo, grad_b2, grad_g1, grad_c1, grad_g2, grad_c2]
    if tuned:
        empty = jnp.zeros((2, D), F32)
        wide_vec = jnp.concatenate(
            [empty, jnp.stack(norm_rows), grad_b1.reshape(4, D), empty, empty]
        )
        by_owner = lambda g: g.reshape(4, 2, -1, g.shape[-1])
        output = send_back(result, share)
        grad_input, *sums = reduce_all(
            my_lengths, qkv, mixed, grad_mixed, logs, rows, full_qkv, grad_one,
            wide_vec, by_owner(gw_up), by_owner(gw_down), by_owner(gw_out),
        )
        at_own = (0, lax.axis_index("tab") * owned)
        sum_vec = lax.dynamic_slice(sums[4], at_own, (16, owned))[:12].T
        shares = [s.astype(F32) for s in (sums[2], sums[3], sums[0], sums[1], sum_vec)]
    else:
        grad_three, sums = attention_backward(my_lengths, qkv, mixed, logs, grad_mixed, share)
        sums = jnp.sum(sums[:, :, :2], axis=0)
        grad_bq, grad_bv = sums[:, 0].reshape(-1), sums[:, 1].reshape(-1)
        grad_qkv = jnp.concatenate([grad_three[i] for i in range(3)], axis=1)
        gw_qkv = inner(rows, grad_qkv).astype(BF16)
        grad_in = grad_one + back_mul(grad_qkv, full_qkv)
        grad_in = grad_in.astype(BF16).reshape(mine.shape)
        gw_vec = jnp.concatenate(
            [jnp.stack([grad_bq, grad_bv] + norm_rows), grad_b1.reshape(4, D)]
        )
        back = partial(lax.all_to_all, axis_name="blk", split_axis=1, concat_axis=0, tiled=True)
        grad_input, output = back(grad_in), back(result)

        def collect(grad):
            part = lax.psum_scatter(
                grad.reshape(shards, -1, grad.shape[-1]), "tab", scatter_dimension=0
            )
            return lax.psum(part.astype(BF16), "blk").astype(F32)

        shares = [collect(g) for g in (gw_qkv, gw_out, gw_up, gw_down)]
        shares.append(collect(gw_vec.T.astype(BF16)))
    grad_input = grad_input.astype(F32)
    step_float = step_count[0].astype(F32)
    results = [output, grad_input]
    for at in range(5):
        results.extend(
            adam(masters[at], shares[at], firsts[at], seconds[at], RATES[at], step_float)
        )
    return tuple(results)


def solution(mesh):
    tokens, flat, rows = P("tab", "blk", None), P("tab"), P("tab", None)
    return jax.shard_map(
        local,
        mesh=mesh,
        in_specs=(tokens, flat, tokens, P()) + (rows,) * 15,
        out_specs=(tokens, tokens) + (rows,) * 20,
        check_vma=False,
    )
```
